32 devices in a mesh: dp: 8 (over z, y), tp: 4 (over x, core).
Axes of the slice: x: 2, y: 2, z: 4, core: 2. Of those that a mesh axis runs over, the one named last changes fastest.
Arguments:
- tokens: bfloat16 [8, 2048, 768], P('dp', 'tp'), may hold values from -6 to 6
- cotangent: bfloat16 [8, 2048, 768], P('dp', 'tp'), may hold values from -6 to 6
- tags: int32 [8], P('dp'), may hold values from 0 to 7
- tag_weight: float32 [8], replicated, may hold values from 0.25 to 4
- query_weight: bfloat16 [768, 768], P(None, 'tp'), may hold values from -0.21875 to 0.21875
- key_value_weight: bfloat16 [768, 128], replicated, may hold values from -0.21875 to 0.21875
- output_weight: bfloat16 [768, 768], P('tp'), may hold values from -1.25 to 1.25
- up_weight: bfloat16 [768, 3072], P(None, 'tp'), may hold values from -0.21875 to 0.21875
- down_weight: bfloat16 [3072, 768], P('tp'), may hold values from -0.109375 to 0.109375
- norm_gain_one: float32 [768], replicated, may hold values from 0.25 to 1.75
- norm_bias_one: float32 [768], replicated, may hold values from -1.5 to 1.5
- norm_gain_two: float32 [768], replicated, may hold values from 0.25 to 1.75
- norm_bias_two: float32 [768], replicated, may hold values from -1.5 to 1.5
Outputs:
- block_out: bfloat16 [8, 2048, 768], P('dp', 'tp')
- grad_tokens: bfloat16 [8, 2048, 768], P('dp', 'tp')
- grad_query: float32 [768, 768], P(None, 'tp')
- grad_keyval: float32 [768, 128], replicated
- grad_output: float32 [768, 768], P('tp')
- grad_upward: float32 [768, 3072], P(None, 'tp')
- grad_downward: float32 [3072, 768], P('tp')
- grad_gain_one: float32 [768], replicated
- grad_bias_one: float32 [768], replicated
- grad_gain_two: float32 [768], replicated
- grad_bias_two: float32 [768], replicated
The draws below stay inside these ranges and needn't reach their ends.
All inputs are finite; a program needn't handle non-finite values.
Results may differ from the reference program's by a relative error of at most 0.013.
Values may be sent and summed in bfloat16 or wider, within the bound.
A program may use at most 128 MiB of HBM per device.

```python
import math
import jax
import jax.numpy as jnp
from jax import lax

D = 768
HEADS = 12
HD = 64
FF = 3072
ROT = 16
LEN = 2048
NTAGS = 8
SEQS = 8


def with_ends(drawn, key, least, largest):
    dims = drawn.shape
    index_at = [jax.random.randint(jax.random.fold_in(key, axis), (), 0, dims[axis]) for axis in range(len(dims))]
    drawn = drawn.at[tuple(index_at)].set(least)
    longest = dims.index(max(dims))
    index_at[longest] = (index_at[longest] + 1) % dims[longest]
    return drawn.at[tuple(index_at)].set(largest)


def block_scale(own_key, dims, cuts, least, largest):
    loudness = 1.0
    for position, blocks in cuts:
        steps = jax.random.uniform(jax.random.fold_in(jax.random.fold_in(own_key, 6), position), (blocks,), jnp.float32, least / len(cuts), largest / len(cuts))
        loudness = loudness * jnp.repeat(jnp.exp(steps), dims[position] // blocks).reshape((-1,) + (1,) * (len(dims) - 1 - position))
    return loudness


def bell_draw(rng, shape, spread, limit, cuts=(), kind=jnp.bfloat16):
    gain = block_scale(rng, shape, cuts, -0.22, 0.18) if cuts else 1.0
    drawn = jax.random.normal(rng, shape, jnp.float32) * spread * gain
    return jnp.minimum(jnp.maximum(drawn, -limit), limit).astype(kind)


def setup_inputs(seed: int = 0) -> dict:
    key_of = jax.random.split(jax.random.key(seed), 14)
    tokens = bell_draw(key_of[0], (SEQS, LEN, D), 1.0, 6.0, ((0, 8), (1, 4)))
    cotangent = bell_draw(key_of[1], (SEQS, LEN, D), 1.0, 6.0, ((0, 8), (1, 4)))
    tags = with_ends(jax.random.randint(key_of[2], (SEQS,), 0, NTAGS), jax.random.fold_in(key_of[2], 1), 0, NTAGS - 1).astype(jnp.int32)
    tag_weight = jnp.clip(jnp.exp(jax.random.uniform(key_of[3], (NTAGS,), jnp.float32, math.log(0.25), math.log(4.0))), 0.25, 4.0)
    query_weight = bell_draw(key_of[4], (D, HEADS * HD), D ** -0.5, 0.21875, ((1, 4),))
    key_value_weight = bell_draw(key_of[5], (D, 2 * HD), D ** -0.5, 0.21875)
    output_weight = bell_draw(key_of[6], (HEADS * HD, D), (D // 32) ** -0.5, 1.25, ((0, 4),))
    up_weight = bell_draw(key_of[7], (D, FF), D ** -0.5, 0.21875, ((1, 4),))
    down_weight = bell_draw(key_of[8], (FF, D), FF ** -0.5, 0.109375, ((0, 4),))
    norm_gain_one = jnp.clip(1.0 + 0.15 * jax.random.normal(key_of[9], (D,), jnp.float32), 0.25, 1.75)
    norm_bias_one = bell_draw(key_of[10], (D,), 0.3, 1.5, (), jnp.float32)
    norm_gain_two = jnp.clip(1.0 + 0.15 * jax.random.normal(key_of[11], (D,), jnp.float32), 0.25, 1.75)
    norm_bias_two = bell_draw(key_of[12], (D,), 0.3, 1.5, (), jnp.float32)
    return dict(tokens=tokens, cotangent=cotangent, tags=tags, tag_weight=tag_weight, query_weight=query_weight, key_value_weight=key_value_weight, output_weight=output_weight, up_weight=up_weight, down_weight=down_weight, norm_gain_one=norm_gain_one, norm_bias_one=norm_bias_one, norm_gain_two=norm_gain_two, norm_bias_two=norm_bias_two)


EXACT_MODE = lax.Precision.HIGHEST

@jax.custom_vjp
def low(v):
    return lax.optimization_barrier(v.astype(jnp.bfloat16)).astype(jnp.float32)

@jax.custom_vjp
def reduced_backward(v):
    return v

def low_keep(v):
    return (low(v), None)

def low_pass(kept, grad):
    return (grad,)

def back_keep(v):
    return (v, None)

def back_low(kept, grad):
    return (low(grad),)
low.defvjp(low_keep, low_pass)
reduced_backward.defvjp(back_keep, back_low)

def layer_norm(values, gain_vec, shift_vec):
    row_mean = lax.optimization_barrier(jnp.mean(values, axis=-1, keepdims=True))
    centred = values - row_mean
    variance = lax.optimization_barrier(jnp.mean(centred * centred, axis=-1, keepdims=True))
    return centred * lax.rsqrt(variance + 1e-05) * gain_vec + shift_vec

def rot_angles(positions):
    frequencies = 10000.0 ** (-jnp.arange(0, ROT, 2, dtype=jnp.float32) / ROT)
    return positions.astype(jnp.float32)[:, None] * frequencies[None, :]

def rotate(values, angles):
    half_rot = ROT // 2
    cosine = jnp.cos(angles)[:, None, :]
    sine_part = jnp.sin(angles)[:, None, :]
    front_half = values[..., :half_rot]
    back_half = values[..., half_rot:ROT]
    return jnp.concatenate([front_half * cosine - back_half * sine_part, back_half * cosine + front_half * sine_part, values[..., ROT:]], axis=-1)

def attend(block_item):
    query_row, key_row, value_row = block_item
    scores = reduced_backward(jnp.dot(query_row, key_row.T, precision=EXACT_MODE) * HD ** (-0.5))
    positions = jnp.arange(LEN)
    allowed = positions[None, :] <= positions[:, None]
    masked = jnp.where(allowed, scores, -1e+30)
    weights = low(jax.nn.softmax(masked, axis=-1))
    return jnp.dot(weights, value_row, precision=EXACT_MODE)

def forward(tokens_f, query_weight, key_value_weight, output_weight, up_weight, down_weight, gain_one, bias_one, gain_two, bias_two):
    angles = rot_angles(jnp.arange(LEN))
    first_normed = low(layer_norm(tokens_f, gain_one, bias_one))
    second_normed = low(layer_norm(tokens_f, gain_two, bias_two))
    query_matrix = reduced_backward(jnp.einsum('nvu,uk->nvk', first_normed, query_weight, precision=EXACT_MODE))
    query_matrix = low(rotate(query_matrix.reshape(SEQS, LEN, HEADS, HD), angles))
    key_value_rows = reduced_backward(jnp.einsum('nvu,uk->nvk', first_normed, key_value_weight, precision=EXACT_MODE))
    key_rows = rotate(key_value_rows[:, :, None, :HD], angles)[:, :, 0, :]
    keyval_low = low(jnp.concatenate([key_rows, key_value_rows[:, :, HD:]], axis=-1))
    query_items = jnp.transpose(query_matrix, (0, 2, 1, 3)).reshape(SEQS * HEADS, LEN, HD)
    key_items = jnp.repeat(keyval_low[:, :, :HD], HEADS, axis=0)
    value_items = jnp.repeat(keyval_low[:, :, HD:], HEADS, axis=0)
    context_rows = lax.map(jax.checkpoint(attend), (query_items, key_items, value_items))
    context_rows = jnp.transpose(context_rows.reshape(SEQS, HEADS, LEN, HD), (0, 2, 1, 3)).reshape(SEQS, LEN, HEADS * HD)
    context_rows = reduced_backward(low(context_rows))
    attention_branch = jnp.einsum('nzi,ib->nzb', context_rows, output_weight, precision=EXACT_MODE)
    hidden_rows = reduced_backward(jnp.einsum('rob,bc->roc', second_normed, up_weight, precision=EXACT_MODE))
    middle_rows = low(jax.nn.gelu(hidden_rows, approximate=False))
    feedforward_branch = jnp.einsum('xiw,wb->xib', middle_rows, down_weight, precision=EXACT_MODE)
    return tokens_f + reduced_backward(attention_branch + feedforward_branch)

def reference(tokens, cotangent, tags, tag_weight, query_weight, key_value_weight, output_weight, up_weight, down_weight, norm_gain_one, norm_bias_one, norm_gain_two, norm_bias_two):
    primals = (tokens.astype(jnp.float32), query_weight.astype(jnp.float32), key_value_weight.astype(jnp.float32), output_weight.astype(jnp.float32), up_weight.astype(jnp.float32), down_weight.astype(jnp.float32), norm_gain_one, norm_bias_one, norm_gain_two, norm_bias_two)
    block_out, pullback = jax.vjp(forward, *primals)
    tag_ids = jnp.arange(NTAGS, dtype=jnp.int32)
    row_weight = lax.optimization_barrier(jnp.sum(jnp.where(tags[:, None] == tag_ids[None, :], tag_weight[None, :], 0.0), axis=1))
    weighted = cotangent.astype(jnp.float32) * row_weight[:, None, None]
    grads = pullback(weighted)
    return (block_out.astype(jnp.bfloat16), grads[0].astype(jnp.bfloat16), grads[1], grads[2], grads[3], grads[4], grads[5], grads[6], grads[7], grads[8], grads[9])
```

```python
import jax
import jax.numpy as jnp
from jax import lax
from jax.sharding import PartitionSpec as P

HD = 64
ROT = 16


def layer_norm(values, gain_vec, shift_vec):
    row_mean = jnp.mean(values, axis=-1, keepdims=True)
    centred = values - row_mean
    variance = jnp.mean(centred * centred, axis=-1, keepdims=True)
    inverse = lax.rsqrt(variance + 1e-05)
    normal = centred * inverse
    return (normal * gain_vec + shift_vec, normal, inverse)


def norm_back(scaled, normal, inverse):
    term_one = jnp.mean(scaled, axis=-1, keepdims=True)
    term_two = jnp.mean(scaled * normal, axis=-1, keepdims=True)
    return inverse * (scaled - term_one - normal * term_two)


def rot_angles(positions):
    frequencies = 10000.0 ** (-jnp.arange(0, ROT, 2, dtype=jnp.float32) / ROT)
    return positions.astype(jnp.float32)[:, None] * frequencies[None, :]


def rotate(values, angles, direction):
    half_rot = ROT // 2
    cosine = jnp.cos(angles)[:, None, :]
    sine_part = direction * jnp.sin(angles)[:, None, :]
    front_half = values[..., :half_rot]
    back_half = values[..., half_rot:ROT]
    return jnp.concatenate(
        [
            front_half * cosine - back_half * sine_part,
            back_half * cosine + front_half * sine_part,
            values[..., ROT:],
        ],
        axis=-1,
    )


def outer_sum(left, right):
    return lax.dot_general(
        left, right, (((0, 1), (0, 1)), ((), ())), preferred_element_type=jnp.float32
    )


def against(left, weight):
    return lax.dot_general(
        left, weight, (((2,), (1,)), ((), ())), preferred_element_type=jnp.float32
    )


def shards(
    tokens,
    cotangent,
    tags,
    tag_weight,
    query_weight,
    key_value_weight,
    output_weight,
    up_weight,
    down_weight,
    norm_gain_one,
    norm_bias_one,
    norm_gain_two,
    norm_bias_two,
):
    seq_dev, own_len, model_width = tokens.shape
    full_len = own_len * lax.axis_size("tp")
    heads_dev = query_weight.shape[1] // HD
    score_scale = HD ** (-0.5)
    block_rows = min(512, full_len)
    blocks = full_len // block_rows
    own_rows = tokens.astype(jnp.float32)
    full_angles = rot_angles(jnp.arange(full_len))
    tag_ids = jnp.arange(tag_weight.shape[0], dtype=jnp.int32)
    row_weight = jnp.sum(
        jnp.where(tags[:, None] == tag_ids[None, :], tag_weight[None, :], 0.0), axis=1
    )
    upstream = cotangent.astype(jnp.float32) * row_weight[:, None, None]
    all_rows = lax.all_gather(tokens, "tp", axis=1, tiled=True).astype(jnp.float32)
    grad_rows = lax.all_gather(upstream.astype(jnp.bfloat16), "tp", axis=1, tiled=True)
    normed_one, normal_all, _ = layer_norm(all_rows, norm_gain_one, norm_bias_one)
    rows_one = normed_one.astype(jnp.bfloat16)
    rows_two = (normal_all * norm_gain_two + norm_bias_two).astype(jnp.bfloat16)
    key_value_rows = jnp.dot(rows_one, key_value_weight, preferred_element_type=jnp.float32)
    key_part = rotate(key_value_rows[:, :, None, :HD], full_angles, 1.0)[:, :, 0, :]
    key_value_rows = jnp.concatenate([key_part, key_value_rows[:, :, HD:]], axis=-1).astype(
        jnp.bfloat16
    )
    key_rows = key_value_rows[:, :, :HD]
    value_rows = key_value_rows[:, :, HD:]
    query_matrix = jnp.dot(rows_one, query_weight, preferred_element_type=jnp.float32).reshape(
        seq_dev, full_len, heads_dev, HD
    )
    query_matrix = rotate(query_matrix, full_angles, 1.0).astype(jnp.bfloat16)

    def block_scores(query_block, block_start):
        block_end = block_start + block_rows
        scores = (
            jnp.einsum(
                "sqhd,skd->sqhk",
                query_block,
                key_rows[:, :block_end],
                preferred_element_type=jnp.float32,
            )
            * score_scale
        )
        allowed = jnp.arange(block_end)[None, :] <= (block_start + jnp.arange(block_rows))[:, None]
        return jnp.where(allowed[None, :, None, :], scores, -1e30)

    context_list = []
    lse_list = []
    for block_index in range(blocks):
        block_start = block_index * block_rows
        block_end = block_start + block_rows
        scores = block_scores(query_matrix[:, block_start:block_end], block_start)
        row_top = jnp.max(scores, axis=-1, keepdims=True)
        weights = jnp.exp(scores - row_top)
        row_total = jnp.sum(weights, axis=-1, keepdims=True)
        weights_low = (weights / row_total).astype(jnp.bfloat16)
        context_list.append(
            jnp.einsum(
                "sqhk,skd->sqhd",
                weights_low,
                value_rows[:, :block_end],
                preferred_element_type=jnp.float32,
            )
        )
        lse_list.append(row_top + jnp.log(row_total))
    context_full = jnp.concatenate(context_list, axis=1)
    low_context = context_full.reshape(seq_dev, full_len, heads_dev * HD).astype(jnp.bfloat16)
    attention_branch = jnp.dot(low_context, output_weight, preferred_element_type=jnp.float32)
    hidden_rows = jnp.dot(rows_two, up_weight, preferred_element_type=jnp.float32)
    middle_rows = jax.nn.gelu(hidden_rows, approximate=False).astype(jnp.bfloat16)
    feedforward_branch = jnp.dot(middle_rows, down_weight, preferred_element_type=jnp.float32)
    branch = lax.psum_scatter(
        (attention_branch + feedforward_branch).astype(jnp.bfloat16),
        "tp",
        scatter_dimension=1,
        tiled=True,
    ).astype(jnp.float32)
    block_out = (own_rows + branch).astype(jnp.bfloat16)
    grad_output = outer_sum(low_context, grad_rows)
    grad_downward = outer_sum(middle_rows, grad_rows)
    grad_context = (
        against(grad_rows, output_weight)
        .astype(jnp.bfloat16)
        .reshape(seq_dev, full_len, heads_dev, HD)
    )
    grad_middle = against(grad_rows, down_weight)
    normal_cdf = 0.5 * (1.0 + lax.erf(hidden_rows * 0.7071067811865476))
    density = jnp.exp(-0.5 * hidden_rows * hidden_rows) * 0.3989422804014327
    grad_hidden = (grad_middle * (normal_cdf + hidden_rows * density)).astype(jnp.bfloat16)
    grad_upward = outer_sum(rows_two, grad_hidden)
    norm_part_two = against(grad_hidden, up_weight)
    grad_kv_full = jnp.zeros((seq_dev, full_len, 2 * HD), jnp.float32)
    query_grad_list = []
    for block_index in range(blocks):
        block_start = block_index * block_rows
        block_end = block_start + block_rows
        query_block = query_matrix[:, block_start:block_end]
        grad_block = grad_context[:, block_start:block_end]
        scores = block_scores(query_block, block_start)
        weights = jnp.exp(scores - lse_list[block_index])
        grad_weights = jnp.einsum(
            "sqhd,skd->sqhk",
            grad_block,
            value_rows[:, :block_end],
            preferred_element_type=jnp.float32,
        )
        row_delta = jnp.sum(
            grad_block.astype(jnp.float32) * context_list[block_index], axis=-1, keepdims=True
        )
        grad_scores = (weights * (grad_weights - row_delta)).astype(jnp.bfloat16)
        query_grad_list.append(
            jnp.einsum(
                "sqhk,skd->sqhd",
                grad_scores,
                key_rows[:, :block_end],
                preferred_element_type=jnp.float32,
            )
            * score_scale
        )
        grad_keys = (
            jnp.einsum(
                "sqhk,sqhd->skd", grad_scores, query_block, preferred_element_type=jnp.float32
            )
            * score_scale
        )
        grad_values = jnp.einsum(
            "sqhk,sqhd->skd",
            weights.astype(jnp.bfloat16),
            grad_block,
            preferred_element_type=jnp.float32,
        )
        grad_kv_full = grad_kv_full.at[:, :block_end].add(
            jnp.concatenate([grad_keys, grad_values], axis=-1)
        )
    grad_queries = jnp.concatenate(query_grad_list, axis=1)
    grad_queries = (
        rotate(grad_queries, full_angles, -1.0)
        .reshape(seq_dev, full_len, heads_dev * HD)
        .astype(jnp.bfloat16)
    )
    grad_query = outer_sum(rows_one, grad_queries)
    norm_part_one = against(grad_queries, query_weight)
    key_back = rotate(grad_kv_full[:, :, None, :HD], full_angles, -1.0)[:, :, 0, :]
    keyval_part = jnp.concatenate([key_back, grad_kv_full[:, :, HD:]], axis=-1)
    low_keyval = keyval_part.astype(jnp.bfloat16)
    grad_keyval = outer_sum(rows_one, low_keyval)
    part_one = norm_part_one + against(low_keyval, key_value_weight)
    small = jnp.stack(
        [
            jnp.sum(part_one * normal_all, axis=(0, 1)),
            jnp.sum(part_one, axis=(0, 1)),
            jnp.sum(norm_part_two * normal_all, axis=(0, 1)),
            jnp.sum(norm_part_two, axis=(0, 1)),
        ]
    )
    scaled = lax.psum_scatter(
        (part_one * norm_gain_one + norm_part_two * norm_gain_two).astype(jnp.bfloat16),
        "tp",
        scatter_dimension=1,
        tiled=True,
    ).astype(jnp.float32)
    _, normal_own, inverse_own = layer_norm(own_rows, norm_gain_one, norm_bias_one)
    grad_tokens = upstream + norm_back(scaled, normal_own, inverse_own)
    grad_query, grad_output, grad_upward, grad_downward = [
        v.astype(jnp.float32)
        for v in lax.psum(
            tuple(
                v.astype(jnp.bfloat16)
                for v in (grad_query, grad_output, grad_upward, grad_downward)
            ),
            "dp",
        )
    ]
    tail = lax.psum(
        jnp.concatenate([grad_keyval.reshape(-1), small.reshape(-1)]).reshape(-1, 128), ("dp", "tp")
    ).reshape(-1)
    grad_keyval, small = (
        tail[: grad_keyval.size].reshape(grad_keyval.shape),
        tail[grad_keyval.size :].reshape(small.shape),
    )
    grad_gain_one, grad_bias_one, grad_gain_two, grad_bias_two = small
    return (
        block_out,
        grad_tokens.astype(jnp.bfloat16),
        grad_query,
        grad_keyval,
        grad_output,
        grad_upward,
        grad_downward,
        grad_gain_one,
        grad_bias_one,
        grad_gain_two,
        grad_bias_two,
    )


def solution(mesh):
    in_specs = (
        P("dp", "tp", None),
        P("dp", "tp", None),
        P("dp"),
        P(),
        P(None, "tp"),
        P(),
        P("tp", None),
        P(None, "tp"),
        P("tp", None),
        P(),
        P(),
        P(),
        P(),
    )
    out_specs = (
        P("dp", "tp", None),
        P("dp", "tp", None),
        P(None, "tp"),
        P(),
        P("tp", None),
        P(None, "tp"),
        P("tp", None),
        P(),
        P(),
        P(),
        P(),
    )
    return jax.shard_map(shards, mesh=mesh, in_specs=in_specs, out_specs=out_specs, check_vma=False)
```

```python
import functools

import jax
import jax.numpy as jnp
import numpy as np
from jax import lax
from jax.experimental import pallas as pl
from jax.experimental.pallas import tpu as pltpu
from jax.sharding import PartitionSpec as P

HD = 64
ROT = 16
HALF = ROT // 2
TILE = 256
LANES = 128
MESH = pl.DeviceIdType.MESH
BF = jnp.bfloat16
F32 = jnp.float32


def mm(left, right):
    return jnp.dot(left, right, preferred_element_type=F32)


def mm_t(left, right):
    return lax.dot_general(left, right, (((1,), (1,)), ((), ())), preferred_element_type=F32)


def turn(values, cosine, sine):
    front, back = values[:HALF], values[HALF:ROT]
    return jnp.concatenate(
        [front * cosine - back * sine, back * cosine + front * sine, values[ROT:]], axis=0
    )


class Plan:
    def __init__(self, dp):
        self.bits = dp.bit_length() - 1
        self.extra = list(range(3, self.bits))
        self.stages = 6 + len(self.extra)
        self.orders = ((0, 1, 2), (1, 0, 2))


class Bundle:
    def __init__(self, plan, d, t, part, landed, swapped, total, send, recv):
        self.plan, self.d, self.t = plan, d, t
        self.part, self.landed, self.swapped, self.total = part, landed, swapped, total
        self.send, self.recv = send, recv
        self.rows = part.shape[1]

    def bit(self, position):
        return (self.d // (2**position)) % 2

    def partner(self, position):
        return self.d + (1 - 2 * self.bit(position)) * (2**position)

    def span(self, kind, depth):
        start = 0
        for level in range(depth):
            start = start + self.bit(self.plan.orders[kind][level]) * (self.rows >> (level + 1))
        return pl.multiple_of(start, 16), self.rows >> depth

    def copy(self, unit, kind, stage):
        order, extra = self.plan.orders[kind], self.plan.extra
        if stage < 3:
            start, size = self.span(kind, stage)
            position = order[stage]
            half = size // 2
            other = pl.multiple_of(start + (1 - self.bit(position)) * half, 16)
            source = self.part.at[unit, pl.ds(other, half)]
            target = self.landed.at[unit, pl.ds(self.rows - size, half)]
        elif stage < 3 + len(extra):
            start, size = self.span(kind, 3)
            position = extra[stage - 3]
            source = self.part.at[unit, pl.ds(start, size)]
            target = self.swapped.at[unit, stage - 3]
        else:
            depth = self.plan.stages - stage
            start, size = self.span(kind, depth)
            position = order[depth - 1]
            source = self.total.at[unit, pl.ds(start, size)]
            target = source
        return pltpu.make_async_remote_copy(
            src_ref=source,
            dst_ref=target,
            send_sem=self.send.at[unit, stage],
            recv_sem=self.recv.at[unit, stage],
            device_id=(self.partner(position), self.t),
            device_id_type=MESH,
        )

    def start(self, unit, kind, stage):
        self.copy(unit, kind, stage).start()

    def finish(self, unit, kind, stage, publish=True):
        self.copy(unit, kind, stage).wait()
        last = 2 + len(self.plan.extra)
        if stage <= last:
            if stage < 3:
                start, size = self.span(kind, stage + 1)
                arrived = self.landed[unit, pl.ds(self.rows - 2 * size, size)]
            else:
                start, size = self.span(kind, 3)
                arrived = self.swapped[unit, stage - 3]
            mine = self.part[unit, pl.ds(start, size)]
            summed = (mine.astype(F32) + arrived.astype(F32)).astype(BF)
            if stage == last and publish:
                self.total[unit, pl.ds(start, size)] = summed
            else:
                self.part[unit, pl.ds(start, size)] = summed


def block_kernel(
    plan,
    tags_ref,
    tag_weight_ref,
    tok_ref,
    cot_ref,
    query_ref,
    keyval_ref,
    output_ref,
    up_ref,
    down_ref,
    norms_ref,
    table_ref,
    block_out_ref,
    grad_tokens_ref,
    total_ref,
    total_small_ref,
    x_all,
    gr_all,
    n1_all,
    br_all,
    g_all,
    up_t,
    down_t,
    qkv_t,
    qkv_w,
    out_t,
    q_t,
    k_t,
    k_r,
    v_t,
    v_r,
    do_t,
    gq_all,
    norms_c,
    bias_acc,
    sum_out,
    sum_qkv,
    score,
    prob,
    acc,
    d_key,
    d_value,
    part,
    landed,
    swapped,
    part_small,
    landed_small,
    swapped_small,
    tp_land,
    tp_land_small,
    pre,
    from_sib,
    from_x,
    ag_send,
    ag_recv,
    rs_send,
    rs_recv,
    rs_send_x,
    rs_recv_x,
    dp_send,
    dp_recv,
    dp_send_small,
    dp_recv_small,
    tp_send,
    tp_recv,
):
    d, t = lax.axis_index("dp"), lax.axis_index("tp")
    chip, core = t // 2, t % 2
    sib = t + 1 - 2 * core
    across = (t + 2) % 4
    diag = (sib + 2) % 4
    width = tok_ref.shape[1]
    hidden = up_ref.shape[1]
    q_cols = query_ref.shape[1]
    heads = q_cols // HD
    own_blocks = tok_ref.shape[0] // TILE
    blocks = 4 * own_blocks
    half_width = width // 2
    tall = width // TILE

    big = Bundle(plan, d, t, part, landed, swapped, total_ref, dp_send, dp_recv)
    small = Bundle(
        plan, d, t, part_small, landed_small, swapped_small, total_small_ref, dp_send_small, dp_recv_small
    )

    barrier = pltpu.get_barrier_semaphore()
    peers = [(d, sib), (d, across), (d, diag)] + [(big.partner(b), t) for b in range(plan.bits)]
    for peer in peers:
        pl.semaphore_signal(barrier, inc=1, device_id=peer, device_id_type=MESH)
    pl.semaphore_wait(barrier, len(peers))

    row_weight = tag_weight_ref[tags_ref[0]]

    sets = (x_all, gr_all)

    def gather_copy(kind, piece, owner, route):
        place = owner * own_blocks + piece
        target = {0: sib, 1: across, 2: sib}[route]
        return pltpu.make_async_remote_copy(
            src_ref=sets[kind].at[place],
            dst_ref=sets[kind].at[place],
            send_sem=ag_send.at[kind, piece, route],
            recv_sem=ag_recv.at[kind, piece, route],
            device_id=(d, target),
            device_id_type=MESH,
        )

    for piece in range(own_blocks):
        rows = slice(piece * TILE, (piece + 1) * TILE)
        x_all[t * own_blocks + piece] = tok_ref[rows, :].T
        gather_copy(0, piece, t, 1).start()
        gather_copy(0, piece, t, 0).start()
        gr_all[t * own_blocks + piece] = (cot_ref[rows, :].astype(F32) * row_weight).astype(BF).T
        gather_copy(1, piece, t, 1).start()
        gather_copy(1, piece, t, 0).start()

    up_t[...] = up_ref[...].T
    down_t[...] = down_ref[...].T
    qkv_t[:q_cols] = query_ref[...].T
    qkv_t[q_cols:] = keyval_ref[...].T
    qkv_w[...] = qkv_t[...].T
    out_t[...] = output_ref[...].T
    norms_c[...] = norms_ref[...].T
    score[...] = jnp.zeros_like(score)
    bias_acc[...] = jnp.zeros_like(bias_acc)
    sum_out[...] = jnp.zeros_like(sum_out)
    sum_qkv[...] = jnp.zeros_like(sum_qkv)
    d_key[...] = jnp.zeros_like(d_key)
    d_value[...] = jnp.zeros_like(d_value)

    def standardize(place):
        x = x_all[place].astype(F32)
        mean = jnp.sum(x, axis=0, keepdims=True) * (1.0 / width)
        centred = x - mean
        variance = jnp.sum(centred * centred, axis=0, keepdims=True) * (1.0 / width)
        inverse = lax.rsqrt(variance + 1e-05)
        return centred * inverse, inverse

    def feed_forward(step, carry):
        late = step // 4
        owner = (1 - late) * (t + (sib - t) * ((step // 2) % 2)) + late * (
            across + (diag - across) * (step % 2)
        )
        piece = (1 - late) * (step % 2) + late * ((step // 2) % 2)
        place = owner * own_blocks + piece

        @pl.when((step == 2) | (step == 3))
        def _():
            for kind in range(2):
                gather_copy(kind, piece, sib, 0).wait_recv()

        @pl.when((step == 4) | (step == 6))
        def _():
            for kind in range(2):
                gather_copy(kind, piece, across, 1).wait_recv()
                gather_copy(kind, piece, across, 2).start()

        @pl.when((step == 5) | (step == 7))
        def _():
            for kind in range(2):
                gather_copy(kind, piece, diag, 2).wait_recv()

        normal, _ = standardize(place)
        n1 = (normal * norms_c[:, 0:1] + norms_c[:, 1:2]).astype(BF)
        n2 = (normal * norms_c[:, 2:3] + norms_c[:, 3:4]).astype(BF)
        n1_all[place] = n1
        gr = gr_all[place]
        qkv = mm(qkv_t[...], n1)
        lanes = pl.ds(pl.multiple_of(place * TILE, TILE), TILE)
        cosine, sine = table_ref[:HALF, lanes], table_ref[HALF:, lanes]
        grad_context = mm(output_ref[...], gr)
        for head in range(heads):
            turned = turn(qkv[head * HD : (head + 1) * HD], cosine, sine) * (HD**-0.5)
            q_t[place, :, head * TILE : (head + 1) * TILE] = turned.astype(BF)
            do_t[place, :, head * TILE : (head + 1) * TILE] = grad_context[
                head * HD : (head + 1) * HD
            ].astype(BF)
        key = turn(qkv[q_cols : q_cols + HD], cosine, sine)
        value = qkv[q_cols + HD :]
        k_t[place] = key.astype(BF)
        k_r[place] = key.T.astype(BF)
        v_t[place, :HD] = value.astype(BF)
        v_t[place, HD:] = jnp.ones((v_t.shape[1] - HD, TILE), BF)
        v_r[place] = value.T.astype(BF)

        pre_act = mm(up_t[...], n2)
        cdf = 0.5 + 0.5 * lax.erf(pre_act * 0.7071067811865476)
        density = jnp.exp(-0.5 * pre_act * pre_act) * 0.3989422804014327
        middle = (pre_act * cdf).astype(BF)
        slope = cdf + pre_act * density
        br_all[place] = mm(down_t[...], middle).astype(BF)
        grad_hidden = (mm(down_ref[...], gr) * slope).astype(BF)
        up_two = mm(up_ref[...], grad_hidden)
        bias_acc[...] += up_two[:, :LANES] + up_two[:, LANES:]
        g_all[place] = (up_two * norms_c[:, 2:3]).astype(BF)
        score[:tall] += mm_t(middle, gr).reshape(tall, TILE, width)
        score[tall : 2 * tall] += mm_t(n2, grad_hidden).reshape(tall, TILE, hidden)
        return carry

    lax.fori_loop(0, blocks, feed_forward, 0)

    for piece in range(own_blocks):
        for kind in range(2):
            gather_copy(kind, piece, t, 0).wait_send()
            gather_copy(kind, piece, t, 1).wait_send()
            gather_copy(kind, piece, across, 2).wait_send()

    slices = width // LANES
    for index in range(slices):
        cols = slice(index * LANES, (index + 1) * LANES)
        part[2 * index] = score[:tall, :, cols].reshape(hidden, LANES).astype(BF)
        part[2 * index + 1] = score[tall : 2 * tall, :, cols].reshape(width, LANES).astype(BF)
    for index in range(tall):
        rows = slice(index * TILE, (index + 1) * TILE)
        product = jnp.sum(up_ref[rows, :].astype(F32) * score[tall + index], axis=1, keepdims=True)
        norms_c[rows, 4:5] = product
    norms_c[:, 5:6] = jnp.sum(bias_acc[...], axis=1, keepdims=True)
    bias_acc[...] = jnp.zeros_like(bias_acc)

    outs = (br_all, g_all)

    def block_of(step):
        return (blocks - 1) - step // 2 - (blocks // 2) * (step % 2)

    def pre_copy(kind, step, block):
        rows = pl.ds(pl.multiple_of((1 - core) * half_width, 16), half_width)
        return pltpu.make_async_remote_copy(
            src_ref=outs[kind].at[block, rows],
            dst_ref=pre.at[kind, step // 2],
            send_sem=rs_send.at[kind, step],
            recv_sem=rs_recv.at[kind, step],
            device_id=(d, sib),
            device_id_type=MESH,
        )

    def sib_copy(kind, step, block):
        return pltpu.make_async_remote_copy(
            src_ref=outs[kind].at[block],
            dst_ref=from_sib.at[kind, block % own_blocks],
            send_sem=rs_send.at[kind, step],
            recv_sem=rs_recv.at[kind, step],
            device_id=(d, sib),
            device_id_type=MESH,
        )

    def x_copy(kind, block, sender_core, owner):
        rows = pl.ds(pl.multiple_of(sender_core * half_width, 16), half_width)
        return pltpu.make_async_remote_copy(
            src_ref=outs[kind].at[block, rows],
            dst_ref=from_x.at[kind, block % own_blocks, rows],
            send_sem=rs_send_x.at[kind, block],
            recv_sem=rs_recv_x.at[kind, block % own_blocks, sender_core],
            device_id=(d, owner),
            device_id_type=MESH,
        )

    def scatter_first(kind, step):
        block = block_of(step)
        owner = block // own_blocks

        @pl.when(owner // 2 != chip)
        def _():
            pre_copy(kind, step, block).start()

        @pl.when((owner // 2 == chip) & (owner != t))
        def _():
            sib_copy(kind, step, block).start()

    def scatter_second(kind, step):
        block = block_of(step)
        owner = block // own_blocks

        @pl.when(owner // 2 != chip)
        def _():
            pre_copy(kind, step, block).wait()
            rows = pl.ds(pl.multiple_of(core * half_width, 16), half_width)
            mine = outs[kind][block, rows].astype(F32)
            outs[kind][block, rows] = (mine + pre[kind, step // 2].astype(F32)).astype(BF)
            x_copy(kind, block, core, owner).start()

        @pl.when((owner // 2 == chip) & (owner != t))
        def _():
            sib_copy(kind, step, block).wait_send()

    def scatter_sent(kind, step):
        block = block_of(step)
        owner = block // own_blocks

        @pl.when(owner // 2 != chip)
        def _():
            x_copy(kind, block, core, owner).wait_send()

    def scatter_arrived(kind, piece):
        block = t * own_blocks + piece
        step = 2 * ((blocks - 1 - block) % (blocks // 2)) + 1 - block // (blocks // 2)
        sib_copy(kind, step, block).wait_recv()
        for sender_core in range(2):
            x_copy(kind, block, sender_core, t).wait_recv()
        return (
            outs[kind][block].astype(F32)
            + from_sib[kind, piece].astype(F32)
            + from_x[kind, piece].astype(F32)
        )

    pairs = slices

    def slot(index):
        for stage in range(plan.stages, -1, -1):
            pair = index - stage

            @pl.when((pair >= 0) & (pair < pairs))
            def _():
                if stage > 0:
                    for kind in range(2):
                        big.finish(2 * pair + kind, kind, stage - 1)
                if stage < plan.stages:
                    for kind in range(2):
                        big.start(2 * pair + kind, kind, stage)

    def attend(step, carry):
        slot(step)
        block = block_of(step)
        queries = q_t[block]
        wide = heads * TILE

        def scores(j, top):
            tile = mm(k_r[j], queries)
            score[j] = tile
            return jnp.maximum(top, jnp.max(tile.reshape(TILE // 8, 8, wide), axis=0))

        top = lax.fori_loop(0, block, scores, jnp.full((8, wide), -1e30, F32))
        tile = mm(k_r[block], queries)
        past = lax.broadcasted_iota(jnp.int32, (TILE, wide), 0)
        now = lax.broadcasted_iota(jnp.int32, (TILE, wide), 1) % TILE
        tile = jnp.where(past <= now, tile, -1e30)
        score[block] = tile
        top = jnp.maximum(top, jnp.max(tile.reshape(TILE // 8, 8, wide), axis=0))
        top = jnp.max(top, axis=0, keepdims=True)

        acc[...] = jnp.zeros_like(acc)

        def weigh(j, carry):
            weights = jnp.exp(score[j] - top).astype(BF)
            prob[j] = weights
            acc[...] += mm(v_t[j], weights)
            return carry

        lax.fori_loop(0, block + 1, weigh, 0)
        inverse = 1.0 / acc[HD : HD + 1]
        context = acc[:HD] * inverse
        grad = (do_t[block].astype(F32) * inverse).astype(BF)
        delta = jnp.sum(grad.astype(F32) * context, axis=0, keepdims=True)
        grad_rows = grad.astype(F32).T.astype(BF)
        query_rows = queries.astype(F32).T.astype(BF)
        acc[:HD] = jnp.zeros((HD, wide), F32)

        def back(j, carry):
            weights = prob[j]
            grad_scores = (
                weights.astype(F32) * (mm(v_r[j], grad) - delta)
            ).astype(BF)
            acc[:HD] += mm(k_t[j], grad_scores)
            d_key[j] += mm(grad_scores, query_rows)
            d_value[j] += mm(weights, grad_rows)
            return carry

        lax.fori_loop(0, block + 1, back, 0)
        lanes = pl.ds(pl.multiple_of(block * TILE, TILE), TILE)
        cosine, sine = table_ref[:HALF, lanes], table_ref[HALF:, lanes]
        for head in range(heads):
            cols = slice(head * TILE, (head + 1) * TILE)
            turned = turn(acc[:HD, cols], cosine, -sine) * (HD**-0.5)
            gq_all[block, head * HD : (head + 1) * HD] = turned.astype(BF)
        context = jnp.concatenate(
            [context[:, h * TILE : (h + 1) * TILE] for h in range(heads)], axis=0
        ).astype(BF)
        br_all[block] = (mm(out_t[...], context) + br_all[block].astype(F32)).astype(BF)
        sum_out[...] += mm_t(context, gr_all[block])
        scatter_first(0, step)

        @pl.when(step > 0)
        def _():
            scatter_second(0, step - 1)

        return carry

    lax.fori_loop(0, blocks, attend, 0)
    scatter_second(0, blocks - 1)

    def project(step, carry):
        @pl.when(step % 2 == 0)
        def _():
            slot(blocks + step // 2)

        block = block_of(step)
        lanes = pl.ds(pl.multiple_of(block * TILE, TILE), TILE)
        cosine, sine = table_ref[:HALF, lanes], table_ref[HALF:, lanes]
        gq_all[block, q_cols : q_cols + HD] = turn(d_key[block].T, cosine, -sine).astype(BF)
        gq_all[block, q_cols + HD :] = d_value[block].T.astype(BF)
        grads = gq_all[block]
        up_one = mm(qkv_w[...], grads)
        bias_acc[...] += up_one[:, :LANES] + up_one[:, LANES:]
        g_all[block] = (g_all[block].astype(F32) + up_one * norms_c[:, 0:1]).astype(BF)
        sum_qkv[...] += mm_t(grads, n1_all[block])
        scatter_first(1, step)

        @pl.when(step > 0)
        def _():
            scatter_second(1, step - 1)

        return carry

    lax.fori_loop(0, blocks, project, 0)
    scatter_second(1, blocks - 1)
    for index in range(blocks + blocks // 2, pairs + plan.stages):
        slot(index)

    base = 2 * pairs
    for index in range(slices):
        cols = slice(index * LANES, (index + 1) * LANES)
        for which, source in ((0, sum_out[:, cols]), (1, sum_qkv[:q_cols, cols])):
            row = (2 * index + which) * q_cols
            part[base + row // width, row % width : row % width + q_cols] = source.astype(BF)
    grad_keyval = sum_qkv[q_cols:].T
    part[base + 3] = grad_keyval.astype(BF)
    shift_one = jnp.sum(bias_acc[...], axis=1, keepdims=True)
    shift_two = norms_c[:, 5:6]
    product_one = jnp.sum(qkv_t[...].astype(F32) * sum_qkv[...], axis=0, keepdims=True)
    product_one = jnp.broadcast_to(product_one, (8, width)).T[:, :1]
    gain_one = (product_one - norms_c[:, 1:2] * shift_one) / norms_c[:, 0:1]
    gain_two = (norms_c[:, 4:5] - norms_c[:, 3:4] * shift_two) / norms_c[:, 2:3]
    lane = lax.broadcasted_iota(jnp.int32, (width, 8), 1)
    columns = jnp.where(
        lane == 0, gain_one, jnp.where(lane == 1, shift_one, jnp.where(lane == 2, gain_two, shift_two))
    )
    rows = columns.T
    part_small[0] = jnp.zeros(part_small.shape[1:], BF)
    for index in range(slices):
        part_small[0, 16 * index : 16 * index + 8] = rows[
            :, index * LANES : (index + 1) * LANES
        ].astype(BF)

    ends = [(big, base + u, u % 2) for u in range(4)] + [(small, 0, 0)]
    shared = [False, False, False, True, True]
    middle_stage = 2 + len(plan.extra)
    for bundle, unit, kind in ends:
        bundle.start(unit, kind, 0)
    for stage in range(middle_stage + 1):
        for (bundle, unit, kind), wide in zip(ends, shared):
            bundle.finish(unit, kind, stage, publish=not wide)
            if stage < middle_stage or not wide:
                bundle.start(unit, kind, stage + 1)

    lands = (tp_land, tp_land_small)
    offsets = []
    for index, (bundle, unit, kind) in enumerate(ends[3:]):
        start, size = bundle.span(kind, 3)
        offsets.append((start, size))
        lands[index][t] = bundle.part[unit, pl.ds(start, size)]

    def tp_copy(index, sender, hop):
        return pltpu.make_async_remote_copy(
            src_ref=lands[index].at[sender],
            dst_ref=lands[index].at[sender],
            send_sem=tp_send.at[index, hop],
            recv_sem=tp_recv.at[index, hop],
            device_id=(d, (t + hop + 1) % 4),
            device_id_type=MESH,
        )

    for index in range(2):
        for hop in range(3):
            tp_copy(index, t, hop).start()
    for index, (bundle, unit, kind) in enumerate(ends[3:]):
        for hop in range(3):
            tp_copy(index, (t + 3 - hop) % 4, hop).wait_recv()
        start, size = offsets[index]
        land = lands[index]
        summed = land[0].astype(F32) + land[1].astype(F32) + land[2].astype(F32) + land[3].astype(F32)
        bundle.total[unit, pl.ds(start, size)] = summed.astype(BF)
        bundle.start(unit, kind, middle_stage + 1)
    for index in range(2):
        for hop in range(3):
            tp_copy(index, t, hop).wait_send()
    for stage in range(middle_stage + 1, plan.stages):
        for bundle, unit, kind in ends:
            bundle.finish(unit, kind, stage)
            if stage + 1 < plan.stages:
                bundle.start(unit, kind, stage + 1)

    for piece in range(own_blocks):
        place = t * own_blocks + piece
        cols = slice(piece * TILE, (piece + 1) * TILE)
        branch = scatter_arrived(0, piece)
        block_out_ref[:, cols] = (x_all[place].astype(F32) + branch).astype(BF)
        scaled = scatter_arrived(1, piece)
        normal, inverse = standardize(place)
        mean_one = jnp.sum(scaled, axis=0, keepdims=True) * (1.0 / width)
        mean_two = jnp.sum(scaled * normal, axis=0, keepdims=True) * (1.0 / width)
        grad_tokens_ref[:, cols] = (
            gr_all[place].astype(F32) + inverse * (scaled - mean_one - normal * mean_two)
        ).astype(BF)

    def drain(step, carry):
        for kind in range(2):
            scatter_sent(kind, step)
        return carry

    lax.fori_loop(0, blocks, drain, 0)


def shards(
    dp,
    tokens,
    cotangent,
    tags,
    tag_weight,
    query_weight,
    key_value_weight,
    output_weight,
    up_weight,
    down_weight,
    norm_gain_one,
    norm_bias_one,
    norm_gain_two,
    norm_bias_two,
):
    plan = Plan(dp)
    _, own_len, width = tokens.shape
    full_len = 4 * own_len
    q_cols, kv_cols, hidden = query_weight.shape[1], key_value_weight.shape[1], up_weight.shape[1]
    heads = q_cols // HD
    wide = heads * TILE
    blocks, own_blocks = full_len // TILE, own_len // TILE
    frequencies = (10000.0 ** (-np.arange(0, ROT, 2, dtype=np.float32) / ROT)).astype(np.float32)
    angles = frequencies[:, None] * np.arange(full_len, dtype=np.float32)[None, :]
    table = np.concatenate([np.cos(angles), np.sin(angles)], axis=0).astype(np.float32)
    norms = jnp.stack([norm_gain_one, norm_bias_one, norm_gain_two, norm_bias_two] * 2)

    slices = width // LANES
    units = 2 * slices + 4
    small_rows = LANES
    extra = max(1, len(plan.extra))
    vmem = lambda *shape, kind=BF: pltpu.VMEM(shape, kind)
    dma = lambda *shape: pltpu.SemaphoreType.DMA(shape)
    scratch = [
        vmem(blocks, width, TILE),
        vmem(blocks, width, TILE),
        vmem(blocks, width, TILE),
        vmem(blocks, width, TILE),
        vmem(blocks, width, TILE),
        vmem(hidden, width),
        vmem(width, hidden),
        vmem(q_cols + kv_cols, width),
        vmem(width, q_cols + kv_cols),
        vmem(width, q_cols),
        vmem(blocks, HD, wide),
        vmem(blocks, HD, TILE),
        vmem(blocks, TILE, HD),
        vmem(blocks, HD + 16, TILE),
        vmem(blocks, TILE, HD),
        vmem(blocks, HD, wide),
        vmem(blocks, q_cols + kv_cols, TILE),
        vmem(width, 8, kind=F32),
        vmem(width, LANES, kind=F32),
        vmem(q_cols, width, kind=F32),
        vmem(q_cols + kv_cols, width, kind=F32),
        vmem(blocks, TILE, wide, kind=F32),
        vmem(blocks, TILE, wide),
        vmem(HD + 16, wide, kind=F32),
        vmem(blocks, TILE, HD, kind=F32),
        vmem(blocks, TILE, HD, kind=F32),
        vmem(units, width, LANES),
        vmem(units, width - width // 8, LANES),
        vmem(units, extra, width // 8, LANES),
        vmem(1, small_rows, LANES),
        vmem(1, small_rows - small_rows // 8, LANES),
        vmem(1, extra, small_rows // 8, LANES),
        vmem(4, width // 8, LANES),
        vmem(4, small_rows // 8, LANES),
        vmem(2, blocks // 2, width // 2, TILE),
        vmem(2, own_blocks, width, TILE),
        vmem(2, own_blocks, width, TILE),
        dma(2, own_blocks, 3),
        dma(2, own_blocks, 3),
        dma(2, blocks),
        dma(2, blocks),
        dma(2, blocks),
        dma(2, own_blocks, 2),
        dma(units, plan.stages),
        dma(units, plan.stages),
        dma(1, plan.stages),
        dma(1, plan.stages),
        dma(2, 3),
        dma(2, 3),
    ]
    in_vmem = pl.BlockSpec(memory_space=pltpu.VMEM)
    in_smem = pl.BlockSpec(memory_space=pltpu.SMEM)
    block_out, grad_tokens, total, total_small = pl.pallas_call(
        functools.partial(block_kernel, plan),
        out_shape=(
            jax.ShapeDtypeStruct((width, own_len), BF),
            jax.ShapeDtypeStruct((width, own_len), BF),
            jax.ShapeDtypeStruct((units, width, LANES), BF),
            jax.ShapeDtypeStruct((1, small_rows, LANES), BF),
        ),
        in_specs=[in_smem] * 2 + [in_vmem] * 9,
        out_specs=(in_vmem,) * 4,
        scratch_shapes=scratch,
        compiler_params=pltpu.CompilerParams(
            collective_id=0, has_side_effects=True, vmem_limit_bytes=63 << 20
        ),
    )(
        tags,
        tag_weight,
        tokens[0],
        cotangent[0],
        query_weight,
        key_value_weight,
        output_weight,
        up_weight,
        down_weight,
        norms,
        jnp.asarray(table),
    )
    split = total[: 2 * slices].reshape(slices, 2, width, LANES).transpose(1, 2, 0, 3)
    grad_downward, grad_upward = split.reshape(2, width, width).astype(F32)
    ends = total[2 * slices : 2 * slices + 3].reshape(slices, 2, q_cols, LANES)
    grad_output = ends[:, 0].transpose(1, 0, 2).reshape(q_cols, width).astype(F32)
    grad_query = ends[:, 1].transpose(0, 2, 1).reshape(width, q_cols).astype(F32)
    grad_keyval = total[2 * slices + 3].astype(F32)
    rows = total_small[0, : 16 * slices].reshape(slices, 16, LANES)[:, :4]
    rows = rows.transpose(1, 0, 2).reshape(4, width).astype(F32)
    return (
        block_out.T[None],
        grad_tokens.T[None],
        grad_query,
        grad_keyval,
        grad_output,
        grad_upward,
        grad_downward,
        rows[0],
        rows[1],
        rows[2],
        rows[3],
    )


def solution(mesh):
    rows = P("dp", "tp", None)
    columns, depth, whole = P(None, "tp"), P("tp", None), P()
    in_specs = (rows, rows, P("dp"), whole, columns, whole, depth, columns, depth) + (whole,) * 4
    out_specs = (rows, rows, columns, whole, depth, columns, depth) + (whole,) * 4
    return jax.shard_map(
        functools.partial(shards, mesh.shape["dp"]),
        mesh=mesh,
        in_specs=in_specs,
        out_specs=out_specs,
        check_vma=False,
    )
```

```python
import functools

import jax
import jax.numpy as jnp
import numpy as np
from jax import lax
from jax.experimental import pallas as pl
from jax.experimental.pallas import tpu as pltpu
from jax.sharding import PartitionSpec as P

HD = 64
ROT = 16
HALF = ROT // 2
TILE = 256
LANES = 128
MESH = pl.DeviceIdType.MESH
BF = jnp.bfloat16
F32 = jnp.float32


def mm(left, right):
    return jnp.dot(left, right, preferred_element_type=F32)


def mm_t(left, right):
    return lax.dot_general(left, right, (((1,), (1,)), ((), ())), preferred_element_type=F32)


def turn(values, cosine, sine):
    front, back = values[:HALF], values[HALF:ROT]
    return jnp.concatenate(
        [front * cosine - back * sine, back * cosine + front * sine, values[ROT:]], axis=0
    )


class Plan:
    def __init__(self, dp):
        self.bits = dp.bit_length() - 1
        self.extra = [2**position for position in range(3, self.bits)]
        self.stages = 6 + len(self.extra)
        self.lag = [1 + 2 * stage for stage in range(self.stages - 1)]
        self.lag.append(self.lag[-1] + 4)

    def strides(self, kind):
        return (1 + kind, 2 - kind, 4)


class Bundle:
    def __init__(self, plan, d, t, part, landed, swapped, total, send, recv):
        self.plan, self.d, self.t = plan, d, t
        self.part, self.landed, self.swapped, self.total = part, landed, swapped, total
        self.send, self.recv = send, recv
        self.rows = part.shape[1]

    def bit(self, stride):
        return (self.d // stride) % 2

    def partner(self, stride):
        return self.d + (1 - 2 * self.bit(stride)) * stride

    def span(self, kind, depth):
        start = 0
        for level in range(depth):
            start = start + self.bit(self.plan.strides(kind)[level]) * (self.rows >> (level + 1))
        return pl.multiple_of(start, 16), self.rows >> depth

    def copy(self, unit, kind, stage):
        order, extra = self.plan.strides(kind), self.plan.extra
        if stage < 3:
            start, size = self.span(kind, stage)
            position = order[stage]
            half = size // 2
            other = pl.multiple_of(start + (1 - self.bit(position)) * half, 16)
            source = self.part.at[unit, pl.ds(other, half)]
            target = self.landed.at[unit, pl.ds(self.rows - size, half)]
        elif stage < 3 + len(extra):
            start, size = self.span(kind, 3)
            position = extra[stage - 3]
            source = self.part.at[unit, pl.ds(start, size)]
            target = self.swapped.at[unit, stage - 3]
        else:
            depth = self.plan.stages - stage
            start, size = self.span(kind, depth)
            position = order[depth - 1]
            source = self.total.at[unit, pl.ds(start, size)]
            target = source
        return pltpu.make_async_remote_copy(
            src_ref=source,
            dst_ref=target,
            send_sem=self.send.at[unit, stage],
            recv_sem=self.recv.at[unit, stage],
            device_id=(self.partner(position), self.t),
            device_id_type=MESH,
        )

    def start(self, unit, kind, stage):
        self.copy(unit, kind, stage).start()

    def finish(self, unit, kind, stage, publish=True):
        self.copy(unit, kind, stage).wait()
        last = 2 + len(self.plan.extra)
        if stage <= last:
            if stage < 3:
                start, size = self.span(kind, stage + 1)
                arrived = self.landed[unit, pl.ds(self.rows - 2 * size, size)]
            else:
                start, size = self.span(kind, 3)
                arrived = self.swapped[unit, stage - 3]
            mine = self.part[unit, pl.ds(start, size)]
            summed = (mine.astype(F32) + arrived.astype(F32)).astype(BF)
            if stage == last and publish:
                self.total[unit, pl.ds(start, size)] = summed
            else:
                self.part[unit, pl.ds(start, size)] = summed


def block_kernel(
    plan,
    tags_ref,
    tag_weight_ref,
    tok_ref,
    cot_ref,
    query_t_ref,
    keyval_ref,
    output_ref,
    up_ref,
    down_ref,
    gain_one_ref,
    bias_one_ref,
    gain_two_ref,
    bias_two_ref,
    table_ref,
    block_out_ref,
    grad_tokens_ref,
    total_ref,
    total_small_ref,
    x_all,
    gr_all,
    n1_all,
    br_all,
    g_all,
    up_t,
    down_t,
    qkv_t,
    qkv_w,
    out_t,
    q_t,
    k_t,
    k_r,
    v_t,
    v_r,
    do_t,
    gq_all,
    norms_c,
    norms_r,
    bias_acc,
    sum_out,
    sum_qkv,
    score,
    prob,
    acc,
    d_key,
    d_value,
    part,
    landed,
    swapped,
    part_small,
    landed_small,
    swapped_small,
    tp_land,
    tp_land_small,
    pre,
    from_sib,
    from_x,
    ag_send,
    ag_recv,
    rs_send,
    rs_recv,
    rs_send_x,
    rs_recv_x,
    dp_send,
    dp_recv,
    dp_send_small,
    dp_recv_small,
    tp_send,
    tp_recv,
):
    d, t = lax.axis_index("dp"), lax.axis_index("tp")
    chip, core = t // 2, t % 2
    sib = t + 1 - 2 * core
    across = (t + 2) % 4
    diag = (sib + 2) % 4
    width = tok_ref.shape[1]
    hidden = up_ref.shape[1]
    q_cols = query_t_ref.shape[0]
    heads = q_cols // HD
    own_blocks = tok_ref.shape[0] // TILE
    blocks = 4 * own_blocks
    half_width = width // 2
    tall = width // TILE

    big = Bundle(plan, d, t, part, landed, swapped, total_ref, dp_send, dp_recv)
    small = Bundle(
        plan, d, t, part_small, landed_small, swapped_small, total_small_ref, dp_send_small, dp_recv_small
    )

    barrier = pltpu.get_barrier_semaphore()
    peers = [(d, sib), (d, across), (d, diag)] + [(big.partner(2**b), t) for b in range(plan.bits)]
    for peer in peers:
        pl.semaphore_signal(barrier, inc=1, device_id=peer, device_id_type=MESH)
    pl.semaphore_wait(barrier, len(peers))

    row_weight = tag_weight_ref[tags_ref[0]]

    sets = (x_all, gr_all)

    def pair(ref, block):
        return jnp.concatenate([ref[2 * block], ref[2 * block + 1]], axis=1)

    def put_pair(ref, block, value):
        ref[2 * block] = value[:, :LANES]
        ref[2 * block + 1] = value[:, LANES:]

    def half_lanes(start, half):
        return pl.ds(pl.multiple_of(start + half * LANES, LANES), LANES)

    def gather_copy(kind, piece, half, owner, route):
        place = owner * own_blocks + piece
        target = {0: sib, 1: across, 2: sib}[route]
        view = sets[kind].at[2 * place + half]
        return pltpu.make_async_remote_copy(
            src_ref=view,
            dst_ref=view,
            send_sem=ag_send.at[kind, piece, half, route],
            recv_sem=ag_recv.at[kind, piece, half, route],
            device_id=(d, target),
            device_id_type=MESH,
        )

    for piece in range(own_blocks):
        rows = slice(piece * TILE, (piece + 1) * TILE)
        put_pair(x_all, t * own_blocks + piece, tok_ref[rows, :].T)
        for half in range(2):
            gather_copy(0, piece, half, t, 0).start()
        gather_copy(0, piece, 0, t, 1).start()
        weighted = (cot_ref[rows, :].astype(F32) * row_weight).astype(BF).T
        put_pair(gr_all, t * own_blocks + piece, weighted)
        for half in range(2):
            gather_copy(1, piece, half, t, 0).start()
        gather_copy(1, piece, 0, t, 1).start()
        gather_copy(0, piece, 1, t, 1).start()
        gather_copy(1, piece, 1, t, 1).start()

    up_t[...] = up_ref[...].T
    down_t[...] = down_ref[...].T
    qkv_t[:q_cols] = query_t_ref[...]
    qkv_t[q_cols:] = keyval_ref[...].T
    qkv_w[...] = qkv_t[...].T
    out_t[...] = output_ref[...].T
    for index, norm in enumerate((gain_one_ref, bias_one_ref, gain_two_ref, bias_two_ref)):
        norms_r[index : index + 1] = norm[...].reshape(1, width)
    norms_c[...] = norms_r[...].T
    score[...] = jnp.zeros_like(score)
    bias_acc[...] = jnp.zeros_like(bias_acc)
    sum_out[...] = jnp.zeros_like(sum_out)
    sum_qkv[...] = jnp.zeros_like(sum_qkv)
    d_key[...] = jnp.zeros_like(d_key)
    d_value[...] = jnp.zeros_like(d_value)

    def standardize(x):
        mean = jnp.sum(x, axis=0, keepdims=True) * (1.0 / width)
        centred = x - mean
        variance = jnp.sum(centred * centred, axis=0, keepdims=True) * (1.0 / width)
        inverse = lax.rsqrt(variance + 1e-05)
        return centred * inverse, inverse

    def feed_forward(step, carry):
        late, piece, half = step // 4, (step % 4) // 2, step % 2
        owners = (
            (1 - late) * t + late * across,
            (1 - late) * sib + late * diag,
        )
        places = [owner * own_blocks + piece for owner in owners]
        sides = [slice(0, LANES), slice(LANES, TILE)]

        @pl.when(late == 0)
        def _():
            for kind in range(2):
                gather_copy(kind, piece, half, sib, 0).wait_recv()

        @pl.when(late == 1)
        def _():
            for kind in range(2):
                gather_copy(kind, piece, half, across, 1).wait_recv()
                gather_copy(kind, piece, half, across, 2).start()
            for kind in range(2):
                gather_copy(kind, piece, half, diag, 2).wait_recv()

        def load(ref):
            return jnp.concatenate([ref[2 * place + half] for place in places], axis=1)

        def store(ref, value):
            for place, side in zip(places, sides):
                ref[2 * place + half] = value[:, side]

        normal, _ = standardize(load(x_all).astype(F32))
        n1 = (normal * norms_c[:, 0:1] + norms_c[:, 1:2]).astype(BF)
        n2 = (normal * norms_c[:, 2:3] + norms_c[:, 3:4]).astype(BF)
        store(n1_all, n1)
        gr = load(gr_all)
        qkv = mm(qkv_t[...], n1)
        lanes = [half_lanes(place * TILE, half) for place in places]
        cosine = jnp.concatenate([table_ref[:HALF, at] for at in lanes], axis=1)
        sine = jnp.concatenate([table_ref[HALF:, at] for at in lanes], axis=1)
        grad_context = mm(output_ref[...], gr)
        for head in range(heads):
            rows = slice(head * HD, (head + 1) * HD)
            turned = (turn(qkv[rows], cosine, sine) * (HD**-0.5)).astype(BF)
            grads = grad_context[rows].astype(BF)
            for place, side in zip(places, sides):
                at = slice(head * LANES, (head + 1) * LANES)
                q_t[2 * place + half, :, at] = turned[:, side]
                do_t[2 * place + half, :, at] = grads[:, side]
        key = turn(qkv[q_cols : q_cols + HD], cosine, sine)
        value = qkv[q_cols + HD :]
        for place, side, at in zip(places, sides, lanes):
            k_t[:, at] = key[:, side].astype(BF)
            v_t[:HD, at] = value[:, side].astype(BF)
            v_t[HD:, at] = jnp.ones((v_t.shape[0] - HD, LANES), BF)
            k_r[place, half_lanes(0, half), :] = key[:, side].T.astype(BF)
            v_r[place, half_lanes(0, half), :] = value[:, side].T.astype(BF)

        pre_act = mm(up_t[...], n2)
        cdf = 0.5 + 0.5 * lax.erf(pre_act * 0.7071067811865476)
        density = jnp.exp(-0.5 * pre_act * pre_act) * 0.3989422804014327
        middle = (pre_act * cdf).astype(BF)
        slope = cdf + pre_act * density
        store(br_all, mm(down_t[...], middle).astype(BF))
        grad_hidden = (mm(down_ref[...], gr) * slope).astype(BF)
        up_two = mm(up_ref[...], grad_hidden)
        bias_acc[...] += up_two[:, :LANES] + up_two[:, LANES:]
        store(g_all, (up_two * norms_c[:, 2:3]).astype(BF))
        score[:tall] += mm_t(middle, gr).reshape(tall, TILE, width)
        score[tall : 2 * tall] += mm_t(n2, grad_hidden).reshape(tall, TILE, hidden)
        return carry

    lax.fori_loop(0, blocks, feed_forward, 0)

    def gathered(index, carry):
        piece, half = index // 2, index % 2
        for kind in range(2):
            gather_copy(kind, piece, half, t, 0).wait_send()
            gather_copy(kind, piece, half, t, 1).wait_send()
            gather_copy(kind, piece, half, across, 2).wait_send()
        return carry

    lax.fori_loop(0, 2 * own_blocks, gathered, 0)

    slices = width // LANES
    for index in range(slices):
        cols = slice(index * LANES, (index + 1) * LANES)
        part[2 * index] = score[:tall, :, cols].reshape(hidden, LANES).astype(BF)
        big.start(2 * index, (2 * index) % 4 // 3, 0)
        part[2 * index + 1] = score[tall : 2 * tall, :, cols].reshape(width, LANES).astype(BF)
        big.start(2 * index + 1, (2 * index + 1) % 4 // 3, 0)
    for index in range(tall):
        rows = slice(index * TILE, (index + 1) * TILE)
        product = jnp.sum(up_ref[rows, :].astype(F32) * score[tall + index], axis=1, keepdims=True)
        norms_c[rows, 4:5] = product
    norms_c[:, 5:6] = jnp.sum(bias_acc[...], axis=1, keepdims=True)
    bias_acc[...] = jnp.zeros_like(bias_acc)

    outs = (br_all, g_all)

    def block_of(step):
        return (blocks - 1) - step // 2 - (blocks // 2) * (step % 2)

    def pre_copy(kind, step, block):
        rows = pl.ds(pl.multiple_of((1 - core) * half_width, 16), half_width)
        return pltpu.make_async_remote_copy(
            src_ref=outs[kind].at[pl.ds(2 * block, 2), rows],
            dst_ref=pre.at[kind, step // 2],
            send_sem=rs_send.at[kind, step],
            recv_sem=rs_recv.at[kind, step],
            device_id=(d, sib),
            device_id_type=MESH,
        )

    def sib_copy(kind, step, block):
        return pltpu.make_async_remote_copy(
            src_ref=outs[kind].at[pl.ds(2 * block, 2)],
            dst_ref=from_sib.at[kind, block % own_blocks],
            send_sem=rs_send.at[kind, step],
            recv_sem=rs_recv.at[kind, step],
            device_id=(d, sib),
            device_id_type=MESH,
        )

    def x_copy(kind, block, sender_core, owner):
        rows = pl.ds(pl.multiple_of(sender_core * half_width, 16), half_width)
        return pltpu.make_async_remote_copy(
            src_ref=outs[kind].at[pl.ds(2 * block, 2), rows],
            dst_ref=from_x.at[kind, block % own_blocks, :, rows],
            send_sem=rs_send_x.at[kind, block],
            recv_sem=rs_recv_x.at[kind, block % own_blocks, sender_core],
            device_id=(d, owner),
            device_id_type=MESH,
        )

    def scatter_first(kind, step):
        block = block_of(step)
        owner = block // own_blocks

        @pl.when(owner // 2 != chip)
        def _():
            pre_copy(kind, step, block).start()

        @pl.when((owner // 2 == chip) & (owner != t))
        def _():
            sib_copy(kind, step, block).start()

    def scatter_second(kind, step):
        block = block_of(step)
        owner = block // own_blocks

        @pl.when(owner // 2 != chip)
        def _():
            pre_copy(kind, step, block).wait()
            rows = pl.ds(pl.multiple_of(core * half_width, 16), half_width)
            mine = outs[kind][pl.ds(2 * block, 2), rows].astype(F32)
            outs[kind][pl.ds(2 * block, 2), rows] = (mine + pre[kind, step // 2].astype(F32)).astype(BF)
            x_copy(kind, block, core, owner).start()

        @pl.when((owner // 2 == chip) & (owner != t))
        def _():
            sib_copy(kind, step, block).wait_send()

    def scatter_sent(kind, step):
        block = block_of(step)
        owner = block // own_blocks

        @pl.when(owner // 2 != chip)
        def _():
            x_copy(kind, block, core, owner).wait_send()

    def scatter_arrived(kind, piece):
        block = t * own_blocks + piece
        step = 2 * ((blocks - 1 - block) % (blocks // 2)) + 1 - block // (blocks // 2)
        sib_copy(kind, step, block).wait_recv()
        for sender_core in range(2):
            x_copy(kind, block, sender_core, t).wait_recv()
        halves = [
            outs[kind][2 * block + half].astype(F32)
            + from_sib[kind, piece, half].astype(F32)
            + from_x[kind, piece, half].astype(F32)
            for half in range(2)
        ]
        return jnp.concatenate(halves, axis=1)

    def emit_block_out(piece):
        cols = slice(piece * TILE, (piece + 1) * TILE)
        x = pair(x_all, t * own_blocks + piece).astype(F32)
        block_out_ref[:, cols] = (x + scatter_arrived(0, piece)).astype(BF)

    def emit_grad_tokens(piece):
        place = t * own_blocks + piece
        scaled = scatter_arrived(1, piece)
        normal, inverse = standardize(pair(x_all, place).astype(F32))
        mean_one = jnp.sum(scaled, axis=0, keepdims=True) * (1.0 / width)
        mean_two = jnp.sum(scaled * normal, axis=0, keepdims=True) * (1.0 / width)
        grad_tokens_ref[:, piece * TILE : (piece + 1) * TILE] = (
            pair(gr_all, place).astype(F32) + inverse * (scaled - mean_one - normal * mean_two)
        ).astype(BF)

    base = 2 * slices

    def slot(index):
        for stage in reversed(range(plan.stages)):
            unit = index - plan.lag[stage]

            @pl.when((unit >= 0) & (unit < base))
            def _():
                kind = (unit % 4) // 3
                big.finish(unit, kind, stage)
                if stage + 1 < plan.stages:
                    big.start(unit, kind, stage + 1)

    def attend(step, carry):
        slot(3 * step)
        block = block_of(step)
        queries = jnp.concatenate([q_t[2 * block], q_t[2 * block + 1]], axis=1)
        wide = heads * TILE

        def in_pairs(count, body, start):
            carry = lax.fori_loop(0, count // 4, lambda i, c: body(4 * i, 4, c), start)
            carry = lax.fori_loop(count // 4 * 2, count // 2, lambda i, c: body(2 * i, 2, c), carry)
            return lax.fori_loop(count // 2 * 2, count, lambda i, c: body(i, 1, c), carry)

        def lanes_of(j, tiles):
            return pl.ds(pl.multiple_of(j * TILE, TILE), tiles * TILE)

        def scores(j, tiles, top):
            tile = mm(k_r[pl.ds(j, tiles)].reshape(tiles * TILE, HD), queries)
            score[pl.ds(j, tiles)] = tile.reshape(tiles, TILE, wide)
            return jnp.maximum(top, jnp.max(tile.reshape(tiles * TILE // 8, 8, wide), axis=0))

        top = in_pairs(block, scores, jnp.full((8, wide), -1e30, F32))
        tile = mm(k_r[block], queries)
        past = lax.broadcasted_iota(jnp.int32, (TILE, wide), 0)
        now = lax.broadcasted_iota(jnp.int32, (TILE, wide), 1)
        now = now // (wide // 2) * LANES + now % LANES
        tile = jnp.where(past <= now, tile, -1e30)
        score[block] = tile
        top = jnp.maximum(top, jnp.max(tile.reshape(TILE // 8, 8, wide), axis=0))
        top = jnp.max(top, axis=0, keepdims=True)

        acc[...] = jnp.zeros_like(acc)
        slot(3 * step + 1)

        def weigh(j, tiles, carry):
            weights = jnp.exp(score[pl.ds(j, tiles)] - top).astype(BF)
            prob[pl.ds(j, tiles)] = weights
            acc[...] += mm(v_t[:, lanes_of(j, tiles)], weights.reshape(tiles * TILE, wide))
            return carry

        in_pairs(block + 1, weigh, 0)
        inverse = 1.0 / acc[HD : HD + 1]
        context = acc[:HD] * inverse
        grad = (pair(do_t, block).astype(F32) * inverse).astype(BF)
        delta = jnp.sum(grad.astype(F32) * context, axis=0, keepdims=True)
        acc[:HD] = jnp.zeros((HD, wide), F32)

        slot(3 * step + 2)

        def back(j, tiles, carry):
            weights = prob[pl.ds(j, tiles)].reshape(tiles * TILE, wide)
            grad_probs = mm(v_r[pl.ds(j, tiles)].reshape(tiles * TILE, HD), grad)
            grad_scores = (weights.astype(F32) * (grad_probs - delta)).astype(BF)
            acc[:HD] += mm(k_t[:, lanes_of(j, tiles)], grad_scores)
            d_key[:, lanes_of(j, tiles)] += mm_t(queries, grad_scores)
            d_value[:, lanes_of(j, tiles)] += mm_t(grad, weights)
            return carry

        in_pairs(block + 1, back, 0)
        lanes = pl.ds(pl.multiple_of(block * TILE, TILE), TILE)
        cosine, sine = table_ref[:HALF, lanes], table_ref[HALF:, lanes]
        def of_head(value, head):
            first = value[:, head * LANES : (head + 1) * LANES]
            second = value[:, (heads + head) * LANES : (heads + head + 1) * LANES]
            return jnp.concatenate([first, second], axis=1)

        grad_queries = acc[:HD]
        for head in range(heads):
            turned = turn(of_head(grad_queries, head), cosine, -sine) * (HD**-0.5)
            gq_all[block, head * HD : (head + 1) * HD] = turned.astype(BF)
        context = jnp.concatenate([of_head(context, h) for h in range(heads)], axis=0).astype(BF)
        branch = mm(out_t[...], context) + pair(br_all, block).astype(F32)
        put_pair(br_all, block, branch.astype(BF))
        sum_out[...] += mm_t(context, pair(gr_all, block))
        sum_qkv[:q_cols] += mm_t(gq_all[block, :q_cols], pair(n1_all, block))
        scatter_first(0, step)

        @pl.when(step > 0)
        def _():
            scatter_second(0, step - 1)

        return carry

    lax.fori_loop(0, blocks, attend, 0)
    scatter_second(0, blocks - 1)

    for index in range(slices):
        cols = slice(index * LANES, (index + 1) * LANES)
        for which, source in ((0, sum_out[:, cols]), (1, sum_qkv[:q_cols, cols])):
            row = (2 * index + which) * q_cols
            part[base + row // width, row % width : row % width + q_cols] = source.astype(BF)
    first_ends = [(big, base, 0), (big, base + 1, 1), (big, base + 2, 0)]
    for bundle, unit, kind in first_ends:
        bundle.start(unit, kind, 0)

    def project(step, carry):
        slot(3 * blocks + step)
        block = block_of(step)
        lanes = pl.ds(pl.multiple_of(block * TILE, TILE), TILE)
        cosine, sine = table_ref[:HALF, lanes], table_ref[HALF:, lanes]
        gq_all[block, q_cols : q_cols + HD] = turn(d_key[:, lanes], cosine, -sine).astype(BF)
        gq_all[block, q_cols + HD :] = d_value[:, lanes].astype(BF)
        grads = gq_all[block]
        up_one = mm(qkv_w[...], grads)
        bias_acc[...] += up_one[:, :LANES] + up_one[:, LANES:]
        put_pair(g_all, block, (pair(g_all, block).astype(F32) + up_one * norms_c[:, 0:1]).astype(BF))
        sum_qkv[q_cols:] += mm_t(grads[q_cols:], pair(n1_all, block))
        scatter_first(1, step)

        @pl.when(step > 0)
        def _():
            scatter_second(1, step - 1)

        for stage, when in ((0, 4), (1, 7)):

            @pl.when(step == when)
            def _():
                for bundle, unit, kind in first_ends:
                    bundle.finish(unit, kind, stage)
                    bundle.start(unit, kind, stage + 1)

        return carry

    lax.fori_loop(0, blocks, project, 0)
    scatter_second(1, blocks - 1)
    for index in range(4 * blocks, base + plan.lag[-1]):
        slot(index)

    grad_keyval = sum_qkv[q_cols:].T
    part[base + 3] = grad_keyval.astype(BF)
    shift_one = jnp.sum(bias_acc[...], axis=1, keepdims=True)
    shift_two = norms_c[:, 5:6]
    product_one = jnp.sum(qkv_t[...].astype(F32) * sum_qkv[...], axis=0, keepdims=True)
    product_one = jnp.broadcast_to(product_one, (8, width)).T[:, :1]
    gain_one = (product_one - norms_c[:, 1:2] * shift_one) / norms_c[:, 0:1]
    gain_two = (norms_c[:, 4:5] - norms_c[:, 3:4] * shift_two) / norms_c[:, 2:3]
    lane = lax.broadcasted_iota(jnp.int32, (width, 8), 1)
    columns = jnp.where(
        lane == 0, gain_one, jnp.where(lane == 1, shift_one, jnp.where(lane == 2, gain_two, shift_two))
    )
    rows = columns.T
    part_small[0] = jnp.zeros(part_small.shape[1:], BF)
    for index in range(slices):
        part_small[0, 16 * index : 16 * index + 8] = rows[
            :, index * LANES : (index + 1) * LANES
        ].astype(BF)

    last_ends = [(big, base + 3, 1), (small, 0, 0)]
    for bundle, unit, kind in last_ends:
        bundle.start(unit, kind, 0)
    lands = (tp_land, tp_land_small)

    def tp_copy(index, sender, hop):
        return pltpu.make_async_remote_copy(
            src_ref=lands[index].at[sender],
            dst_ref=lands[index].at[sender],
            send_sem=tp_send.at[index, hop],
            recv_sem=tp_recv.at[index, hop],
            device_id=(d, (t + hop + 1) % 4),
            device_id_type=MESH,
        )

    middle_stage = 2 + len(plan.extra)
    for beat in range(plan.stages + 1):
        stage = beat + 2
        if stage < plan.stages:
            for bundle, unit, kind in first_ends:
                bundle.finish(unit, kind, stage)
                if stage + 1 < plan.stages:
                    bundle.start(unit, kind, stage + 1)
        for index, (bundle, unit, kind) in enumerate(last_ends):
            rows = pl.ds(*bundle.span(kind, 3))
            if beat < middle_stage:
                bundle.finish(unit, kind, beat)
                bundle.start(unit, kind, beat + 1)
            elif beat == middle_stage:
                bundle.finish(unit, kind, beat, publish=False)
                lands[index][t] = bundle.part[unit, rows]
                for hop in range(3):
                    tp_copy(index, t, hop).start()
            elif beat == middle_stage + 1:
                for hop in range(3):
                    tp_copy(index, (t + 3 - hop) % 4, hop).wait_recv()
                land = [lands[index][sender].astype(F32) for sender in range(4)]
                bundle.total[unit, rows] = (land[0] + land[1] + land[2] + land[3]).astype(BF)
                bundle.start(unit, kind, beat)
            else:
                bundle.finish(unit, kind, beat - 1)
                if beat < plan.stages:
                    bundle.start(unit, kind, beat)
        if beat == 0:
            for piece in range(own_blocks):
                emit_block_out(piece)
    for index in range(2):
        for hop in range(3):
            tp_copy(index, t, hop).wait_send()
    for piece in range(own_blocks):
        emit_grad_tokens(piece)

    def drain(step, carry):
        for kind in range(2):
            scatter_sent(kind, step)
        return carry

    lax.fori_loop(0, blocks, drain, 0)


def finish_kernel(
    block_out_t,
    grad_tokens_t,
    split,
    ends,
    keyval,
    small,
    block_out_ref,
    grad_tokens_ref,
    grad_query_ref,
    grad_keyval_ref,
    grad_output_ref,
    grad_up_ref,
    grad_down_ref,
    *vector_refs,
):
    block_out_ref[...] = block_out_t[...].T
    grad_tokens_ref[...] = grad_tokens_t[...].T
    grad_output_ref[...] = ends[0].astype(F32)
    grad_query_ref[...] = ends[1].astype(F32)
    grad_keyval_ref[...] = keyval[0].astype(F32)
    grad_down_ref[...] = split[0].astype(F32)
    grad_up_ref[...] = split[1].astype(F32)
    for index, vector in enumerate(vector_refs):
        rows = [small[0, 16 * k + index : 16 * k + index + 1] for k in range(pl.num_programs(0))]
        vector[...] = jnp.concatenate(rows, axis=1).astype(F32).reshape(vector.shape)


def shards(
    dp,
    tokens,
    cotangent,
    tags,
    tag_weight,
    query_weight,
    key_value_weight,
    output_weight,
    up_weight,
    down_weight,
    norm_gain_one,
    norm_bias_one,
    norm_gain_two,
    norm_bias_two,
):
    plan = Plan(dp)
    _, own_len, width = tokens.shape
    full_len = 4 * own_len
    q_cols, kv_cols, hidden = query_weight.shape[1], key_value_weight.shape[1], up_weight.shape[1]
    heads = q_cols // HD
    wide = heads * TILE
    blocks, own_blocks = full_len // TILE, own_len // TILE
    frequencies = (10000.0 ** (-np.arange(0, ROT, 2, dtype=np.float32) / ROT)).astype(np.float32)
    angles = frequencies[:, None] * np.arange(full_len, dtype=np.float32)[None, :]
    table = np.concatenate([np.cos(angles), np.sin(angles)], axis=0).astype(np.float32)

    slices = width // LANES
    units = 2 * slices + 4
    small_rows = LANES
    extra = max(1, len(plan.extra))
    vmem = lambda *shape, kind=BF: pltpu.VMEM(shape, kind)
    dma = lambda *shape: pltpu.SemaphoreType.DMA(shape)
    scratch = [
        vmem(2 * blocks, width, LANES),
        vmem(2 * blocks, width, LANES),
        vmem(2 * blocks, width, LANES),
        vmem(2 * blocks, width, LANES),
        vmem(2 * blocks, width, LANES),
        vmem(hidden, width),
        vmem(width, hidden),
        vmem(q_cols + kv_cols, width),
        vmem(width, q_cols + kv_cols),
        vmem(width, q_cols),
        vmem(2 * blocks, HD, wide // 2),
        vmem(HD, full_len),
        vmem(blocks, TILE, HD),
        vmem(HD + 16, full_len),
        vmem(blocks, TILE, HD),
        vmem(2 * blocks, HD, wide // 2),
        vmem(blocks, q_cols + kv_cols, TILE),
        vmem(width, 8, kind=F32),
        vmem(8, width, kind=F32),
        vmem(width, LANES, kind=F32),
        vmem(q_cols, width, kind=F32),
        vmem(q_cols + kv_cols, width, kind=F32),
        vmem(blocks, TILE, wide, kind=F32),
        vmem(blocks, TILE, wide),
        vmem(HD + 16, wide, kind=F32),
        vmem(HD, full_len, kind=F32),
        vmem(HD, full_len, kind=F32),
        vmem(units, width, LANES),
        vmem(units, width - width // 8, LANES),
        vmem(units, extra, width // 8, LANES),
        vmem(1, small_rows, LANES),
        vmem(1, small_rows - small_rows // 8, LANES),
        vmem(1, extra, small_rows // 8, LANES),
        vmem(4, width // 8, LANES),
        vmem(4, small_rows // 8, LANES),
        vmem(2, blocks // 2, 2, width // 2, LANES),
        vmem(2, own_blocks, 2, width, LANES),
        vmem(2, own_blocks, 2, width, LANES),
        dma(2, own_blocks, 2, 3),
        dma(2, own_blocks, 2, 3),
        dma(2, blocks),
        dma(2, blocks),
        dma(2, blocks),
        dma(2, own_blocks, 2),
        dma(units, plan.stages),
        dma(units, plan.stages),
        dma(1, plan.stages),
        dma(1, plan.stages),
        dma(2, 3),
        dma(2, 3),
    ]
    in_vmem = pl.BlockSpec(memory_space=pltpu.VMEM)
    in_smem = pl.BlockSpec(memory_space=pltpu.SMEM)
    block_out, grad_tokens, total, total_small = pl.pallas_call(
        functools.partial(block_kernel, plan),
        out_shape=(
            jax.ShapeDtypeStruct((width, own_len), BF),
            jax.ShapeDtypeStruct((width, own_len), BF),
            jax.ShapeDtypeStruct((units, width, LANES), BF),
            jax.ShapeDtypeStruct((1, small_rows, LANES), BF),
        ),
        in_specs=[in_smem] * 2 + [in_vmem] * 12,
        out_specs=(in_vmem,) * 4,
        scratch_shapes=scratch,
        compiler_params=pltpu.CompilerParams(
            collective_id=0, has_side_effects=True, vmem_limit_bytes=63 << 20
        ),
    )(
        tags,
        tag_weight,
        tokens[0],
        cotangent[0],
        query_weight.T,
        key_value_weight,
        output_weight,
        up_weight,
        down_weight,
        norm_gain_one,
        norm_bias_one,
        norm_gain_two,
        norm_bias_two,
        jnp.asarray(table),
    )
    first_end = slices * width // q_cols
    finish_shapes = (
        ((own_len, width), BF),
        ((own_len, width), BF),
        ((q_cols, width), F32),
        ((width, kv_cols), F32),
        ((q_cols, width), F32),
        ((width, hidden), F32),
        ((hidden, width), F32),
        ((width,), F32),
        ((width,), F32),
        ((width,), F32),
        ((width,), F32),
    )
    by_columns = lambda rows: pl.BlockSpec((rows, LANES), lambda i: (0, i))
    by_rows = pl.BlockSpec((LANES, own_len), lambda i: (i, 0))
    block_out, grad_tokens, grad_query, grad_keyval, grad_output, grad_up, grad_down, *vectors = (
        pl.pallas_call(
            finish_kernel,
            grid=(slices,),
            out_shape=tuple(jax.ShapeDtypeStruct(*shape) for shape in finish_shapes),
            in_specs=[
                by_rows,
                by_rows,
                pl.BlockSpec((2, width, LANES), lambda i: (i, 0, 0)),
                pl.BlockSpec((2, q_cols, LANES), lambda i: (first_end + i, 0, 0)),
                pl.BlockSpec((1, width, LANES), lambda i: (2 * slices + 3, 0, 0)),
                pl.BlockSpec((1, small_rows, LANES), lambda i: (0, 0, 0)),
            ],
            out_specs=(
                by_columns(own_len),
                by_columns(own_len),
                by_columns(q_cols),
                pl.BlockSpec((width, kv_cols), lambda i: (0, 0)),
                by_columns(q_cols),
                by_columns(width),
                by_columns(hidden),
                pl.BlockSpec((width,), lambda i: (0,)),
                pl.BlockSpec((width,), lambda i: (0,)),
                pl.BlockSpec((width,), lambda i: (0,)),
                pl.BlockSpec((width,), lambda i: (0,)),
            ),
            compiler_params=pltpu.CompilerParams(vmem_limit_bytes=60 << 20),
        )(
            block_out,
            grad_tokens,
            total,
            total.reshape(units * width // q_cols, q_cols, LANES),
            total,
            total_small,
        )
    )
    return (
        block_out[None],
        grad_tokens[None],
        grad_query.T,
        grad_keyval,
        grad_output,
        grad_up,
        grad_down,
        *vectors,
    )


def solution(mesh):
    rows = P("dp", "tp", None)
    columns, depth, whole = P(None, "tp"), P("tp", None), P()
    in_specs = (rows, rows, P("dp"), whole, columns, whole, depth, columns, depth) + (whole,) * 4
    out_specs = (rows, rows, columns, whole, depth, columns, depth) + (whole,) * 4
    return jax.shard_map(
        functools.partial(shards, mesh.shape["dp"]),
        mesh=mesh,
        in_specs=in_specs,
        out_specs=out_specs,
        check_vma=False,
    )
```

```python
import functools

import jax
import jax.numpy as jnp
import numpy as np
from jax import lax
from jax.experimental import pallas as pl
from jax.experimental.pallas import tpu as pltpu
from jax.sharding import PartitionSpec as P

HD = 64
ROT = 16
HALF = ROT // 2
TILE = 256
LANES = 128
RING = 8
MESH = pl.DeviceIdType.MESH
BF = jnp.bfloat16
F32 = jnp.float32


def mm(left, right):
    return jnp.dot(left, right, preferred_element_type=F32)


def mm_t(left, right):
    return lax.dot_general(left, right, (((1,), (1,)), ((), ())), preferred_element_type=F32)


def turn(values, cosine, sine):
    front, back = values[:HALF], values[HALF:ROT]
    return jnp.concatenate(
        [front * cosine - back * sine, back * cosine + front * sine, values[ROT:]], axis=0
    )


class Plan:
    def __init__(self, dp):
        self.bits = dp.bit_length() - 1
        self.extra = [2**position for position in range(3, self.bits)]
        self.stages = 6 + len(self.extra)
        self.steps = 2 * (RING - 1) + len(self.extra)
        self.slots = 2 * (self.steps + 1)

    def strides(self, kind):
        return (1 + kind, 2 - kind, 4)


class Bundle:
    def __init__(self, plan, d, t, part, landed, swapped, total, send, recv):
        self.plan, self.d, self.t = plan, d, t
        self.part, self.landed, self.swapped, self.total = part, landed, swapped, total
        self.send, self.recv = send, recv
        self.rows = part.shape[1]

    def bit(self, stride):
        return (self.d // stride) % 2

    def partner(self, stride):
        return self.d + (1 - 2 * self.bit(stride)) * stride

    def span(self, kind, depth):
        start = 0
        for level in range(depth):
            start = start + self.bit(self.plan.strides(kind)[level]) * (self.rows >> (level + 1))
        return pl.multiple_of(start, 16), self.rows >> depth

    def copy(self, unit, kind, stage):
        order, extra = self.plan.strides(kind), self.plan.extra
        if stage < 3:
            start, size = self.span(kind, stage)
            position = order[stage]
            half = size // 2
            other = pl.multiple_of(start + (1 - self.bit(position)) * half, 16)
            source = self.part.at[unit, pl.ds(other, half)]
            target = self.landed.at[unit, pl.ds(self.rows - size, half)]
        elif stage < 3 + len(extra):
            start, size = self.span(kind, 3)
            position = extra[stage - 3]
            source = self.part.at[unit, pl.ds(start, size)]
            target = self.swapped.at[unit, stage - 3]
        else:
            depth = self.plan.stages - stage
            start, size = self.span(kind, depth)
            position = order[depth - 1]
            source = self.total.at[unit, pl.ds(start, size)]
            target = source
        return pltpu.make_async_remote_copy(
            src_ref=source,
            dst_ref=target,
            send_sem=self.send.at[unit, stage],
            recv_sem=self.recv.at[unit, stage],
            device_id=(self.partner(position), self.t),
            device_id_type=MESH,
        )

    def start(self, unit, kind, stage):
        self.copy(unit, kind, stage).start()

    def finish(self, unit, kind, stage, publish=True):
        self.copy(unit, kind, stage).wait()
        last = 2 + len(self.plan.extra)
        if stage <= last:
            if stage < 3:
                start, size = self.span(kind, stage + 1)
                arrived = self.landed[unit, pl.ds(self.rows - 2 * size, size)]
            else:
                start, size = self.span(kind, 3)
                arrived = self.swapped[unit, stage - 3]
            mine = self.part[unit, pl.ds(start, size)]
            summed = (mine.astype(F32) + arrived.astype(F32)).astype(BF)
            if stage == last and publish:
                self.total[unit, pl.ds(start, size)] = summed
            else:
                self.part[unit, pl.ds(start, size)] = summed


class Ring:
    def __init__(self, plan, d, t, part, landed, swapped, total, send, recv, height):
        self.plan, self.d, self.t = plan, d, t
        self.part, self.landed, self.swapped, self.total = part, landed, swapped, total
        self.send, self.recv = send, recv
        self.height = height
        self.rows = part.shape[1] // RING
        self.first = d - d % RING
        line, side = (d % RING) // 2, d % 2
        self.place = line + side * (RING - 1 - 2 * line)

    def device(self, place):
        far = place // (RING // 2)
        return self.first + (1 - far) * 2 * place + far * (2 * RING - 1 - 2 * place)

    def neighbour(self, way):
        return self.device((self.place + (1, RING - 1)[way]) % RING)

    def units(self, way, sub):
        return pl.ds((2 * way + sub) * self.height, self.height)

    def chunk(self, way, ahead):
        index = (self.place + RING + (1, -1)[way] * ahead) % RING
        return pl.ds(pl.multiple_of(index * self.rows, 16), self.rows)

    def copy(self, way, sub, phase, index, step):
        units = self.units(way, sub)
        peer = self.neighbour(way)
        if phase == 0:
            source = self.part.at[units, self.chunk(way, -index)]
            slot = pl.ds(pl.multiple_of(index * self.rows, 16), self.rows)
            target = self.landed.at[units, slot]
        elif phase == 1:
            stride = self.plan.extra[index]
            peer = self.d + (1 - 2 * ((self.d // stride) % 2)) * stride
            source = self.part.at[units, self.chunk(way, 1)]
            target = self.swapped.at[units, index]
        else:
            source = self.total.at[units, self.chunk(way, 1 - index)]
            target = source
        return pltpu.make_async_remote_copy(
            src_ref=source,
            dst_ref=target,
            send_sem=self.send.at[2 * way + sub, step],
            recv_sem=self.recv.at[2 * way + sub, step],
            device_id=(peer, self.t),
            device_id_type=MESH,
        )

    def finish(self, way, sub, phase, index, step):
        self.copy(way, sub, phase, index, step).wait()
        if phase == 2:
            return
        units = self.units(way, sub)
        if phase == 0:
            slot = pl.ds(pl.multiple_of(index * self.rows, 16), self.rows)
            rows, arrived = self.chunk(way, -1 - index), self.landed[units, slot]
        else:
            rows, arrived = self.chunk(way, 1), self.swapped[units, index]
        summed = (self.part[units, rows].astype(F32) + arrived.astype(F32)).astype(BF)
        self.part[units, rows] = summed
        if phase == 1:
            if index == len(self.plan.extra) - 1:
                self.total[units, rows] = summed
        elif not self.plan.extra:

            @pl.when(index == RING - 2)
            def _():
                self.total[units, rows] = summed

    def slot(self, number):
        sub = number % 2
        extra = len(self.plan.extra)
        middle = RING - 1 + extra

        def act(step, method):
            @pl.when((step >= 0) & (step < RING - 1))
            def _():
                method(way, sub, 0, step, step)

            for index in range(extra):

                @pl.when(step == RING - 1 + index)
                def _():
                    method(way, sub, 1, index, step)

            @pl.when((step >= middle) & (step < self.plan.steps))
            def _():
                method(way, sub, 2, step - middle, step)

        for way in range(2):
            act(number // 2 - 1, self.finish)
            act(number // 2, lambda *where: self.copy(*where).start())


def block_kernel(
    plan,
    tags_ref,
    tag_weight_ref,
    tok_ref,
    cot_ref,
    query_t_ref,
    keyval_ref,
    output_ref,
    up_ref,
    down_ref,
    gain_one_ref,
    bias_one_ref,
    gain_two_ref,
    bias_two_ref,
    table_ref,
    block_out_ref,
    grad_tokens_ref,
    total_ref,
    total_small_ref,
    x_all,
    gr_all,
    n1_all,
    br_all,
    g_all,
    up_t,
    down_t,
    qkv_t,
    qkv_w,
    out_t,
    q_t,
    k_t,
    k_r,
    v_t,
    v_r,
    do_t,
    gkv_all,
    kv_land,
    norms_c,
    norms_r,
    bias_acc,
    sum_out,
    sum_qkv,
    score,
    prob,
    acc,
    d_key,
    d_value,
    part,
    landed,
    swapped,
    part_small,
    landed_small,
    swapped_small,
    tp_land,
    tp_land_small,
    pre,
    from_sib,
    from_x,
    ag_send,
    ag_recv,
    rs_send,
    rs_recv,
    rs_send_x,
    rs_recv_x,
    ring_send,
    ring_recv,
    dp_send,
    dp_recv,
    dp_send_small,
    dp_recv_small,
    tp_send,
    tp_recv,
    kv_send,
    kv_recv,
):
    d, t = lax.axis_index("dp"), lax.axis_index("tp")
    chip, core = t // 2, t % 2
    sib = t + 1 - 2 * core
    across = (t + 2) % 4
    diag = (sib + 2) % 4
    width = tok_ref.shape[1]
    hidden = up_ref.shape[1]
    q_cols = query_t_ref.shape[0]
    heads = q_cols // HD
    own_blocks = tok_ref.shape[0] // TILE
    blocks = 4 * own_blocks
    half_width = width // 2
    tall = width // TILE

    slices = width // LANES
    base = 2 * slices
    big = Bundle(plan, d, t, part, landed, swapped, total_ref, dp_send, dp_recv)
    ring = Ring(
        plan, d, t, part, landed, swapped, total_ref, ring_send, ring_recv, slices // 2
    )
    small = Bundle(
        plan, d, t, part_small, landed_small, swapped_small, total_small_ref, dp_send_small, dp_recv_small
    )

    barrier = pltpu.get_barrier_semaphore()
    peers = [(d, sib), (d, across), (d, diag)] + [(big.partner(2**b), t) for b in range(plan.bits)]
    peers += [(ring.neighbour(way), t) for way in range(2)]
    for peer in peers:
        pl.semaphore_signal(barrier, inc=1, device_id=peer, device_id_type=MESH)
    pl.semaphore_wait(barrier, len(peers))

    row_weight = tag_weight_ref[tags_ref[0]]

    sets = (x_all, gr_all)

    def pair(ref, block):
        return jnp.concatenate([ref[2 * block], ref[2 * block + 1]], axis=1)

    def put_pair(ref, block, value):
        ref[2 * block] = value[:, :LANES]
        ref[2 * block + 1] = value[:, LANES:]

    def half_lanes(start, half):
        return pl.ds(pl.multiple_of(start + half * LANES, LANES), LANES)

    def gather_copy(kind, piece, half, owner, route):
        place = owner * own_blocks + piece
        target = {0: sib, 1: across, 2: sib}[route]
        view = sets[kind].at[2 * place + half]
        return pltpu.make_async_remote_copy(
            src_ref=view,
            dst_ref=view,
            send_sem=ag_send.at[kind, piece, half, route],
            recv_sem=ag_recv.at[kind, piece, half, route],
            device_id=(d, target),
            device_id_type=MESH,
        )

    for piece in range(own_blocks):
        rows = slice(piece * TILE, (piece + 1) * TILE)
        put_pair(x_all, t * own_blocks + piece, tok_ref[rows, :].T)
        for half in range(2):
            gather_copy(0, piece, half, t, 0).start()
        gather_copy(0, piece, 0, t, 1).start()
        weighted = (cot_ref[rows, :].astype(F32) * row_weight).astype(BF).T
        put_pair(gr_all, t * own_blocks + piece, weighted)
        for half in range(2):
            gather_copy(1, piece, half, t, 0).start()
        gather_copy(1, piece, 0, t, 1).start()
        gather_copy(0, piece, 1, t, 1).start()
        gather_copy(1, piece, 1, t, 1).start()

    up_t[...] = up_ref[...].T
    down_t[...] = down_ref[...].T
    qkv_t[:q_cols] = query_t_ref[...]
    qkv_t[q_cols:] = keyval_ref[...].T
    qkv_w[...] = qkv_t[...].T
    out_t[...] = output_ref[...].T
    for index, norm in enumerate((gain_one_ref, bias_one_ref, gain_two_ref, bias_two_ref)):
        norms_r[index : index + 1] = norm[...].reshape(1, width)
    norms_c[...] = norms_r[...].T
    score[...] = jnp.zeros_like(score)
    bias_acc[...] = jnp.zeros_like(bias_acc)
    sum_out[...] = jnp.zeros_like(sum_out)
    sum_qkv[...] = jnp.zeros_like(sum_qkv)
    d_key[...] = jnp.zeros_like(d_key)
    d_value[...] = jnp.zeros_like(d_value)

    def standardize(x):
        mean = jnp.sum(x, axis=0, keepdims=True) * (1.0 / width)
        centred = x - mean
        variance = jnp.sum(centred * centred, axis=0, keepdims=True) * (1.0 / width)
        inverse = lax.rsqrt(variance + 1e-05)
        return centred * inverse, inverse

    def feed_forward(step, carry):
        late, piece, half = step // 4, (step % 4) // 2, step % 2
        owners = (
            (1 - late) * t + late * across,
            (1 - late) * sib + late * diag,
        )
        places = [owner * own_blocks + piece for owner in owners]
        sides = [slice(0, LANES), slice(LANES, TILE)]

        @pl.when(late == 0)
        def _():
            for kind in range(2):
                gather_copy(kind, piece, half, sib, 0).wait_recv()

        @pl.when(late == 1)
        def _():
            for kind in range(2):
                gather_copy(kind, piece, half, across, 1).wait_recv()
                gather_copy(kind, piece, half, across, 2).start()
            for kind in range(2):
                gather_copy(kind, piece, half, diag, 2).wait_recv()

        def load(ref):
            return jnp.concatenate([ref[2 * place + half] for place in places], axis=1)

        def store(ref, value):
            for place, side in zip(places, sides):
                ref[2 * place + half] = value[:, side]

        normal, _ = standardize(load(x_all).astype(F32))
        n1 = (normal * norms_c[:, 0:1] + norms_c[:, 1:2]).astype(BF)
        n2 = (normal * norms_c[:, 2:3] + norms_c[:, 3:4]).astype(BF)
        store(n1_all, n1)
        gr = load(gr_all)
        qkv = mm(qkv_t[...], n1)
        lanes = [half_lanes(place * TILE, half) for place in places]
        cosine = jnp.concatenate([table_ref[:HALF, at] for at in lanes], axis=1)
        sine = jnp.concatenate([table_ref[HALF:, at] for at in lanes], axis=1)
        grad_context = mm(output_ref[...], gr)
        for head in range(heads):
            rows = slice(head * HD, (head + 1) * HD)
            turned = (turn(qkv[rows], cosine, sine) * (HD**-0.5)).astype(BF)
            grads = grad_context[rows].astype(BF)
            for place, side in zip(places, sides):
                at = slice(head * LANES, (head + 1) * LANES)
                q_t[2 * place + half, :, at] = turned[:, side]
                do_t[2 * place + half, :, at] = grads[:, side]
        key = turn(qkv[q_cols : q_cols + HD], cosine, sine)
        value = qkv[q_cols + HD :]
        for place, side, at in zip(places, sides, lanes):
            k_t[:, at] = key[:, side].astype(BF)
            v_t[:HD, at] = value[:, side].astype(BF)
            v_t[HD:, at] = jnp.ones((v_t.shape[0] - HD, LANES), BF)
            k_r[place, half_lanes(0, half), :] = key[:, side].T.astype(BF)
            v_r[place, half_lanes(0, half), :] = value[:, side].T.astype(BF)

        chunks = [slice(c * TILE, (c + 1) * TILE) for c in range(tall)]

        def activate(pre_act):
            cdf = 0.5 + 0.5 * lax.erf(pre_act * 0.7071067811865476)
            density = jnp.exp(-0.5 * pre_act * pre_act) * 0.3989422804014327
            return (pre_act * cdf).astype(BF), cdf + pre_act * density

        pre_acts = [mm(up_t[chunks[0], :], n2)]
        grad_mids, middles, grads = [], [], []
        for c in range(tall):
            grad_mids.append(mm(down_ref[chunks[c], :], gr))
            if c + 1 < tall:
                pre_acts.append(mm(up_t[chunks[c + 1], :], n2))
            middle, slope = activate(pre_acts[c])
            middles.append(middle)
            grads.append((grad_mids[c] * slope).astype(BF))
            if c > 0:
                score[c - 1] += mm_t(middles[c - 1], gr)
        middle = jnp.concatenate(middles, axis=0)
        grad_hidden = jnp.concatenate(grads, axis=0)
        score[tall - 1] += mm_t(middles[-1], gr)
        store(br_all, mm(down_t[...], middle).astype(BF))
        up_two = mm(up_ref[...], grad_hidden)
        bias_acc[...] += up_two[:, :LANES] + up_two[:, LANES:]
        store(g_all, (up_two * norms_c[:, 2:3]).astype(BF))
        score[tall : 2 * tall] += mm_t(n2, grad_hidden).reshape(tall, TILE, hidden)
        return carry

    lax.fori_loop(0, blocks, feed_forward, 0)

    def gathered(index, carry):
        piece, half = index // 2, index % 2
        for kind in range(2):
            gather_copy(kind, piece, half, t, 0).wait_send()
            gather_copy(kind, piece, half, t, 1).wait_send()
            gather_copy(kind, piece, half, across, 2).wait_send()
        return carry

    lax.fori_loop(0, 2 * own_blocks, gathered, 0)

    for first in range(2):
        for index in range(first * slices // 2, (first + 1) * slices // 2):
            cols = slice(index * LANES, (index + 1) * LANES)
            part[index] = score[:tall, :, cols].reshape(hidden, LANES).astype(BF)
            part[slices + index] = score[tall : 2 * tall, :, cols].reshape(width, LANES).astype(BF)
        ring.slot(first)
    for index in range(tall):
        rows = slice(index * TILE, (index + 1) * TILE)
        product = jnp.sum(up_ref[rows, :].astype(F32) * score[tall + index], axis=1, keepdims=True)
        norms_c[rows, 4:5] = product
    norms_c[:, 5:6] = jnp.sum(bias_acc[...], axis=1, keepdims=True)
    bias_acc[...] = jnp.zeros_like(bias_acc)

    outs = (br_all, g_all)

    def block_of(step):
        return step // 2 + (blocks // 2) * (step % 2)

    def pre_copy(kind, step, block):
        rows = pl.ds(pl.multiple_of((1 - core) * half_width, 16), half_width)
        return pltpu.make_async_remote_copy(
            src_ref=outs[kind].at[pl.ds(2 * block, 2), rows],
            dst_ref=pre.at[kind, step // 2],
            send_sem=rs_send.at[kind, step],
            recv_sem=rs_recv.at[kind, step],
            device_id=(d, sib),
            device_id_type=MESH,
        )

    def sib_copy(kind, step, block):
        return pltpu.make_async_remote_copy(
            src_ref=outs[kind].at[pl.ds(2 * block, 2)],
            dst_ref=from_sib.at[kind, block % own_blocks],
            send_sem=rs_send.at[kind, step],
            recv_sem=rs_recv.at[kind, step],
            device_id=(d, sib),
            device_id_type=MESH,
        )

    def x_copy(kind, block, sender_core, owner):
        rows = pl.ds(pl.multiple_of(sender_core * half_width, 16), half_width)
        return pltpu.make_async_remote_copy(
            src_ref=outs[kind].at[pl.ds(2 * block, 2), rows],
            dst_ref=from_x.at[kind, block % own_blocks, :, rows],
            send_sem=rs_send_x.at[kind, block],
            recv_sem=rs_recv_x.at[kind, block % own_blocks, sender_core],
            device_id=(d, owner),
            device_id_type=MESH,
        )

    def scatter_first(kind, step):
        block = block_of(step)
        owner = block // own_blocks

        @pl.when(owner // 2 != chip)
        def _():
            pre_copy(kind, step, block).start()

        @pl.when((owner // 2 == chip) & (owner != t))
        def _():
            sib_copy(kind, step, block).start()

    def scatter_second(kind, step):
        block = block_of(step)
        owner = block // own_blocks

        @pl.when(owner // 2 != chip)
        def _():
            pre_copy(kind, step, block).wait()
            rows = pl.ds(pl.multiple_of(core * half_width, 16), half_width)
            mine = outs[kind][pl.ds(2 * block, 2), rows].astype(F32)
            outs[kind][pl.ds(2 * block, 2), rows] = (mine + pre[kind, step // 2].astype(F32)).astype(BF)
            x_copy(kind, block, core, owner).start()

        @pl.when((owner // 2 == chip) & (owner != t))
        def _():
            sib_copy(kind, step, block).wait_send()

    def scatter_sent(kind, step):
        block = block_of(step)
        owner = block // own_blocks

        @pl.when(owner // 2 != chip)
        def _():
            x_copy(kind, block, core, owner).wait_send()

    def scatter_arrived(kind, piece):
        block = t * own_blocks + piece
        step = 2 * (block % (blocks // 2)) + block // (blocks // 2)
        sib_copy(kind, step, block).wait_recv()
        for sender_core in range(2):
            x_copy(kind, block, sender_core, t).wait_recv()
        halves = [
            outs[kind][2 * block + half].astype(F32)
            + from_sib[kind, piece, half].astype(F32)
            + from_x[kind, piece, half].astype(F32)
            for half in range(2)
        ]
        return jnp.concatenate(halves, axis=1)

    def emit_block_out(piece):
        cols = slice(piece * TILE, (piece + 1) * TILE)
        x = pair(x_all, t * own_blocks + piece).astype(F32)
        block_out_ref[:, cols] = (x + scatter_arrived(0, piece)).astype(BF)

    def emit_grad_tokens(piece):
        place = t * own_blocks + piece
        if piece == 0:
            for hop in range(3):
                kv_copy(t, hop, (t + hop + 1) % 4).wait_recv()
        key_value_grad = gkv_all[place].astype(F32)
        for hop in range(3):
            key_value_grad = key_value_grad + kv_land[hop, piece].astype(F32)
        up_kv = mm(qkv_w[:, q_cols:], key_value_grad.astype(BF))
        scaled = scatter_arrived(1, piece) + up_kv * norms_c[:, 0:1]
        normal, inverse = standardize(pair(x_all, place).astype(F32))
        mean_one = jnp.sum(scaled, axis=0, keepdims=True) * (1.0 / width)
        mean_two = jnp.sum(scaled * normal, axis=0, keepdims=True) * (1.0 / width)
        grad_tokens_ref[:, piece * TILE : (piece + 1) * TILE] = (
            pair(gr_all, place).astype(F32) + inverse * (scaled - mean_one - normal * mean_two)
        ).astype(BF)

    def attend(step, carry):
        heavy = step % 2
        turn_slot = 6 * (step // 2) + 2

        def ring_point(light_slot, heavy_slot):
            if light_slot is None:

                @pl.when(heavy == 1)
                def _():
                    ring.slot(turn_slot + heavy_slot)
            else:
                ring.slot(turn_slot + light_slot + heavy * (heavy_slot - light_slot))

        ring_point(None, 2)
        block = block_of(step)
        queries = jnp.concatenate([q_t[2 * block], q_t[2 * block + 1]], axis=1)
        wide = heads * TILE

        def of_head(value, head):
            first = value[:, head * LANES : (head + 1) * LANES]
            second = value[:, (heads + head) * LANES : (heads + head + 1) * LANES]
            return jnp.concatenate([first, second], axis=1)

        def in_pairs(count, body, start):
            carry = lax.fori_loop(0, count // 4, lambda i, c: body(4 * i, 4, c), start)
            carry = lax.fori_loop(count // 4 * 2, count // 2, lambda i, c: body(2 * i, 2, c), carry)
            return lax.fori_loop(count // 2 * 2, count, lambda i, c: body(i, 1, c), carry)

        def lanes_of(j, tiles):
            return pl.ds(pl.multiple_of(j * TILE, TILE), tiles * TILE)

        def scores(j, tiles, top):
            tile = mm(k_r[pl.ds(j, tiles)].reshape(tiles * TILE, HD), queries)
            score[pl.ds(j, tiles)] = tile.reshape(tiles, TILE, wide)
            return jnp.maximum(top, jnp.max(tile.reshape(tiles * TILE // 8, 8, wide), axis=0))

        top = in_pairs(block, scores, jnp.full((8, wide), -1e30, F32))
        tile = mm(k_r[block], queries)
        past = lax.broadcasted_iota(jnp.int32, (TILE, wide), 0)
        now = lax.broadcasted_iota(jnp.int32, (TILE, wide), 1)
        now = now // (wide // 2) * LANES + now % LANES
        tile = jnp.where(past <= now, tile, -1e30)
        score[block] = tile
        top = jnp.maximum(top, jnp.max(tile.reshape(TILE // 8, 8, wide), axis=0))
        top = jnp.max(top, axis=0, keepdims=True)

        acc[...] = jnp.zeros_like(acc)
        ring_point(0, 3)

        def weigh(j, tiles, carry):
            weights = jnp.exp(score[pl.ds(j, tiles)] - top).astype(BF)
            prob[pl.ds(j, tiles)] = weights
            acc[...] += mm(v_t[:, lanes_of(j, tiles)], weights.reshape(tiles * TILE, wide))
            return carry

        in_pairs(block + 1, weigh, 0)
        inverse = 1.0 / acc[HD : HD + 1]
        context = acc[:HD] * inverse
        grad = (pair(do_t, block).astype(F32) * inverse).astype(BF)
        delta = jnp.sum(grad.astype(F32) * context, axis=0, keepdims=True)
        acc[:HD] = jnp.zeros((HD, wide), F32)

        context_rows = jnp.concatenate([of_head(context, h) for h in range(heads)], axis=0).astype(BF)
        branch = mm(out_t[...], context_rows) + pair(br_all, block).astype(F32)
        put_pair(br_all, block, branch.astype(BF))
        scatter_first(0, step)

        @pl.when(step > 0)
        def _():
            scatter_second(1, step - 1)

        ring_point(None, 4)

        def back(j, tiles, carry):
            weights = prob[pl.ds(j, tiles)].reshape(tiles * TILE, wide)
            grad_probs = mm(v_r[pl.ds(j, tiles)].reshape(tiles * TILE, HD), grad)
            grad_scores = (weights.astype(F32) * (grad_probs - delta)).astype(BF)
            acc[:HD] += mm(k_t[:, lanes_of(j, tiles)], grad_scores)
            d_key[:, lanes_of(j, tiles)] += mm_t(queries, grad_scores)
            d_value[:, lanes_of(j, tiles)] += mm_t(grad, weights)
            return carry

        in_pairs(block + 1, back, 0)
        lanes = pl.ds(pl.multiple_of(block * TILE, TILE), TILE)
        cosine, sine = table_ref[:HALF, lanes], table_ref[HALF:, lanes]
        grad_queries = acc[:HD]
        turned = [
            turn(of_head(grad_queries, head), cosine, -sine) * (HD**-0.5) for head in range(heads)
        ]
        turned = jnp.concatenate(turned, axis=0).astype(BF)
        scatter_second(0, step)
        ring_point(1, 5)
        scaled = mm(qkv_w[:, :q_cols], turned) * norms_c[:, 0:1] + pair(g_all, block).astype(F32)
        put_pair(g_all, block, scaled.astype(BF))
        scatter_first(1, step)
        sum_out[...] += mm_t(context_rows, pair(gr_all, block))
        sum_qkv[:q_cols] += mm_t(turned, pair(n1_all, block))
        bias_acc[:q_cols] += turned[:, :LANES].astype(F32) + turned[:, LANES:].astype(F32)
        return carry

    lax.fori_loop(0, blocks, attend, 0)
    scatter_second(1, blocks - 1)

    def key_value(block, carry):
        lanes = pl.ds(pl.multiple_of(block * TILE, TILE), TILE)
        cosine, sine = table_ref[:HALF, lanes], table_ref[HALF:, lanes]
        gkv_all[block, :HD] = turn(d_key[:, lanes], cosine, -sine).astype(BF)
        gkv_all[block, HD:] = d_value[:, lanes].astype(BF)
        grads = gkv_all[block]
        bias_acc[q_cols : q_cols + 2 * HD] += grads[:, :LANES].astype(F32) + grads[:, LANES:].astype(F32)
        sum_qkv[q_cols:] += mm_t(grads, pair(n1_all, block))
        return carry

    lax.fori_loop(0, blocks, key_value, 0)

    def kv_copy(owner, hop, target):
        return pltpu.make_async_remote_copy(
            src_ref=gkv_all.at[pl.ds(owner * own_blocks, own_blocks)],
            dst_ref=kv_land.at[hop],
            send_sem=kv_send.at[hop],
            recv_sem=kv_recv.at[hop],
            device_id=(d, target),
            device_id_type=MESH,
        )

    for hop in range(3):
        owner = (t + hop + 1) % 4
        kv_copy(owner, hop, owner).start()

    for index in range(slices):
        cols = slice(index * LANES, (index + 1) * LANES)
        for which, source in ((0, sum_out[:, cols]), (1, sum_qkv[:q_cols, cols])):
            row = (2 * index + which) * q_cols
            part[base + row // width, row % width : row % width + q_cols] = source.astype(BF)
    part[base + 3] = sum_qkv[q_cols:].T.astype(BF)
    ends = [(big, base + unit, unit % 2) for unit in range(4)] + [(small, 0, 0)]
    for bundle, unit, kind in ends[:4]:
        bundle.start(unit, kind, 0)
    row_sums = jnp.sum(bias_acc[: q_cols + 2 * HD], axis=1, keepdims=True)
    shift_one = jnp.sum(qkv_t[...].astype(F32) * row_sums, axis=0, keepdims=True)
    shift_two = norms_c[:, 5:6]
    product_one = jnp.sum(qkv_t[...].astype(F32) * sum_qkv[...], axis=0, keepdims=True)
    gain_one = (product_one - norms_r[1:2] * shift_one) / norms_r[0:1]
    gain_two = (norms_c[:, 4:5] - norms_c[:, 3:4] * shift_two) / norms_c[:, 2:3]
    lane = lax.broadcasted_iota(jnp.int32, (width, 8), 1)
    columns = jnp.where(lane == 0, gain_two, shift_two).T
    rows = jnp.concatenate([gain_one, shift_one, columns[:6]], axis=0)
    part_small[0] = jnp.zeros(part_small.shape[1:], BF)
    for index in range(slices):
        part_small[0, 16 * index : 16 * index + 8] = rows[
            :, index * LANES : (index + 1) * LANES
        ].astype(BF)

    small.start(0, 0, 0)
    lands = (tp_land, tp_land_small)

    def tp_copy(index, sender, hop):
        return pltpu.make_async_remote_copy(
            src_ref=lands[index].at[sender],
            dst_ref=lands[index].at[sender],
            send_sem=tp_send.at[index, hop],
            recv_sem=tp_recv.at[index, hop],
            device_id=(d, (t + hop + 1) % 4),
            device_id_type=MESH,
        )

    middle_stage = 2 + len(plan.extra)
    ring_slots = list(range(3 * blocks + 2, plan.slots))
    for beat in range(plan.stages + 1):
        for index in ring_slots[2 * beat : 2 * beat + 2]:
            ring.slot(index)
        for index, (bundle, unit, kind) in enumerate(ends):
            rows = pl.ds(*bundle.span(kind, 3))
            shared = index - 3
            if shared < 0 or beat < middle_stage:
                if beat < plan.stages:
                    bundle.finish(unit, kind, beat)
                if beat + 1 < plan.stages:
                    bundle.start(unit, kind, beat + 1)
            elif beat == middle_stage:
                bundle.finish(unit, kind, beat, publish=False)
                lands[shared][t] = bundle.part[unit, rows]
                for hop in range(3):
                    tp_copy(shared, t, hop).start()
            elif beat == middle_stage + 1:
                for hop in range(3):
                    tp_copy(shared, (t + 3 - hop) % 4, hop).wait_recv()
                land = [lands[shared][sender].astype(F32) for sender in range(4)]
                bundle.total[unit, rows] = (land[0] + land[1] + land[2] + land[3]).astype(BF)
                bundle.start(unit, kind, beat)
            else:
                bundle.finish(unit, kind, beat - 1)
                if beat < plan.stages:
                    bundle.start(unit, kind, beat)
        if 0 < beat <= own_blocks:
            emit_block_out(beat - 1)
        elif 4 <= beat < 4 + own_blocks:
            emit_grad_tokens(beat - 4)
    for index in range(2):
        for hop in range(3):
            tp_copy(index, t, hop).wait_send()
    for hop in range(3):
        kv_copy((t + hop + 1) % 4, hop, (t + hop + 1) % 4).wait_send()

    def drain(step, carry):
        for kind in range(2):
            scatter_sent(kind, step)
        return carry

    lax.fori_loop(0, blocks, drain, 0)


def finish_kernel(
    block_out_t,
    grad_tokens_t,
    down,
    up,
    ends,
    keyval,
    small,
    block_out_ref,
    grad_tokens_ref,
    grad_query_ref,
    grad_keyval_ref,
    grad_output_ref,
    grad_up_ref,
    grad_down_ref,
    *vector_refs,
):
    block_out_ref[...] = block_out_t[...].T
    grad_tokens_ref[...] = grad_tokens_t[...].T
    grad_output_ref[...] = ends[0].astype(F32)
    grad_query_ref[...] = ends[1].astype(F32)
    grad_keyval_ref[...] = keyval[0].astype(F32)
    grad_down_ref[...] = down[0].astype(F32)
    grad_up_ref[...] = up[0].astype(F32)
    for index, vector in enumerate(vector_refs):
        rows = [small[0, 16 * k + index : 16 * k + index + 1] for k in range(pl.num_programs(0))]
        vector[...] = jnp.concatenate(rows, axis=1).astype(F32).reshape(vector.shape)


def shards(
    dp,
    tokens,
    cotangent,
    tags,
    tag_weight,
    query_weight,
    key_value_weight,
    output_weight,
    up_weight,
    down_weight,
    norm_gain_one,
    norm_bias_one,
    norm_gain_two,
    norm_bias_two,
):
    plan = Plan(dp)
    _, own_len, width = tokens.shape
    full_len = 4 * own_len
    q_cols, kv_cols, hidden = query_weight.shape[1], key_value_weight.shape[1], up_weight.shape[1]
    heads = q_cols // HD
    wide = heads * TILE
    blocks, own_blocks = full_len // TILE, own_len // TILE
    frequencies = (10000.0 ** (-np.arange(0, ROT, 2, dtype=np.float32) / ROT)).astype(np.float32)
    angles = frequencies[:, None] * np.arange(full_len, dtype=np.float32)[None, :]
    table = np.concatenate([np.cos(angles), np.sin(angles)], axis=0).astype(np.float32)

    slices = width // LANES
    units = 2 * slices + 4
    small_rows = LANES
    extra = max(1, len(plan.extra))
    vmem = lambda *shape, kind=BF: pltpu.VMEM(shape, kind)
    dma = lambda *shape: pltpu.SemaphoreType.DMA(shape)
    scratch = [
        vmem(2 * blocks, width, LANES),
        vmem(2 * blocks, width, LANES),
        vmem(2 * blocks, width, LANES),
        vmem(2 * blocks, width, LANES),
        vmem(2 * blocks, width, LANES),
        vmem(hidden, width),
        vmem(width, hidden),
        vmem(q_cols + kv_cols, width),
        vmem(width, q_cols + kv_cols),
        vmem(width, q_cols),
        vmem(2 * blocks, HD, wide // 2),
        vmem(HD, full_len),
        vmem(blocks, TILE, HD),
        vmem(HD + 16, full_len),
        vmem(blocks, TILE, HD),
        vmem(2 * blocks, HD, wide // 2),
        vmem(blocks, kv_cols, TILE),
        vmem(4, own_blocks, kv_cols, TILE),
        vmem(width, 8, kind=F32),
        vmem(8, width, kind=F32),
        vmem(width, LANES, kind=F32),
        vmem(q_cols, width, kind=F32),
        vmem(q_cols + kv_cols, width, kind=F32),
        vmem(blocks, TILE, wide, kind=F32),
        vmem(blocks, TILE, wide),
        vmem(HD + 16, wide, kind=F32),
        vmem(HD, full_len, kind=F32),
        vmem(HD, full_len, kind=F32),
        vmem(units, width, LANES),
        vmem(units, width - width // 8, LANES),
        vmem(units, extra, width // 8, LANES),
        vmem(1, small_rows, LANES),
        vmem(1, small_rows - small_rows // 8, LANES),
        vmem(1, extra, small_rows // 8, LANES),
        vmem(4, width // 8, LANES),
        vmem(4, small_rows // 8, LANES),
        vmem(2, blocks // 2, 2, width // 2, LANES),
        vmem(2, own_blocks, 2, width, LANES),
        vmem(2, own_blocks, 2, width, LANES),
        dma(2, own_blocks, 2, 3),
        dma(2, own_blocks, 2, 3),
        dma(2, blocks),
        dma(2, blocks),
        dma(2, blocks),
        dma(2, own_blocks, 2),
        dma(4, plan.steps),
        dma(4, plan.steps),
        dma(units, plan.stages),
        dma(units, plan.stages),
        dma(1, plan.stages),
        dma(1, plan.stages),
        dma(2, 3),
        dma(2, 3),
        dma(3),
        dma(3),
    ]
    in_vmem = pl.BlockSpec(memory_space=pltpu.VMEM)
    in_smem = pl.BlockSpec(memory_space=pltpu.SMEM)
    block_out, grad_tokens, total, total_small = pl.pallas_call(
        functools.partial(block_kernel, plan),
        out_shape=(
            jax.ShapeDtypeStruct((width, own_len), BF),
            jax.ShapeDtypeStruct((width, own_len), BF),
            jax.ShapeDtypeStruct((units, width, LANES), BF),
            jax.ShapeDtypeStruct((1, small_rows, LANES), BF),
        ),
        in_specs=[in_smem] * 2 + [in_vmem] * 12,
        out_specs=(in_vmem,) * 4,
        scratch_shapes=scratch,
        compiler_params=pltpu.CompilerParams(
            collective_id=0, has_side_effects=True, vmem_limit_bytes=63 << 20
        ),
    )(
        tags,
        tag_weight,
        tokens[0],
        cotangent[0],
        query_weight.T,
        key_value_weight,
        output_weight,
        up_weight,
        down_weight,
        norm_gain_one,
        norm_bias_one,
        norm_gain_two,
        norm_bias_two,
        jnp.asarray(table),
    )
    first_end = slices * width // q_cols
    finish_shapes = (
        ((own_len, width), BF),
        ((own_len, width), BF),
        ((q_cols, width), F32),
        ((width, kv_cols), F32),
        ((q_cols, width), F32),
        ((width, hidden), F32),
        ((hidden, width), F32),
        ((width,), F32),
        ((width,), F32),
        ((width,), F32),
        ((width,), F32),
    )
    by_columns = lambda rows: pl.BlockSpec((rows, LANES), lambda i: (0, i))
    by_rows = pl.BlockSpec((LANES, own_len), lambda i: (i, 0))
    block_out, grad_tokens, grad_query, grad_keyval, grad_output, grad_up, grad_down, *vectors = (
        pl.pallas_call(
            finish_kernel,
            grid=(slices,),
            out_shape=tuple(jax.ShapeDtypeStruct(*shape) for shape in finish_shapes),
            in_specs=[
                by_rows,
                by_rows,
                pl.BlockSpec((1, width, LANES), lambda i: (i, 0, 0)),
                pl.BlockSpec((1, width, LANES), lambda i: (slices + i, 0, 0)),
                pl.BlockSpec((2, q_cols, LANES), lambda i: (first_end + i, 0, 0)),
                pl.BlockSpec((1, width, LANES), lambda i: (2 * slices + 3, 0, 0)),
                pl.BlockSpec((1, small_rows, LANES), lambda i: (0, 0, 0)),
            ],
            out_specs=(
                by_columns(own_len),
                by_columns(own_len),
                by_columns(q_cols),
                pl.BlockSpec((width, kv_cols), lambda i: (0, 0)),
                by_columns(q_cols),
                by_columns(width),
                by_columns(hidden),
                pl.BlockSpec((width,), lambda i: (0,)),
                pl.BlockSpec((width,), lambda i: (0,)),
                pl.BlockSpec((width,), lambda i: (0,)),
                pl.BlockSpec((width,), lambda i: (0,)),
            ),
            compiler_params=pltpu.CompilerParams(vmem_limit_bytes=60 << 20),
        )(
            block_out,
            grad_tokens,
            total,
            total,
            total.reshape(units * width // q_cols, q_cols, LANES),
            total,
            total_small,
        )
    )
    return (
        block_out[None],
        grad_tokens[None],
        grad_query.T,
        grad_keyval,
        grad_output,
        grad_up,
        grad_down,
        *vectors,
    )


def solution(mesh):
    rows = P("dp", "tp", None)
    columns, depth, whole = P(None, "tp"), P("tp", None), P()
    in_specs = (rows, rows, P("dp"), whole, columns, whole, depth, columns, depth) + (whole,) * 4
    out_specs = (rows, rows, columns, whole, depth, columns, depth) + (whole,) * 4
    return jax.shard_map(
        functools.partial(shards, mesh.shape["dp"]),
        mesh=mesh,
        in_specs=in_specs,
        out_specs=out_specs,
        check_vma=False,
    )
```

```python
import functools

import jax
import jax.numpy as jnp
import numpy as np
from jax import lax
from jax.experimental import pallas as pl
from jax.experimental.pallas import tpu as pltpu
from jax.sharding import PartitionSpec as P

HD = 64
ROT = 16
HALF = ROT // 2
TILE = 256
LANES = 128
RING = 8
SUBS = 3
MESH = pl.DeviceIdType.MESH
BF = jnp.bfloat16
F32 = jnp.float32


def mm(left, right):
    return jnp.dot(left, right, preferred_element_type=F32)


def mm_t(left, right):
    return lax.dot_general(left, right, (((1,), (1,)), ((), ())), preferred_element_type=F32)


def turn(values, cosine, sine):
    front, back = values[:HALF], values[HALF:ROT]
    return jnp.concatenate(
        [front * cosine - back * sine, back * cosine + front * sine, values[ROT:]], axis=0
    )


class Plan:
    def __init__(self, dp):
        self.bits = dp.bit_length() - 1
        self.extra = [2**position for position in range(3, self.bits)]
        self.stages = 6 + len(self.extra)
        self.steps = 2 * (RING - 1) + len(self.extra)
        self.slots = SUBS * (self.steps + 1)

    def strides(self, kind):
        return (1 + kind, 2 - kind, 4)


class Bundle:
    def __init__(self, plan, d, t, part, landed, swapped, total, send, recv):
        self.plan, self.d, self.t = plan, d, t
        self.part, self.landed, self.swapped, self.total = part, landed, swapped, total
        self.send, self.recv = send, recv
        self.rows = part.shape[1]

    def bit(self, stride):
        return (self.d // stride) % 2

    def partner(self, stride):
        return self.d + (1 - 2 * self.bit(stride)) * stride

    def span(self, kind, depth):
        start = 0
        for level in range(depth):
            start = start + self.bit(self.plan.strides(kind)[level]) * (self.rows >> (level + 1))
        return pl.multiple_of(start, 16), self.rows >> depth

    def copy(self, unit, kind, stage):
        order, extra = self.plan.strides(kind), self.plan.extra
        if stage < 3:
            start, size = self.span(kind, stage)
            position = order[stage]
            half = size // 2
            other = pl.multiple_of(start + (1 - self.bit(position)) * half, 16)
            source = self.part.at[unit, pl.ds(other, half)]
            target = self.landed.at[unit, pl.ds(self.rows - size, half)]
        elif stage < 3 + len(extra):
            start, size = self.span(kind, 3)
            position = extra[stage - 3]
            source = self.part.at[unit, pl.ds(start, size)]
            target = self.swapped.at[unit, stage - 3]
        else:
            depth = self.plan.stages - stage
            start, size = self.span(kind, depth)
            position = order[depth - 1]
            source = self.total.at[unit, pl.ds(start, size)]
            target = source
        return pltpu.make_async_remote_copy(
            src_ref=source,
            dst_ref=target,
            send_sem=self.send.at[unit, stage],
            recv_sem=self.recv.at[unit, stage],
            device_id=(self.partner(position), self.t),
            device_id_type=MESH,
        )

    def start(self, unit, kind, stage):
        self.copy(unit, kind, stage).start()

    def finish(self, unit, kind, stage, publish=True):
        self.copy(unit, kind, stage).wait()
        last = 2 + len(self.plan.extra)
        if stage <= last:
            if stage < 3:
                start, size = self.span(kind, stage + 1)
                arrived = self.landed[unit, pl.ds(self.rows - 2 * size, size)]
            else:
                start, size = self.span(kind, 3)
                arrived = self.swapped[unit, stage - 3]
            mine = self.part[unit, pl.ds(start, size)]
            summed = (mine.astype(F32) + arrived.astype(F32)).astype(BF)
            if stage == last and publish:
                self.total[unit, pl.ds(start, size)] = summed
            else:
                self.part[unit, pl.ds(start, size)] = summed


class Ring:
    def __init__(self, plan, d, t, part, landed, swapped, total, send, recv, height):
        self.plan, self.d, self.t = plan, d, t
        self.part, self.landed, self.swapped, self.total = part, landed, swapped, total
        self.send, self.recv = send, recv
        self.height = height
        self.rows = part.shape[1] // RING
        self.first = d - d % RING
        line, side = (d % RING) // 2, d % 2
        self.place = line + side * (RING - 1 - 2 * line)
        self.neighbours = [
            self.device(lax.rem(self.place + ahead, jnp.int32(RING))) for ahead in (1, RING - 1)
        ]

    def device(self, place):
        far = place // (RING // 2)
        return self.first + (1 - far) * 2 * place + far * (2 * RING - 1 - 2 * place)

    def units(self, way, sub):
        return pl.ds((SUBS * way + sub) * self.height, self.height)

    def chunk(self, way, ahead):
        index = lax.rem(self.place + RING + (1, -1)[way] * ahead, jnp.int32(RING))
        return pl.ds(pl.multiple_of(index * self.rows, 16), self.rows)

    def copy(self, way, sub, phase, index, step):
        units = self.units(way, sub)
        peer = self.neighbours[way]
        if phase == 0:
            source = self.part.at[units, self.chunk(way, -index)]
            slot = pl.ds(pl.multiple_of(index * self.rows, 16), self.rows)
            target = self.landed.at[units, slot]
        elif phase == 1:
            stride = self.plan.extra[index]
            peer = self.d + (1 - 2 * ((self.d // stride) % 2)) * stride
            source = self.part.at[units, self.chunk(way, 1)]
            target = self.swapped.at[units, index]
        else:
            source = self.total.at[units, self.chunk(way, 1 - index)]
            target = source
        return pltpu.make_async_remote_copy(
            src_ref=source,
            dst_ref=target,
            send_sem=self.send.at[SUBS * way + sub, step],
            recv_sem=self.recv.at[SUBS * way + sub, step],
            device_id=(peer, self.t),
            device_id_type=MESH,
        )

    def finish(self, way, sub, phase, index, step, last):
        if phase == 2:
            return
        units = self.units(way, sub)
        if phase == 0:
            slot = pl.ds(pl.multiple_of(index * self.rows, 16), self.rows)
            rows, arrived = self.chunk(way, -1 - index), self.landed[units, slot]
        else:
            rows, arrived = self.chunk(way, 1), self.swapped[units, index]
        summed = (self.part[units, rows].astype(F32) + arrived.astype(F32)).astype(BF)
        (self.total if last else self.part)[units, rows] = summed

    def slot(self, number):
        number = jnp.int32(number)
        step = lax.div(number, jnp.int32(SUBS))
        sub = number - step * SUBS
        extra = len(self.plan.extra)
        turns = RING - 1
        middle = turns + extra

        def when(condition, ended, begun, last=False):
            @pl.when(condition)
            def _():
                if ended is not None:
                    for way in range(2):
                        self.copy(way, sub, *ended, step - 1).wait()
                        self.finish(way, sub, *ended, step - 1, last)
                        if begun is not None:
                            self.copy(way, sub, *begun, step).start()
                else:
                    for way in range(2):
                        self.copy(way, sub, *begun, step).start()

        when(step == 0, None, (0, 0))
        when((step > 0) & (step < turns), (0, step - 1), (0, step))
        for index in range(extra + 1):
            ended = (0, turns - 1) if index == 0 else (1, index - 1)
            begun = (2, 0) if index == extra else (1, index)
            when(step == turns + index, ended, begun, last=index == extra)
        when((step > middle) & (step < self.plan.steps), (2, step - 1 - middle), (2, step - middle))
        when(step == self.plan.steps, (2, turns - 1), None)


def block_kernel(
    plan,
    tags_ref,
    tag_weight_ref,
    tok_hbm,
    cot_hbm,
    query_t_hbm,
    keyval_hbm,
    output_hbm,
    up_hbm,
    down_hbm,
    gain_one_ref,
    bias_one_ref,
    gain_two_ref,
    bias_two_ref,
    table_hbm,
    block_out_hbm,
    grad_tokens_hbm,
    total_hbm,
    end_total_hbm,
    tok_ref,
    cot_ref,
    query_t_ref,
    keyval_ref,
    output_ref,
    up_ref,
    down_ref,
    table_ref,
    block_out_ref,
    grad_tokens_ref,
    total_ref,
    end_total_ref,
    load_sem,
    store_sem,
    x_all,
    gr_all,
    n1_all,
    br_all,
    g_all,
    up_t,
    down_t,
    qkv_t,
    qkv_w,
    out_t,
    q_t,
    k_t,
    k_r,
    v_t,
    v_r,
    do_t,
    gkv_all,
    kv_land,
    norms_c,
    norms_r,
    bias_acc,
    sum_out,
    sum_qkv,
    score,
    prob,
    acc,
    d_key,
    d_value,
    part,
    landed,
    swapped,
    end_part,
    end_land,
    end_swap,
    tp_land,
    pre,
    from_sib,
    from_x,
    ag_send,
    ag_recv,
    rs_send,
    rs_recv,
    rs_send_x,
    rs_recv_x,
    ring_send,
    ring_recv,
    dp_send,
    dp_recv,
    end_send,
    end_recv,
    tp_send,
    tp_recv,
    kv_send,
    kv_recv,
):
    d, t = lax.axis_index("dp"), lax.axis_index("tp")
    chip, core = t // 2, t % 2
    sib = t + 1 - 2 * core
    across = (t + 2) % 4
    diag = (sib + 2) % 4
    width = tok_ref.shape[1]
    hidden = up_ref.shape[1]
    q_cols = query_t_ref.shape[0]
    heads = q_cols // HD
    own_blocks = tok_ref.shape[0] // TILE
    blocks = 4 * own_blocks
    half_width = width // 2
    tall = width // TILE

    slices = width // LANES
    base = 2 * slices
    big = Bundle(plan, d, t, part, landed, swapped, total_ref, dp_send, dp_recv)
    ring = Ring(
        plan, d, t, part, landed, swapped, total_ref, ring_send, ring_recv, slices // SUBS
    )

    loads = [
        pltpu.make_async_copy(source, target, load_sem.at[index])
        for index, (source, target) in enumerate(
            (
                (tok_hbm, tok_ref),
                (cot_hbm, cot_ref),
                (up_hbm, up_ref),
                (down_hbm, down_ref),
                (query_t_hbm, query_t_ref),
                (keyval_hbm, keyval_ref),
                (output_hbm, output_ref),
                (table_hbm, table_ref),
            )
        )
    ]
    for load in loads:
        load.start()

    barrier = pltpu.get_barrier_semaphore()
    first_of_ring, spot = d - d % RING, d % RING
    ring_peers = [first_of_ring + (spot + hop) % RING for hop in range(1, RING)]
    extra_peers = [d + (1 - 2 * ((d // stride) % 2)) * stride for stride in plan.extra]
    peers = [(d, sib), (d, across), (d, diag)] + [(peer, t) for peer in ring_peers + extra_peers]
    for peer in peers:
        pl.semaphore_signal(barrier, inc=1, device_id=peer, device_id_type=MESH)
    pl.semaphore_wait(barrier, len(peers))

    row_weight = tag_weight_ref[tags_ref[0]]

    sets = (x_all, gr_all)

    def pair(ref, block):
        return jnp.concatenate([ref[2 * block], ref[2 * block + 1]], axis=1)

    def put_pair(ref, block, value):
        ref[2 * block] = value[:, :LANES]
        ref[2 * block + 1] = value[:, LANES:]

    def half_lanes(start, half):
        return pl.ds(pl.multiple_of(start + half * LANES, LANES), LANES)

    def gather_copy(kind, piece, half, owner, route):
        place = owner * own_blocks + piece
        target = {0: sib, 1: across, 2: sib}[route]
        view = sets[kind].at[2 * place + half]
        return pltpu.make_async_remote_copy(
            src_ref=view,
            dst_ref=view,
            send_sem=ag_send.at[kind, piece, half, route],
            recv_sem=ag_recv.at[kind, piece, half, route],
            device_id=(d, target),
            device_id_type=MESH,
        )

    loads[0].wait()
    loads[1].wait()
    for piece in range(own_blocks):
        rows = slice(piece * TILE, (piece + 1) * TILE)
        put_pair(x_all, t * own_blocks + piece, tok_ref[rows, :].T)
        for half in range(2):
            gather_copy(0, piece, half, t, 0).start()
        gather_copy(0, piece, 0, t, 1).start()
        weighted = (cot_ref[rows, :].astype(F32) * row_weight).astype(BF).T
        put_pair(gr_all, t * own_blocks + piece, weighted)
        for half in range(2):
            gather_copy(1, piece, half, t, 0).start()
        gather_copy(1, piece, 0, t, 1).start()
        gather_copy(0, piece, 1, t, 1).start()
        gather_copy(1, piece, 1, t, 1).start()

    for load in loads[2:]:
        load.wait()
    up_t[...] = up_ref[...].T
    down_t[...] = down_ref[...].T
    qkv_t[:q_cols] = query_t_ref[...]
    qkv_t[q_cols:] = keyval_ref[...].T
    qkv_w[...] = qkv_t[...].T
    out_t[...] = output_ref[...].T
    for index, norm in enumerate((gain_one_ref, bias_one_ref, gain_two_ref, bias_two_ref)):
        norms_r[index : index + 1] = norm[...].reshape(1, width)
    norms_c[...] = norms_r[...].T
    score[...] = jnp.zeros_like(score)
    bias_acc[...] = jnp.zeros_like(bias_acc)
    sum_out[...] = jnp.zeros_like(sum_out)
    sum_qkv[...] = jnp.zeros_like(sum_qkv)
    d_key[...] = jnp.zeros_like(d_key)
    d_value[...] = jnp.zeros_like(d_value)

    def standardize(x):
        mean = jnp.sum(x, axis=0, keepdims=True) * (1.0 / width)
        centred = x - mean
        variance = jnp.sum(centred * centred, axis=0, keepdims=True) * (1.0 / width)
        inverse = lax.rsqrt(variance + 1e-05)
        return centred * inverse, inverse

    def feed_forward(step, carry):
        late, piece, half = step // 4, (step % 4) // 2, step % 2
        owners = (
            (1 - late) * t + late * across,
            (1 - late) * sib + late * diag,
        )
        places = [owner * own_blocks + piece for owner in owners]
        sides = [slice(0, LANES), slice(LANES, TILE)]

        @pl.when(late == 0)
        def _():
            for kind in range(2):
                gather_copy(kind, piece, half, sib, 0).wait_recv()

        @pl.when(late == 1)
        def _():
            for kind in range(2):
                gather_copy(kind, piece, half, across, 1).wait_recv()
                gather_copy(kind, piece, half, across, 2).start()
            for kind in range(2):
                gather_copy(kind, piece, half, diag, 2).wait_recv()

        def load(ref):
            return jnp.concatenate([ref[2 * place + half] for place in places], axis=1)

        def store(ref, value):
            for place, side in zip(places, sides):
                ref[2 * place + half] = value[:, side]

        normal, _ = standardize(load(x_all).astype(F32))
        n1 = (normal * norms_c[:, 0:1] + norms_c[:, 1:2]).astype(BF)
        n2 = (normal * norms_c[:, 2:3] + norms_c[:, 3:4]).astype(BF)
        store(n1_all, n1)
        gr = load(gr_all)
        qkv = mm(qkv_t[...], n1)
        lanes = [half_lanes(place * TILE, half) for place in places]
        cosine = jnp.concatenate([table_ref[:HALF, at] for at in lanes], axis=1)
        sine = jnp.concatenate([table_ref[HALF:, at] for at in lanes], axis=1)
        grad_context = mm(output_ref[...], gr)
        for head in range(heads):
            rows = slice(head * HD, (head + 1) * HD)
            turned = (turn(qkv[rows], cosine, sine) * (HD**-0.5)).astype(BF)
            grads = grad_context[rows].astype(BF)
            for place, side in zip(places, sides):
                at = slice(head * LANES, (head + 1) * LANES)
                q_t[2 * place + half, :, at] = turned[:, side]
                do_t[2 * place + half, :, at] = grads[:, side]
        key = turn(qkv[q_cols : q_cols + HD], cosine, sine)
        value = qkv[q_cols + HD :]
        for place, side, at in zip(places, sides, lanes):
            k_t[:, at] = key[:, side].astype(BF)
            v_t[:HD, at] = value[:, side].astype(BF)
            v_t[HD:, at] = jnp.ones((v_t.shape[0] - HD, LANES), BF)
            k_r[place, half_lanes(0, half), :] = key[:, side].T.astype(BF)
            v_r[place, half_lanes(0, half), :] = value[:, side].T.astype(BF)

        chunks = [slice(c * TILE, (c + 1) * TILE) for c in range(tall)]

        def activate(pre_act):
            cdf = 0.5 + 0.5 * lax.erf(pre_act * 0.7071067811865476)
            density = jnp.exp(-0.5 * pre_act * pre_act) * 0.3989422804014327
            return (pre_act * cdf).astype(BF), cdf + pre_act * density

        pre_acts = [mm(up_t[chunks[0], :], n2)]
        grad_mids, middles, grads = [], [], []
        for c in range(tall):
            grad_mids.append(mm(down_ref[chunks[c], :], gr))
            if c + 1 < tall:
                pre_acts.append(mm(up_t[chunks[c + 1], :], n2))
            middle, slope = activate(pre_acts[c])
            middles.append(middle)
            grads.append((grad_mids[c] * slope).astype(BF))
            if c > 0:
                score[c - 1] += mm_t(middles[c - 1], gr)
        middle = jnp.concatenate(middles, axis=0)
        grad_hidden = jnp.concatenate(grads, axis=0)
        score[tall - 1] += mm_t(middles[-1], gr)
        store(br_all, mm(down_t[...], middle).astype(BF))
        up_two = mm(up_ref[...], grad_hidden)
        bias_acc[...] += up_two[:, :LANES] + up_two[:, LANES:]
        store(g_all, (up_two * norms_c[:, 2:3]).astype(BF))
        score[tall : 2 * tall] += mm_t(n2, grad_hidden).reshape(tall, TILE, hidden)
        return carry

    lax.fori_loop(0, blocks, feed_forward, 0)

    def gathered(index, carry):
        piece, half = index // 2, index % 2
        for kind in range(2):
            gather_copy(kind, piece, half, t, 0).wait_send()
            gather_copy(kind, piece, half, t, 1).wait_send()
            gather_copy(kind, piece, half, across, 2).wait_send()
        return carry

    lax.fori_loop(0, 2 * own_blocks, gathered, 0)

    for first in range(SUBS):
        for index in range(first * slices // SUBS, (first + 1) * slices // SUBS):
            cols = slice(index * LANES, (index + 1) * LANES)
            part[index] = score[:tall, :, cols].reshape(hidden, LANES).astype(BF)
            part[slices + index] = score[tall : 2 * tall, :, cols].reshape(width, LANES).astype(BF)
        ring.slot(first)
    for index in range(tall):
        rows = slice(index * TILE, (index + 1) * TILE)
        product = jnp.sum(up_ref[rows, :].astype(F32) * score[tall + index], axis=1, keepdims=True)
        norms_c[rows, 4:5] = product
    norms_c[:, 5:6] = jnp.sum(bias_acc[...], axis=1, keepdims=True)
    bias_acc[...] = jnp.zeros_like(bias_acc)

    outs = (br_all, g_all)

    def block_of(step):
        return step // 2 + (blocks // 2) * (step % 2)

    def pre_copy(kind, step, block):
        rows = pl.ds(pl.multiple_of((1 - core) * half_width, 16), half_width)
        return pltpu.make_async_remote_copy(
            src_ref=outs[kind].at[pl.ds(2 * block, 2), rows],
            dst_ref=pre.at[kind, step // 2],
            send_sem=rs_send.at[kind, step],
            recv_sem=rs_recv.at[kind, step],
            device_id=(d, sib),
            device_id_type=MESH,
        )

    def sib_copy(kind, step, block):
        return pltpu.make_async_remote_copy(
            src_ref=outs[kind].at[pl.ds(2 * block, 2)],
            dst_ref=from_sib.at[kind, block % own_blocks],
            send_sem=rs_send.at[kind, step],
            recv_sem=rs_recv.at[kind, step],
            device_id=(d, sib),
            device_id_type=MESH,
        )

    def x_copy(kind, block, sender_core, owner):
        rows = pl.ds(pl.multiple_of(sender_core * half_width, 16), half_width)
        return pltpu.make_async_remote_copy(
            src_ref=outs[kind].at[pl.ds(2 * block, 2), rows],
            dst_ref=from_x.at[kind, block % own_blocks, :, rows],
            send_sem=rs_send_x.at[kind, block],
            recv_sem=rs_recv_x.at[kind, block % own_blocks, sender_core],
            device_id=(d, owner),
            device_id_type=MESH,
        )

    def scatter_first(kind, step):
        block = block_of(step)
        owner = block // own_blocks

        @pl.when(owner // 2 != chip)
        def _():
            pre_copy(kind, step, block).start()

        @pl.when((owner // 2 == chip) & (owner != t))
        def _():
            sib_copy(kind, step, block).start()

    def scatter_second(kind, step):
        block = block_of(step)
        owner = block // own_blocks

        @pl.when(owner // 2 != chip)
        def _():
            pre_copy(kind, step, block).wait()
            rows = pl.ds(pl.multiple_of(core * half_width, 16), half_width)
            mine = outs[kind][pl.ds(2 * block, 2), rows].astype(F32)
            outs[kind][pl.ds(2 * block, 2), rows] = (mine + pre[kind, step // 2].astype(F32)).astype(BF)
            x_copy(kind, block, core, owner).start()

        @pl.when((owner // 2 == chip) & (owner != t))
        def _():
            sib_copy(kind, step, block).wait_send()

    def scatter_sent(kind, step):
        block = block_of(step)
        owner = block // own_blocks

        @pl.when(owner // 2 != chip)
        def _():
            x_copy(kind, block, core, owner).wait_send()

    def scatter_arrived(kind, piece):
        block = t * own_blocks + piece
        step = 2 * (block % (blocks // 2)) + block // (blocks // 2)
        sib_copy(kind, step, block).wait_recv()
        for sender_core in range(2):
            x_copy(kind, block, sender_core, t).wait_recv()
        halves = [
            outs[kind][2 * block + half].astype(F32)
            + from_sib[kind, piece, half].astype(F32)
            + from_x[kind, piece, half].astype(F32)
            for half in range(2)
        ]
        return jnp.concatenate(halves, axis=1)

    def emit_block_out(piece):
        cols = slice(piece * TILE, (piece + 1) * TILE)
        x = pair(x_all, t * own_blocks + piece).astype(F32)
        block_out_ref[:, cols] = (x + scatter_arrived(0, piece)).astype(BF)

    def emit_grad_tokens(piece):
        place = t * own_blocks + piece
        if piece == 0:
            for hop in range(3):
                kv_copy(t, hop, (t + hop + 1) % 4).wait_recv()
        key_value_grad = gkv_all[place].astype(F32)
        for hop in range(3):
            key_value_grad = key_value_grad + kv_land[hop, piece].astype(F32)
        up_kv = mm(qkv_w[:, q_cols:], key_value_grad.astype(BF))
        scaled = scatter_arrived(1, piece) + up_kv * norms_c[:, 0:1]
        normal, inverse = standardize(pair(x_all, place).astype(F32))
        mean_one = jnp.sum(scaled, axis=0, keepdims=True) * (1.0 / width)
        mean_two = jnp.sum(scaled * normal, axis=0, keepdims=True) * (1.0 / width)
        grad_tokens_ref[:, piece * TILE : (piece + 1) * TILE] = (
            pair(gr_all, place).astype(F32) + inverse * (scaled - mean_one - normal * mean_two)
        ).astype(BF)

    def attend(step, number):
        heavy = step % 2
        ring.slot(number)
        number = number + 1
        block = block_of(step)
        queries = jnp.concatenate([q_t[2 * block], q_t[2 * block + 1]], axis=1)
        wide = heads * TILE

        def of_head(value, head):
            first = value[:, head * LANES : (head + 1) * LANES]
            second = value[:, (heads + head) * LANES : (heads + head + 1) * LANES]
            return jnp.concatenate([first, second], axis=1)

        def in_pairs(count, body, start):
            carry = lax.fori_loop(0, count // 4, lambda i, c: body(4 * i, 4, c), start)
            carry = lax.fori_loop(count // 4 * 2, count // 2, lambda i, c: body(2 * i, 2, c), carry)
            return lax.fori_loop(count // 2 * 2, count, lambda i, c: body(i, 1, c), carry)

        def lanes_of(j, tiles):
            return pl.ds(pl.multiple_of(j * TILE, TILE), tiles * TILE)

        def scores(j, tiles, top):
            tile = mm(k_r[pl.ds(j, tiles)].reshape(tiles * TILE, HD), queries)
            score[pl.ds(j, tiles)] = tile.reshape(tiles, TILE, wide)
            return jnp.maximum(top, jnp.max(tile.reshape(tiles * TILE // 8, 8, wide), axis=0))

        top = in_pairs(block, scores, jnp.full((8, wide), -1e30, F32))
        tile = mm(k_r[block], queries)
        past = lax.broadcasted_iota(jnp.int32, (TILE, wide), 0)
        now = lax.broadcasted_iota(jnp.int32, (TILE, wide), 1)
        now = now // (wide // 2) * LANES + now % LANES
        tile = jnp.where(past <= now, tile, -1e30)
        score[block] = tile
        top = jnp.maximum(top, jnp.max(tile.reshape(TILE // 8, 8, wide), axis=0))
        top = jnp.max(top, axis=0, keepdims=True)

        acc[...] = jnp.zeros_like(acc)

        @pl.when(heavy == 1)
        def _():
            ring.slot(number)

        number = number + heavy

        def weigh(j, tiles, carry):
            weights = jnp.exp(score[pl.ds(j, tiles)] - top).astype(BF)
            prob[pl.ds(j, tiles)] = weights
            acc[...] += mm(v_t[:, lanes_of(j, tiles)], weights.reshape(tiles * TILE, wide))
            return carry

        in_pairs(block + 1, weigh, 0)
        inverse = 1.0 / acc[HD : HD + 1]
        context = acc[:HD] * inverse
        grad = (pair(do_t, block).astype(F32) * inverse).astype(BF)
        delta = jnp.sum(grad.astype(F32) * context, axis=0, keepdims=True)
        acc[:HD] = jnp.zeros((HD, wide), F32)

        context_rows = jnp.concatenate([of_head(context, h) for h in range(heads)], axis=0).astype(BF)
        branch = mm(out_t[...], context_rows) + pair(br_all, block).astype(F32)
        put_pair(br_all, block, branch.astype(BF))
        scatter_first(0, step)

        @pl.when(step > 0)
        def _():
            scatter_second(1, step - 1)


        def back(j, tiles, number):
            ring.slot(number)
            weights = prob[pl.ds(j, tiles)].reshape(tiles * TILE, wide)
            grad_probs = mm(v_r[pl.ds(j, tiles)].reshape(tiles * TILE, HD), grad)
            grad_scores = (weights.astype(F32) * (grad_probs - delta)).astype(BF)
            acc[:HD] += mm(k_t[:, lanes_of(j, tiles)], grad_scores)
            d_key[:, lanes_of(j, tiles)] += mm_t(queries, grad_scores)
            d_value[:, lanes_of(j, tiles)] += mm_t(grad, weights)
            return number + 1

        number = in_pairs(block + 1, back, number)
        lanes = pl.ds(pl.multiple_of(block * TILE, TILE), TILE)
        cosine, sine = table_ref[:HALF, lanes], table_ref[HALF:, lanes]
        grad_queries = acc[:HD]
        turned = [
            turn(of_head(grad_queries, head), cosine, -sine) * (HD**-0.5) for head in range(heads)
        ]
        turned = jnp.concatenate(turned, axis=0).astype(BF)
        scatter_second(0, step)
        ring.slot(number)
        number = number + 1
        scaled = mm(qkv_w[:, :q_cols], turned) * norms_c[:, 0:1] + pair(g_all, block).astype(F32)
        put_pair(g_all, block, scaled.astype(BF))
        scatter_first(1, step)
        sum_out[...] += mm_t(context_rows, pair(gr_all, block))
        sum_qkv[:q_cols] += mm_t(turned, pair(n1_all, block))
        bias_acc[:q_cols] += turned[:, :LANES].astype(F32) + turned[:, LANES:].astype(F32)
        return number

    lax.fori_loop(0, blocks, attend, SUBS)
    groups = [n // 4 + n % 4 // 2 + n % 2 for n in range(1, blocks + 1)]
    attended = SUBS + sum(groups) + 2 * blocks + blocks // 2
    scatter_second(1, blocks - 1)
    for index in range(slices):
        cols = slice(index * LANES, (index + 1) * LANES)
        for which, source in ((0, sum_out[:, cols]), (1, sum_qkv[:q_cols, cols])):
            row = (2 * index + which) * q_cols
            part[base + row // width, row % width : row % width + q_cols] = source.astype(BF)
    ends = [(base, 0), (base + 1, 1), (base + 2, 0)]
    for unit, kind in ends:
        big.start(unit, kind, 0)

    def key_value(block, carry):
        @pl.when(block < 2)
        def _():
            ring.slot(attended + block)

        lanes = pl.ds(pl.multiple_of(block * TILE, TILE), TILE)
        cosine, sine = table_ref[:HALF, lanes], table_ref[HALF:, lanes]
        gkv_all[block, :HD] = turn(d_key[:, lanes], cosine, -sine).astype(BF)
        gkv_all[block, HD:] = d_value[:, lanes].astype(BF)
        grads = gkv_all[block]
        bias_acc[q_cols : q_cols + 2 * HD] += grads[:, :LANES].astype(F32) + grads[:, LANES:].astype(F32)
        sum_qkv[q_cols:] += mm_t(grads, pair(n1_all, block))
        return carry

    lax.fori_loop(0, blocks, key_value, 0)

    def kv_copy(owner, hop, target):
        return pltpu.make_async_remote_copy(
            src_ref=gkv_all.at[pl.ds(owner * own_blocks, own_blocks)],
            dst_ref=kv_land.at[hop],
            send_sem=kv_send.at[hop],
            recv_sem=kv_recv.at[hop],
            device_id=(d, target),
            device_id_type=MESH,
        )

    for hop in range(3):
        owner = (t + hop + 1) % 4
        kv_copy(owner, hop, owner).start()

    end_part[:width] = sum_qkv[q_cols:].T.astype(BF)
    row_sums = jnp.sum(bias_acc[: q_cols + 2 * HD], axis=1, keepdims=True)
    shift_one = jnp.sum(qkv_t[...].astype(F32) * row_sums, axis=0, keepdims=True)
    shift_two = norms_c[:, 5:6]
    product_one = jnp.sum(qkv_t[...].astype(F32) * sum_qkv[...], axis=0, keepdims=True)
    gain_one = (product_one - norms_r[1:2] * shift_one) / norms_r[0:1]
    gain_two = (norms_c[:, 4:5] - norms_c[:, 3:4] * shift_two) / norms_c[:, 2:3]
    lane = lax.broadcasted_iota(jnp.int32, (width, 8), 1)
    columns = jnp.where(lane == 0, gain_two, shift_two).T
    rows = jnp.concatenate([gain_one, shift_one, columns[:6]], axis=0)
    end_part[width:] = jnp.zeros((end_part.shape[0] - width, LANES), BF)
    for index in range(slices):
        end_part[width + 16 * index : width + 16 * index + 8] = rows[
            :, index * LANES : (index + 1) * LANES
        ].astype(BF)

    end_rows = end_part.shape[0] // RING

    def end_chunk(index):
        return pl.ds(pl.multiple_of(index * end_rows, 16), end_rows)

    def end_copy(hop, gather):
        peer = (spot + hop) % RING
        done = end_total_ref.at[end_chunk(spot)]
        return pltpu.make_async_remote_copy(
            src_ref=done if gather else end_part.at[end_chunk(peer)],
            dst_ref=done if gather else end_land.at[hop - 1],
            send_sem=end_send.at[int(gather), hop - 1],
            recv_sem=end_recv.at[int(gather), hop - 1],
            device_id=(first_of_ring + peer, t),
            device_id_type=MESH,
        )

    def end_exchange(index):
        return pltpu.make_async_remote_copy(
            src_ref=end_part.at[end_chunk(spot)],
            dst_ref=end_swap.at[index],
            send_sem=end_send.at[2, index],
            recv_sem=end_recv.at[2, index],
            device_id=(extra_peers[index], t),
            device_id_type=MESH,
        )

    def tp_copy(sender, hop):
        return pltpu.make_async_remote_copy(
            src_ref=tp_land.at[sender],
            dst_ref=tp_land.at[sender],
            send_sem=tp_send.at[hop],
            recv_sem=tp_recv.at[hop],
            device_id=(d, (t + hop + 1) % 4),
            device_id_type=MESH,
        )

    hops = range(1, RING)
    stores = [
        pltpu.make_async_copy(source, target, store_sem.at[index])
        for index, (source, target) in enumerate(
            (
                (block_out_ref, block_out_hbm),
                (grad_tokens_ref, grad_tokens_hbm),
                (total_ref.at[pl.ds(0, base)], total_hbm.at[pl.ds(0, base)]),
                (total_ref.at[pl.ds(base, 3)], total_hbm.at[pl.ds(base, 3)]),
                (end_total_ref, end_total_hbm),
            )
        )
    ]
    for hop in hops:
        end_copy(hop, False).start()

    def end_reduced():
        for hop in hops:
            end_copy(hop, False).wait()
        summed = end_part[end_chunk(spot)].astype(F32)
        for hop in hops:
            summed = summed + end_land[hop - 1].astype(F32)
        for index in range(len(plan.extra)):
            end_part[end_chunk(spot)] = summed.astype(BF)
            end_exchange(index).start()
            end_exchange(index).wait()
            summed = summed.astype(BF).astype(F32) + end_swap[index].astype(F32)
        tp_land[t] = summed.astype(BF)
        for hop in range(3):
            tp_copy(t, hop).start()

    def end_shared():
        for hop in range(3):
            tp_copy((t + 3 - hop) % 4, hop).wait_recv()
        land = [tp_land[sender].astype(F32) for sender in range(4)]
        end_total_ref[end_chunk(spot)] = (land[0] + land[1] + land[2] + land[3]).astype(BF)
        for hop in hops:
            end_copy(hop, True).start()

    ring_slots = list(range(attended + 2, plan.slots))
    for beat in range(max(plan.stages, 1 + (len(ring_slots) + 1) // 2)):
        for index in ring_slots[2 * beat : 2 * beat + 2]:
            ring.slot(index)
        if beat < plan.stages:
            for unit, kind in ends:
                big.finish(unit, kind, beat)
                if beat + 1 < plan.stages:
                    big.start(unit, kind, beat + 1)
        if beat == 0:
            emit_block_out(0)
        if beat == 1:
            end_reduced()
            emit_block_out(1)
            stores[0].start()
        if beat == 2:
            end_shared()
            emit_grad_tokens(0)
        if beat == 3:
            emit_grad_tokens(1)
            stores[1].start()
        if beat == (len(ring_slots) + 1) // 2:
            stores[2].start()
    for hop in hops:
        end_copy(hop, True).wait()
    stores[3].start()
    stores[4].start()
    for hop in range(3):
        tp_copy(t, hop).wait_send()
    for hop in range(3):
        kv_copy((t + hop + 1) % 4, hop, (t + hop + 1) % 4).wait_send()

    def drain(step, carry):
        for kind in range(2):
            scatter_sent(kind, step)
        return carry

    lax.fori_loop(0, blocks, drain, 0)
    for store in stores:
        store.wait()


def finish_kernel(
    block_out_t,
    grad_tokens_t,
    down,
    up,
    ends,
    shared,
    block_out_ref,
    grad_tokens_ref,
    grad_query_ref,
    grad_keyval_ref,
    grad_output_ref,
    grad_up_ref,
    grad_down_ref,
    *vector_refs,
):
    width = down.shape[1]
    block_out_ref[...] = block_out_t[...].T
    grad_tokens_ref[...] = grad_tokens_t[...].T
    grad_keyval_ref[...] = shared[:width].astype(F32)
    for index in range(down.shape[0]):
        cols = slice(index * LANES, (index + 1) * LANES)
        grad_down_ref[:, cols] = down[index].astype(F32)
        grad_up_ref[:, cols] = up[index].astype(F32)
        grad_output_ref[:, cols] = ends[2 * index].astype(F32)
        grad_query_ref[:, cols] = ends[2 * index + 1].astype(F32)
    for index, vector in enumerate(vector_refs):
        starts = [width + 16 * k + index for k in range(width // LANES)]
        rows = [shared[start : start + 1] for start in starts]
        vector[...] = jnp.concatenate(rows, axis=1).astype(F32).reshape(vector.shape)


def shards(
    dp,
    tokens,
    cotangent,
    tags,
    tag_weight,
    query_weight,
    key_value_weight,
    output_weight,
    up_weight,
    down_weight,
    norm_gain_one,
    norm_bias_one,
    norm_gain_two,
    norm_bias_two,
):
    plan = Plan(dp)
    _, own_len, width = tokens.shape
    full_len = 4 * own_len
    q_cols, kv_cols, hidden = query_weight.shape[1], key_value_weight.shape[1], up_weight.shape[1]
    heads = q_cols // HD
    wide = heads * TILE
    blocks, own_blocks = full_len // TILE, own_len // TILE
    frequencies = (10000.0 ** (-np.arange(0, ROT, 2, dtype=np.float32) / ROT)).astype(np.float32)
    angles = frequencies[:, None] * np.arange(full_len, dtype=np.float32)[None, :]
    table = np.concatenate([np.cos(angles), np.sin(angles)], axis=0).astype(np.float32)

    slices = width // LANES
    units = 2 * slices + 3
    end_rows = width + LANES
    extra = max(1, len(plan.extra))
    vmem = lambda *shape, kind=BF: pltpu.VMEM(shape, kind)
    dma = lambda *shape: pltpu.SemaphoreType.DMA(shape)
    scratch = [
        vmem(own_len, width),
        vmem(own_len, width),
        vmem(q_cols, width),
        vmem(width, kv_cols),
        vmem(q_cols, width),
        vmem(width, hidden),
        vmem(hidden, width),
        vmem(ROT, full_len, kind=F32),
        vmem(width, own_len),
        vmem(width, own_len),
        vmem(units, width, LANES),
        vmem(end_rows, LANES),
        dma(8),
        dma(5),
        vmem(2 * blocks, width, LANES),
        vmem(2 * blocks, width, LANES),
        vmem(2 * blocks, width, LANES),
        vmem(2 * blocks, width, LANES),
        vmem(2 * blocks, width, LANES),
        vmem(hidden, width),
        vmem(width, hidden),
        vmem(q_cols + kv_cols, width),
        vmem(width, q_cols + kv_cols),
        vmem(width, q_cols),
        vmem(2 * blocks, HD, wide // 2),
        vmem(HD, full_len),
        vmem(blocks, TILE, HD),
        vmem(HD + 16, full_len),
        vmem(blocks, TILE, HD),
        vmem(2 * blocks, HD, wide // 2),
        vmem(blocks, kv_cols, TILE),
        vmem(4, own_blocks, kv_cols, TILE),
        vmem(width, 8, kind=F32),
        vmem(8, width, kind=F32),
        vmem(width, LANES, kind=F32),
        vmem(q_cols, width, kind=F32),
        vmem(q_cols + kv_cols, width, kind=F32),
        vmem(blocks, TILE, wide, kind=F32),
        vmem(blocks, TILE, wide),
        vmem(HD + 16, wide, kind=F32),
        vmem(HD, full_len, kind=F32),
        vmem(HD, full_len, kind=F32),
        vmem(units, width, LANES),
        vmem(units, width - width // 8, LANES),
        vmem(units, extra, width // 8, LANES),
        vmem(end_rows, LANES),
        vmem(RING - 1, end_rows // RING, LANES),
        vmem(extra, end_rows // RING, LANES),
        vmem(4, end_rows // RING, LANES),
        vmem(2, blocks // 2, 2, width // 2, LANES),
        vmem(2, own_blocks, 2, width, LANES),
        vmem(2, own_blocks, 2, width, LANES),
        dma(2, own_blocks, 2, 3),
        dma(2, own_blocks, 2, 3),
        dma(2, blocks),
        dma(2, blocks),
        dma(2, blocks),
        dma(2, own_blocks, 2),
        dma(2 * SUBS, plan.steps),
        dma(2 * SUBS, plan.steps),
        dma(units, plan.stages),
        dma(units, plan.stages),
        dma(3, RING - 1),
        dma(3, RING - 1),
        dma(3),
        dma(3),
        dma(3),
        dma(3),
    ]
    in_vmem = pl.BlockSpec(memory_space=pltpu.VMEM)
    anywhere = pl.BlockSpec(memory_space=pl.ANY)
    in_smem = pl.BlockSpec(memory_space=pltpu.SMEM)
    block_out, grad_tokens, total, end_total = pl.pallas_call(
        functools.partial(block_kernel, plan),
        out_shape=(
            jax.ShapeDtypeStruct((width, own_len), BF),
            jax.ShapeDtypeStruct((width, own_len), BF),
            jax.ShapeDtypeStruct((units, width, LANES), BF),
            jax.ShapeDtypeStruct((end_rows, LANES), BF),
        ),
        in_specs=[in_smem] * 2 + [anywhere] * 7 + [in_vmem] * 4 + [anywhere],
        out_specs=(anywhere,) * 4,
        scratch_shapes=scratch,
        compiler_params=pltpu.CompilerParams(
            collective_id=0, has_side_effects=True, vmem_limit_bytes=63 << 20
        ),
    )(
        tags,
        tag_weight,
        tokens[0],
        cotangent[0],
        query_weight.T,
        key_value_weight,
        output_weight,
        up_weight,
        down_weight,
        norm_gain_one,
        norm_bias_one,
        norm_gain_two,
        norm_bias_two,
        jnp.asarray(table),
    )
    first_end = slices * width // q_cols
    finish_shapes = (
        ((own_len, width), BF),
        ((own_len, width), BF),
        ((q_cols, width), F32),
        ((width, kv_cols), F32),
        ((q_cols, width), F32),
        ((width, hidden), F32),
        ((hidden, width), F32),
        ((width,), F32),
        ((width,), F32),
        ((width,), F32),
        ((width,), F32),
    )
    group = 3
    by_columns = lambda rows: pl.BlockSpec((rows, group * LANES), lambda i: (0, i))
    by_rows = pl.BlockSpec((group * LANES, own_len), lambda i: (i, 0))
    block_out, grad_tokens, grad_query, grad_keyval, grad_output, grad_up, grad_down, *vectors = (
        pl.pallas_call(
            finish_kernel,
            grid=(slices // group,),
            out_shape=tuple(jax.ShapeDtypeStruct(*shape) for shape in finish_shapes),
            in_specs=[
                by_rows,
                by_rows,
                pl.BlockSpec((group, width, LANES), lambda i: (i, 0, 0)),
                pl.BlockSpec((group, width, LANES), lambda i: (slices // group + i, 0, 0)),
                pl.BlockSpec((2 * group, q_cols, LANES), lambda i: (first_end // group + i, 0, 0)),
                pl.BlockSpec((end_rows, LANES), lambda i: (0, 0)),
            ],
            out_specs=(
                by_columns(own_len),
                by_columns(own_len),
                by_columns(q_cols),
                pl.BlockSpec((width, kv_cols), lambda i: (0, 0)),
                by_columns(q_cols),
                by_columns(width),
                by_columns(hidden),
                pl.BlockSpec((width,), lambda i: (0,)),
                pl.BlockSpec((width,), lambda i: (0,)),
                pl.BlockSpec((width,), lambda i: (0,)),
                pl.BlockSpec((width,), lambda i: (0,)),
            ),
            compiler_params=pltpu.CompilerParams(vmem_limit_bytes=60 << 20),
        )(
            block_out,
            grad_tokens,
            total,
            total,
            total.reshape(units * width // q_cols, q_cols, LANES),
            end_total,
        )
    )
    return (
        block_out[None],
        grad_tokens[None],
        grad_query.T,
        grad_keyval,
        grad_output,
        grad_up,
        grad_down,
        *vectors,
    )


def solution(mesh):
    rows = P("dp", "tp", None)
    columns, depth, whole = P(None, "tp"), P("tp", None), P()
    in_specs = (rows, rows, P("dp"), whole, columns, whole, depth, columns, depth) + (whole,) * 4
    out_specs = (rows, rows, columns, whole, depth, columns, depth) + (whole,) * 4
    return jax.shard_map(
        functools.partial(shards, mesh.shape["dp"]),
        mesh=mesh,
        in_specs=in_specs,
        out_specs=out_specs,
        check_vma=False,
    )
```

```python
import functools

import jax
import jax.numpy as jnp
import numpy as np
from jax import lax
from jax.experimental import pallas as pl
from jax.experimental.pallas import tpu as pltpu
from jax.sharding import PartitionSpec as P

HD = 64
ROT = 16
HALF = ROT // 2
TILE = 256
LANES = 128
RING = 8
SUBS = 3
MESH = pl.DeviceIdType.MESH
BF = jnp.bfloat16
F32 = jnp.float32


def mm(left, right):
    return jnp.dot(left, right, preferred_element_type=F32)


def mm_t(left, right):
    return lax.dot_general(left, right, (((1,), (1,)), ((), ())), preferred_element_type=F32)


def turn(values, cosine, sine):
    front, back = values[:HALF], values[HALF:ROT]
    return jnp.concatenate(
        [front * cosine - back * sine, back * cosine + front * sine, values[ROT:]], axis=0
    )


class Plan:
    def __init__(self, dp):
        self.bits = dp.bit_length() - 1
        self.extra = [2**position for position in range(3, self.bits)]
        self.stages = 6 + len(self.extra)
        self.steps = 2 * (RING - 1) + len(self.extra)
        self.slots = SUBS * (self.steps + 1)

    def strides(self, kind):
        return (1 + kind, 2 - kind, 4)


class Bundle:
    def __init__(self, plan, d, t, part, landed, swapped, total, send, recv):
        self.plan, self.d, self.t = plan, d, t
        self.part, self.landed, self.swapped, self.total = part, landed, swapped, total
        self.send, self.recv = send, recv
        self.rows = part.shape[1]

    def bit(self, stride):
        return (self.d // stride) % 2

    def partner(self, stride):
        return self.d + (1 - 2 * self.bit(stride)) * stride

    def span(self, kind, depth):
        start = 0
        for level in range(depth):
            start = start + self.bit(self.plan.strides(kind)[level]) * (self.rows >> (level + 1))
        return pl.multiple_of(start, 16), self.rows >> depth

    def copy(self, unit, kind, stage):
        order, extra = self.plan.strides(kind), self.plan.extra
        if stage < 3:
            start, size = self.span(kind, stage)
            position = order[stage]
            half = size // 2
            other = pl.multiple_of(start + (1 - self.bit(position)) * half, 16)
            source = self.part.at[unit, pl.ds(other, half)]
            target = self.landed.at[unit, pl.ds(self.rows - size, half)]
        elif stage < 3 + len(extra):
            start, size = self.span(kind, 3)
            position = extra[stage - 3]
            source = self.part.at[unit, pl.ds(start, size)]
            target = self.swapped.at[unit, stage - 3]
        else:
            depth = self.plan.stages - stage
            start, size = self.span(kind, depth)
            position = order[depth - 1]
            source = self.total.at[unit, pl.ds(start, size)]
            target = source
        return pltpu.make_async_remote_copy(
            src_ref=source,
            dst_ref=target,
            send_sem=self.send.at[unit, stage],
            recv_sem=self.recv.at[unit, stage],
            device_id=(self.partner(position), self.t),
            device_id_type=MESH,
        )

    def start(self, unit, kind, stage):
        self.copy(unit, kind, stage).start()

    def finish(self, unit, kind, stage, publish=True):
        self.copy(unit, kind, stage).wait()
        last = 2 + len(self.plan.extra)
        if stage <= last:
            if stage < 3:
                start, size = self.span(kind, stage + 1)
                arrived = self.landed[unit, pl.ds(self.rows - 2 * size, size)]
            else:
                start, size = self.span(kind, 3)
                arrived = self.swapped[unit, stage - 3]
            mine = self.part[unit, pl.ds(start, size)]
            summed = (mine.astype(F32) + arrived.astype(F32)).astype(BF)
            if stage == last and publish:
                self.total[unit, pl.ds(start, size)] = summed
            else:
                self.part[unit, pl.ds(start, size)] = summed


class Ring:
    def __init__(self, plan, d, t, part, landed, swapped, total, send, recv, height):
        self.plan, self.d, self.t = plan, d, t
        self.part, self.landed, self.swapped, self.total = part, landed, swapped, total
        self.send, self.recv = send, recv
        self.height = height
        self.rows = part.shape[1] // RING
        self.first = d - d % RING
        line, side = (d % RING) // 2, d % 2
        self.place = line + side * (RING - 1 - 2 * line)
        self.neighbours = [
            self.device(lax.rem(self.place + ahead, jnp.int32(RING))) for ahead in (1, RING - 1)
        ]

    def device(self, place):
        far = place // (RING // 2)
        return self.first + (1 - far) * 2 * place + far * (2 * RING - 1 - 2 * place)

    def units(self, way, sub):
        return pl.ds((SUBS * way + sub) * self.height, self.height)

    def chunk(self, way, ahead):
        index = lax.rem(self.place + RING + (1, -1)[way] * ahead, jnp.int32(RING))
        return pl.ds(pl.multiple_of(index * self.rows, 16), self.rows)

    def copy(self, way, sub, phase, index, step):
        units = self.units(way, sub)
        peer = self.neighbours[way]
        if phase == 0:
            source = self.part.at[units, self.chunk(way, -index)]
            slot = pl.ds(pl.multiple_of(index * self.rows, 16), self.rows)
            target = self.landed.at[units, slot]
        elif phase == 1:
            stride = self.plan.extra[index]
            peer = self.d + (1 - 2 * ((self.d // stride) % 2)) * stride
            source = self.part.at[units, self.chunk(way, 1)]
            target = self.swapped.at[units, index]
        else:
            source = self.total.at[units, self.chunk(way, 1 - index)]
            target = source
        return pltpu.make_async_remote_copy(
            src_ref=source,
            dst_ref=target,
            send_sem=self.send.at[SUBS * way + sub, step],
            recv_sem=self.recv.at[SUBS * way + sub, step],
            device_id=(peer, self.t),
            device_id_type=MESH,
        )

    def finish(self, way, sub, phase, index, step, last):
        if phase == 2:
            return
        units = self.units(way, sub)
        if phase == 0:
            slot = pl.ds(pl.multiple_of(index * self.rows, 16), self.rows)
            rows, arrived = self.chunk(way, -1 - index), self.landed[units, slot]
        else:
            rows, arrived = self.chunk(way, 1), self.swapped[units, index]
        summed = (self.part[units, rows].astype(F32) + arrived.astype(F32)).astype(BF)
        (self.total if last else self.part)[units, rows] = summed

    def slot(self, number):
        number = jnp.int32(number)
        step = lax.div(number, jnp.int32(SUBS))
        sub = number - step * SUBS
        extra = len(self.plan.extra)
        turns = RING - 1
        middle = turns + extra

        def when(condition, ended, begun, last=False):
            @pl.when(condition)
            def _():
                if ended is not None:
                    for way in range(2):
                        self.copy(way, sub, *ended, step - 1).wait()
                        self.finish(way, sub, *ended, step - 1, last)
                        if begun is not None:
                            self.copy(way, sub, *begun, step).start()
                else:
                    for way in range(2):
                        self.copy(way, sub, *begun, step).start()

        when(step == 0, None, (0, 0))
        when((step > 0) & (step < turns), (0, step - 1), (0, step))
        for index in range(extra + 1):
            ended = (0, turns - 1) if index == 0 else (1, index - 1)
            begun = (2, 0) if index == extra else (1, index)
            when(step == turns + index, ended, begun, last=index == extra)
        when((step > middle) & (step < self.plan.steps), (2, step - 1 - middle), (2, step - middle))
        when(step == self.plan.steps, (2, turns - 1), None)


def block_kernel(
    plan,
    tags_ref,
    tag_weight_ref,
    tok_hbm,
    cot_hbm,
    query_t_hbm,
    keyval_hbm,
    output_hbm,
    up_hbm,
    down_hbm,
    gain_one_ref,
    bias_one_ref,
    gain_two_ref,
    bias_two_ref,
    table_hbm,
    block_out_hbm,
    grad_tokens_hbm,
    total_hbm,
    end_total_hbm,
    tok_ref,
    cot_ref,
    query_t_ref,
    keyval_ref,
    output_ref,
    up_ref,
    down_ref,
    table_ref,
    block_out_ref,
    grad_tokens_ref,
    total_ref,
    end_total_ref,
    load_sem,
    store_sem,
    x_all,
    gr_all,
    n1_all,
    br_all,
    g_all,
    up_t,
    down_t,
    qkv_t,
    qkv_w,
    out_t,
    q_t,
    k_t,
    k_r,
    v_t,
    v_r,
    do_t,
    gkv_all,
    kv_land,
    norms_c,
    norms_r,
    bias_acc,
    sum_out,
    sum_qkv,
    score,
    prob,
    acc,
    d_key,
    d_value,
    part,
    landed,
    swapped,
    end_part,
    end_land,
    end_swap,
    tp_land,
    pre,
    from_sib,
    from_x,
    ag_send,
    ag_recv,
    rs_send,
    rs_recv,
    rs_send_x,
    rs_recv_x,
    ring_send,
    ring_recv,
    dp_send,
    dp_recv,
    end_send,
    end_recv,
    tp_send,
    tp_recv,
    kv_send,
    kv_recv,
):
    d, t = lax.axis_index("dp"), lax.axis_index("tp")
    chip, core = t // 2, t % 2
    sib = t + 1 - 2 * core
    across = (t + 2) % 4
    diag = (sib + 2) % 4
    width = tok_ref.shape[1]
    hidden = up_ref.shape[1]
    q_cols = query_t_ref.shape[0]
    heads = q_cols // HD
    own_blocks = tok_ref.shape[0] // TILE
    blocks = 4 * own_blocks
    half_width = width // 2
    tall = width // TILE

    slices = width // LANES
    base = 2 * slices
    big = Bundle(plan, d, t, part, landed, swapped, total_ref, dp_send, dp_recv)
    ring = Ring(
        plan, d, t, part, landed, swapped, total_ref, ring_send, ring_recv, slices // SUBS
    )

    loads = [
        pltpu.make_async_copy(source, target, load_sem.at[index])
        for index, (source, target) in enumerate(
            (
                (tok_hbm, tok_ref),
                (cot_hbm, cot_ref),
                (up_hbm, up_ref),
                (down_hbm, down_ref),
                (query_t_hbm, query_t_ref),
                (keyval_hbm, keyval_ref),
                (output_hbm, output_ref),
                (table_hbm, table_ref),
            )
        )
    ]
    for load in loads:
        load.start()

    barrier = pltpu.get_barrier_semaphore()
    first_of_ring, spot = d - d % RING, d % RING
    ring_peers = [first_of_ring + (spot + hop) % RING for hop in range(1, RING)]
    extra_peers = [d + (1 - 2 * ((d // stride) % 2)) * stride for stride in plan.extra]
    peers = [(d, sib), (d, across), (d, diag)] + [(peer, t) for peer in ring_peers + extra_peers]
    for peer in peers:
        pl.semaphore_signal(barrier, inc=1, device_id=peer, device_id_type=MESH)
    pl.semaphore_wait(barrier, len(peers))

    row_weight = tag_weight_ref[tags_ref[0]]

    sets = (x_all, gr_all)

    def pair(ref, block):
        return jnp.concatenate([ref[2 * block], ref[2 * block + 1]], axis=1)

    def put_pair(ref, block, value):
        ref[2 * block] = value[:, :LANES]
        ref[2 * block + 1] = value[:, LANES:]

    def half_lanes(start, half):
        return pl.ds(pl.multiple_of(start + half * LANES, LANES), LANES)

    def gather_copy(kind, piece, half, owner, route):
        place = owner * own_blocks + piece
        target = {0: sib, 1: across, 2: sib}[route]
        view = sets[kind].at[2 * place + half]
        return pltpu.make_async_remote_copy(
            src_ref=view,
            dst_ref=view,
            send_sem=ag_send.at[kind, piece, half, route],
            recv_sem=ag_recv.at[kind, piece, half, route],
            device_id=(d, target),
            device_id_type=MESH,
        )

    loads[0].wait()
    loads[1].wait()
    for piece in range(own_blocks):
        rows = slice(piece * TILE, (piece + 1) * TILE)
        put_pair(x_all, t * own_blocks + piece, tok_ref[rows, :].T)
        for half in range(2):
            gather_copy(0, piece, half, t, 0).start()
        gather_copy(0, piece, 0, t, 1).start()
        weighted = (cot_ref[rows, :].astype(F32) * row_weight).astype(BF).T
        put_pair(gr_all, t * own_blocks + piece, weighted)
        for half in range(2):
            gather_copy(1, piece, half, t, 0).start()
        gather_copy(1, piece, 0, t, 1).start()
        gather_copy(0, piece, 1, t, 1).start()
        gather_copy(1, piece, 1, t, 1).start()

    for load in loads[2:]:
        load.wait()
    up_t[...] = up_ref[...].T
    down_t[...] = down_ref[...].T
    qkv_t[:q_cols] = query_t_ref[...]
    qkv_t[q_cols:] = keyval_ref[...].T
    qkv_w[...] = qkv_t[...].T
    out_t[...] = output_ref[...].T
    for index, norm in enumerate((gain_one_ref, bias_one_ref, gain_two_ref, bias_two_ref)):
        norms_r[index : index + 1] = norm[...].reshape(1, width)
    norms_c[...] = norms_r[...].T
    score[...] = jnp.zeros_like(score)
    bias_acc[...] = jnp.zeros_like(bias_acc)
    sum_out[...] = jnp.zeros_like(sum_out)
    sum_qkv[...] = jnp.zeros_like(sum_qkv)
    d_key[...] = jnp.zeros_like(d_key)
    d_value[...] = jnp.zeros_like(d_value)

    def standardize(x):
        mean = jnp.sum(x, axis=0, keepdims=True) * (1.0 / width)
        centred = x - mean
        variance = jnp.sum(centred * centred, axis=0, keepdims=True) * (1.0 / width)
        inverse = lax.rsqrt(variance + 1e-05)
        return centred * inverse, inverse

    def feed_forward(step, carry):
        late, piece, half = step // 4, (step % 4) // 2, step % 2
        owners = (
            (1 - late) * t + late * across,
            (1 - late) * sib + late * diag,
        )
        places = [owner * own_blocks + piece for owner in owners]
        sides = [slice(0, LANES), slice(LANES, TILE)]

        @pl.when(late == 0)
        def _():
            for kind in range(2):
                gather_copy(kind, piece, half, sib, 0).wait_recv()

        @pl.when(late == 1)
        def _():
            for kind in range(2):
                gather_copy(kind, piece, half, across, 1).wait_recv()
                gather_copy(kind, piece, half, across, 2).start()
            for kind in range(2):
                gather_copy(kind, piece, half, diag, 2).wait_recv()

        def load(ref):
            return jnp.concatenate([ref[2 * place + half] for place in places], axis=1)

        def store(ref, value):
            for place, side in zip(places, sides):
                ref[2 * place + half] = value[:, side]

        normal, _ = standardize(load(x_all).astype(F32))
        n1 = (normal * norms_c[:, 0:1] + norms_c[:, 1:2]).astype(BF)
        n2 = (normal * norms_c[:, 2:3] + norms_c[:, 3:4]).astype(BF)
        store(n1_all, n1)
        gr = load(gr_all)
        qkv = mm(qkv_t[...], n1)
        lanes = [half_lanes(place * TILE, half) for place in places]
        cosine = jnp.concatenate([table_ref[:HALF, at] for at in lanes], axis=1)
        sine = jnp.concatenate([table_ref[HALF:, at] for at in lanes], axis=1)
        grad_context = mm(output_ref[...], gr)
        for head in range(heads):
            rows = slice(head * HD, (head + 1) * HD)
            turned = (turn(qkv[rows], cosine, sine) * (HD**-0.5)).astype(BF)
            grads = grad_context[rows].astype(BF)
            for place, side in zip(places, sides):
                at = slice(head * LANES, (head + 1) * LANES)
                q_t[2 * place + half, :, at] = turned[:, side]
                do_t[2 * place + half, :, at] = grads[:, side]
        key = turn(qkv[q_cols : q_cols + HD], cosine, sine)
        value = qkv[q_cols + HD :]
        for place, side, at in zip(places, sides, lanes):
            k_t[:, at] = key[:, side].astype(BF)
            v_t[:HD, at] = value[:, side].astype(BF)
            v_t[HD:, at] = jnp.ones((v_t.shape[0] - HD, LANES), BF)
            k_r[place, half_lanes(0, half), :] = key[:, side].T.astype(BF)
            v_r[place, half_lanes(0, half), :] = value[:, side].T.astype(BF)

        chunks = [slice(c * TILE, (c + 1) * TILE) for c in range(tall)]

        def activate(pre_act):
            cdf = 0.5 + 0.5 * lax.erf(pre_act * 0.7071067811865476)
            density = jnp.exp(-0.5 * pre_act * pre_act) * 0.3989422804014327
            return (pre_act * cdf).astype(BF), cdf + pre_act * density

        pre_acts = [mm(up_t[chunks[0], :], n2)]
        grad_mids, middles, grads = [], [], []
        for c in range(tall):
            grad_mids.append(mm(down_ref[chunks[c], :], gr))
            if c + 1 < tall:
                pre_acts.append(mm(up_t[chunks[c + 1], :], n2))
            middle, slope = activate(pre_acts[c])
            middles.append(middle)
            grads.append((grad_mids[c] * slope).astype(BF))
            if c > 0:
                score[c - 1] += mm_t(middles[c - 1], gr)
        middle = jnp.concatenate(middles, axis=0)
        grad_hidden = jnp.concatenate(grads, axis=0)
        score[tall - 1] += mm_t(middles[-1], gr)
        store(br_all, mm(down_t[...], middle).astype(BF))
        up_two = mm(up_ref[...], grad_hidden)
        bias_acc[...] += up_two[:, :LANES] + up_two[:, LANES:]
        store(g_all, (up_two * norms_c[:, 2:3]).astype(BF))
        score[tall : 2 * tall] += mm_t(n2, grad_hidden).reshape(tall, TILE, hidden)
        return carry

    lax.fori_loop(0, blocks, feed_forward, 0)

    def gathered(index, carry):
        piece, half = index // 2, index % 2
        for kind in range(2):
            gather_copy(kind, piece, half, t, 0).wait_send()
            gather_copy(kind, piece, half, t, 1).wait_send()
            gather_copy(kind, piece, half, across, 2).wait_send()
        return carry

    lax.fori_loop(0, 2 * own_blocks, gathered, 0)

    for first in range(SUBS):
        for index in range(first * slices // SUBS, (first + 1) * slices // SUBS):
            cols = slice(index * LANES, (index + 1) * LANES)
            part[index] = score[:tall, :, cols].reshape(hidden, LANES).astype(BF)
            part[slices + index] = score[tall : 2 * tall, :, cols].reshape(width, LANES).astype(BF)
        ring.slot(first)
    for index in range(tall):
        rows = slice(index * TILE, (index + 1) * TILE)
        product = jnp.sum(up_ref[rows, :].astype(F32) * score[tall + index], axis=1, keepdims=True)
        norms_c[rows, 4:5] = product
    norms_c[:, 5:6] = jnp.sum(bias_acc[...], axis=1, keepdims=True)
    bias_acc[...] = jnp.zeros_like(bias_acc)

    outs = (br_all, g_all)

    def block_of(step):
        return step // 2 + (blocks // 2) * (step % 2)

    def pre_copy(kind, step, block):
        rows = pl.ds(pl.multiple_of((1 - core) * half_width, 16), half_width)
        return pltpu.make_async_remote_copy(
            src_ref=outs[kind].at[pl.ds(2 * block, 2), rows],
            dst_ref=pre.at[kind, step // 2],
            send_sem=rs_send.at[kind, step],
            recv_sem=rs_recv.at[kind, step],
            device_id=(d, sib),
            device_id_type=MESH,
        )

    def sib_copy(kind, step, block):
        return pltpu.make_async_remote_copy(
            src_ref=outs[kind].at[pl.ds(2 * block, 2)],
            dst_ref=from_sib.at[kind, block % own_blocks],
            send_sem=rs_send.at[kind, step],
            recv_sem=rs_recv.at[kind, step],
            device_id=(d, sib),
            device_id_type=MESH,
        )

    def x_copy(kind, block, sender_core, owner):
        rows = pl.ds(pl.multiple_of(sender_core * half_width, 16), half_width)
        return pltpu.make_async_remote_copy(
            src_ref=outs[kind].at[pl.ds(2 * block, 2), rows],
            dst_ref=from_x.at[kind, block % own_blocks, :, rows],
            send_sem=rs_send_x.at[kind, block],
            recv_sem=rs_recv_x.at[kind, block % own_blocks, sender_core],
            device_id=(d, owner),
            device_id_type=MESH,
        )

    def scatter_first(kind, step):
        block = block_of(step)
        owner = block // own_blocks

        @pl.when(owner // 2 != chip)
        def _():
            pre_copy(kind, step, block).start()

        @pl.when((owner // 2 == chip) & (owner != t))
        def _():
            sib_copy(kind, step, block).start()

    def scatter_second(kind, step):
        block = block_of(step)
        owner = block // own_blocks

        @pl.when(owner // 2 != chip)
        def _():
            pre_copy(kind, step, block).wait()
            rows = pl.ds(pl.multiple_of(core * half_width, 16), half_width)
            mine = outs[kind][pl.ds(2 * block, 2), rows].astype(F32)
            outs[kind][pl.ds(2 * block, 2), rows] = (mine + pre[kind, step // 2].astype(F32)).astype(BF)
            x_copy(kind, block, core, owner).start()

        @pl.when((owner // 2 == chip) & (owner != t))
        def _():
            sib_copy(kind, step, block).wait_send()

    def scatter_sent(kind, step):
        block = block_of(step)
        owner = block // own_blocks

        @pl.when(owner // 2 != chip)
        def _():
            x_copy(kind, block, core, owner).wait_send()

    def scatter_arrived(kind, piece):
        block = t * own_blocks + piece
        step = 2 * (block % (blocks // 2)) + block // (blocks // 2)
        sib_copy(kind, step, block).wait_recv()
        for sender_core in range(2):
            x_copy(kind, block, sender_core, t).wait_recv()
        halves = [
            outs[kind][2 * block + half].astype(F32)
            + from_sib[kind, piece, half].astype(F32)
            + from_x[kind, piece, half].astype(F32)
            for half in range(2)
        ]
        return jnp.concatenate(halves, axis=1)

    def emit_block_out(piece):
        cols = slice(piece * TILE, (piece + 1) * TILE)
        x = pair(x_all, t * own_blocks + piece).astype(F32)
        block_out_ref[:, cols] = (x + scatter_arrived(0, piece)).astype(BF)

    def emit_grad_tokens(piece):
        place = t * own_blocks + piece
        if piece == 0:
            for hop in range(3):
                kv_copy(t, hop, (t + hop + 1) % 4).wait_recv()
        key_value_grad = gkv_all[place].astype(F32)
        for hop in range(3):
            key_value_grad = key_value_grad + kv_land[hop, piece].astype(F32)
        up_kv = mm(qkv_w[:, q_cols:], key_value_grad.astype(BF))
        scaled = scatter_arrived(1, piece) + up_kv * norms_c[:, 0:1]
        normal, inverse = standardize(pair(x_all, place).astype(F32))
        mean_one = jnp.sum(scaled, axis=0, keepdims=True) * (1.0 / width)
        mean_two = jnp.sum(scaled * normal, axis=0, keepdims=True) * (1.0 / width)
        grad_tokens_ref[:, piece * TILE : (piece + 1) * TILE] = (
            pair(gr_all, place).astype(F32) + inverse * (scaled - mean_one - normal * mean_two)
        ).astype(BF)

    def attend(step, number):
        heavy = step % 2
        ring.slot(number)
        number = number + 1
        block = block_of(step)
        queries = jnp.concatenate([q_t[2 * block], q_t[2 * block + 1]], axis=1)
        wide = heads * TILE

        def of_head(value, head):
            first = value[:, head * LANES : (head + 1) * LANES]
            second = value[:, (heads + head) * LANES : (heads + head + 1) * LANES]
            return jnp.concatenate([first, second], axis=1)

        def in_pairs(count, body, start):
            carry = lax.fori_loop(0, count // 4, lambda i, c: body(4 * i, 4, c), start)
            carry = lax.fori_loop(count // 4 * 2, count // 2, lambda i, c: body(2 * i, 2, c), carry)
            return lax.fori_loop(count // 2 * 2, count, lambda i, c: body(i, 1, c), carry)

        def lanes_of(j, tiles):
            return pl.ds(pl.multiple_of(j * TILE, TILE), tiles * TILE)

        def scores(j, tiles, top):
            tile = mm(k_r[pl.ds(j, tiles)].reshape(tiles * TILE, HD), queries)
            score[pl.ds(j, tiles)] = tile.reshape(tiles, TILE, wide)
            return jnp.maximum(top, jnp.max(tile.reshape(tiles * TILE // 8, 8, wide), axis=0))

        top = in_pairs(block, scores, jnp.full((8, wide), -1e30, F32))
        tile = mm(k_r[block], queries)
        past = lax.broadcasted_iota(jnp.int32, (TILE, wide), 0)
        now = lax.broadcasted_iota(jnp.int32, (TILE, wide), 1)
        now = now // (wide // 2) * LANES + now % LANES
        tile = jnp.where(past <= now, tile, -1e30)
        score[block] = tile
        top = jnp.maximum(top, jnp.max(tile.reshape(TILE // 8, 8, wide), axis=0))
        top = jnp.max(top, axis=0, keepdims=True)

        acc[...] = jnp.zeros_like(acc)

        @pl.when(heavy == 1)
        def _():
            ring.slot(number)

        number = number + heavy

        def weigh(j, tiles, carry):
            weights = jnp.exp(score[pl.ds(j, tiles)] - top).astype(BF)
            prob[pl.ds(j, tiles)] = weights
            acc[...] += mm(v_t[:, lanes_of(j, tiles)], weights.reshape(tiles * TILE, wide))
            return carry

        in_pairs(block + 1, weigh, 0)
        inverse = 1.0 / acc[HD : HD + 1]
        context = acc[:HD] * inverse
        grad = (pair(do_t, block).astype(F32) * inverse).astype(BF)
        delta = jnp.sum(grad.astype(F32) * context, axis=0, keepdims=True)
        acc[:HD] = jnp.zeros((HD, wide), F32)

        context_rows = jnp.concatenate([of_head(context, h) for h in range(heads)], axis=0).astype(BF)
        branch = mm(out_t[...], context_rows) + pair(br_all, block).astype(F32)
        put_pair(br_all, block, branch.astype(BF))
        scatter_first(0, step)

        @pl.when(step > 0)
        def _():
            scatter_second(1, step - 1)


        def back(j, tiles, number):
            ring.slot(number)
            weights = prob[pl.ds(j, tiles)].reshape(tiles * TILE, wide)
            grad_probs = mm(v_r[pl.ds(j, tiles)].reshape(tiles * TILE, HD), grad)
            grad_scores = (weights.astype(F32) * (grad_probs - delta)).astype(BF)
            acc[:HD] += mm(k_t[:, lanes_of(j, tiles)], grad_scores)
            d_key[:, lanes_of(j, tiles)] += mm_t(queries, grad_scores)
            d_value[:, lanes_of(j, tiles)] += mm_t(grad, weights)
            return number + 1

        number = in_pairs(block + 1, back, number)
        lanes = pl.ds(pl.multiple_of(block * TILE, TILE), TILE)
        cosine, sine = table_ref[:HALF, lanes], table_ref[HALF:, lanes]
        grad_queries = acc[:HD]
        turned = [
            turn(of_head(grad_queries, head), cosine, -sine) * (HD**-0.5) for head in range(heads)
        ]
        turned = jnp.concatenate(turned, axis=0).astype(BF)
        scatter_second(0, step)
        ring.slot(number)
        number = number + 1
        scaled = mm(qkv_w[:, :q_cols], turned) * norms_c[:, 0:1] + pair(g_all, block).astype(F32)
        put_pair(g_all, block, scaled.astype(BF))
        scatter_first(1, step)
        sum_out[...] += mm_t(context_rows, pair(gr_all, block))
        sum_qkv[:q_cols] += mm_t(turned, pair(n1_all, block))
        bias_acc[:q_cols] += turned[:, :LANES].astype(F32) + turned[:, LANES:].astype(F32)
        return number

    lax.fori_loop(0, blocks, attend, SUBS)
    groups = [n // 4 + n % 4 // 2 + n % 2 for n in range(1, blocks + 1)]
    attended = SUBS + sum(groups) + 2 * blocks + blocks // 2
    scatter_second(1, blocks - 1)
    for index in range(slices):
        cols = slice(index * LANES, (index + 1) * LANES)
        for which, source in ((0, sum_out[:, cols]), (1, sum_qkv[:q_cols, cols])):
            row = (2 * index + which) * q_cols
            part[base + row // width, row % width : row % width + q_cols] = source.astype(BF)
    ends = [(base, 0), (base + 1, 1), (base + 2, 0)]
    for unit, kind in ends:
        big.start(unit, kind, 0)

    def key_value(step, carry):
        for block in (2 * step, 2 * step + 1):
            lanes = pl.ds(pl.multiple_of(block * TILE, TILE), TILE)
            cosine, sine = table_ref[:HALF, lanes], table_ref[HALF:, lanes]
            key_grads = turn(d_key[:, lanes], cosine, -sine)
            grads = jnp.concatenate([key_grads, d_value[:, lanes]], axis=0).astype(BF)
            gkv_all[block] = grads
            bias_acc[q_cols : q_cols + 2 * HD] += grads[:, :LANES].astype(F32) + grads[:, LANES:].astype(F32)
            sum_qkv[q_cols:] += mm_t(grads, pair(n1_all, block))
        return carry

    lax.fori_loop(0, blocks // 2, key_value, 0)

    def kv_copy(owner, hop, target):
        return pltpu.make_async_remote_copy(
            src_ref=gkv_all.at[pl.ds(owner * own_blocks, own_blocks)],
            dst_ref=kv_land.at[hop],
            send_sem=kv_send.at[hop],
            recv_sem=kv_recv.at[hop],
            device_id=(d, target),
            device_id_type=MESH,
        )

    for hop in range(3):
        owner = (t + hop + 1) % 4
        kv_copy(owner, hop, owner).start()

    end_part[:width] = sum_qkv[q_cols:].T.astype(BF)
    row_sums = jnp.sum(bias_acc[: q_cols + 2 * HD], axis=1, keepdims=True)
    shift_one = jnp.sum(qkv_t[...].astype(F32) * row_sums, axis=0, keepdims=True)
    shift_two = norms_c[:, 5:6]
    product_one = jnp.sum(qkv_t[...].astype(F32) * sum_qkv[...], axis=0, keepdims=True)
    gain_one = (product_one - norms_r[1:2] * shift_one) / norms_r[0:1]
    gain_two = (norms_c[:, 4:5] - norms_c[:, 3:4] * shift_two) / norms_c[:, 2:3]
    lane = lax.broadcasted_iota(jnp.int32, (width, 8), 1)
    columns = jnp.where(lane == 0, gain_two, shift_two).T
    rows = jnp.concatenate([gain_one, shift_one, columns[:6]], axis=0)
    end_part[width:] = jnp.zeros((end_part.shape[0] - width, LANES), BF)
    for index in range(slices):
        end_part[width + 16 * index : width + 16 * index + 8] = rows[
            :, index * LANES : (index + 1) * LANES
        ].astype(BF)

    end_rows = end_part.shape[0] // RING

    def end_chunk(index):
        return pl.ds(pl.multiple_of(index * end_rows, 16), end_rows)

    def end_copy(hop, gather):
        peer = (spot + hop) % RING
        done = end_total_ref.at[end_chunk(spot)]
        return pltpu.make_async_remote_copy(
            src_ref=done if gather else end_part.at[end_chunk(peer)],
            dst_ref=done if gather else end_land.at[hop - 1],
            send_sem=end_send.at[int(gather), hop - 1],
            recv_sem=end_recv.at[int(gather), hop - 1],
            device_id=(first_of_ring + peer, t),
            device_id_type=MESH,
        )

    def end_exchange(index):
        return pltpu.make_async_remote_copy(
            src_ref=end_part.at[end_chunk(spot)],
            dst_ref=end_swap.at[index],
            send_sem=end_send.at[2, index],
            recv_sem=end_recv.at[2, index],
            device_id=(extra_peers[index], t),
            device_id_type=MESH,
        )

    def tp_copy(sender, hop):
        return pltpu.make_async_remote_copy(
            src_ref=tp_land.at[sender],
            dst_ref=tp_land.at[sender],
            send_sem=tp_send.at[hop],
            recv_sem=tp_recv.at[hop],
            device_id=(d, (t + hop + 1) % 4),
            device_id_type=MESH,
        )

    hops = range(1, RING)
    stores = [
        pltpu.make_async_copy(source, target, store_sem.at[index])
        for index, (source, target) in enumerate(
            (
                (block_out_ref, block_out_hbm),
                (grad_tokens_ref, grad_tokens_hbm),
                (total_ref.at[pl.ds(0, base)], total_hbm.at[pl.ds(0, base)]),
                (total_ref.at[pl.ds(base, 3)], total_hbm.at[pl.ds(base, 3)]),
                (end_total_ref, end_total_hbm),
            )
        )
    ]
    for hop in hops:
        end_copy(hop, False).start()

    def end_reduced():
        for hop in hops:
            end_copy(hop, False).wait()
        summed = end_part[end_chunk(spot)].astype(F32)
        for hop in hops:
            summed = summed + end_land[hop - 1].astype(F32)
        for index in range(len(plan.extra)):
            end_part[end_chunk(spot)] = summed.astype(BF)
            end_exchange(index).start()
            end_exchange(index).wait()
            summed = summed.astype(BF).astype(F32) + end_swap[index].astype(F32)
        tp_land[t] = summed.astype(BF)
        for hop in range(3):
            tp_copy(t, hop).start()

    def end_shared():
        for hop in range(3):
            tp_copy((t + 3 - hop) % 4, hop).wait_recv()
        land = [tp_land[sender].astype(F32) for sender in range(4)]
        end_total_ref[end_chunk(spot)] = (land[0] + land[1] + land[2] + land[3]).astype(BF)
        for hop in hops:
            end_copy(hop, True).start()

    ring_slots = list(range(attended, plan.slots))
    for beat in range(max(plan.stages, 1 + (len(ring_slots) + 1) // 2)):
        if beat < plan.stages:
            for unit, kind in ends:
                big.finish(unit, kind, beat)
                if beat + 1 < plan.stages:
                    big.start(unit, kind, beat + 1)
        for index in ring_slots[2 * beat : 2 * beat + 2]:
            ring.slot(index)
        if beat == 0:
            emit_block_out(0)
        if beat == 1:
            end_reduced()
            emit_block_out(1)
            stores[0].start()
        if beat == 2:
            end_shared()
            emit_grad_tokens(0)
        if beat == 3:
            emit_grad_tokens(1)
            stores[1].start()
        if beat == (len(ring_slots) + 1) // 2:
            stores[2].start()
    for hop in hops:
        end_copy(hop, True).wait()
    stores[3].start()
    stores[4].start()
    for hop in range(3):
        tp_copy(t, hop).wait_send()
    for hop in range(3):
        kv_copy((t + hop + 1) % 4, hop, (t + hop + 1) % 4).wait_send()

    def drain(step, carry):
        for kind in range(2):
            scatter_sent(kind, step)
        return carry

    lax.fori_loop(0, blocks, drain, 0)
    for store in stores:
        store.wait()


def finish_kernel(
    block_out_t,
    grad_tokens_t,
    down,
    up,
    ends,
    shared,
    block_out_ref,
    grad_tokens_ref,
    grad_query_ref,
    grad_keyval_ref,
    grad_output_ref,
    grad_up_ref,
    grad_down_ref,
    *vector_refs,
):
    width = down.shape[1]
    block_out_ref[...] = block_out_t[...].T
    grad_tokens_ref[...] = grad_tokens_t[...].T
    grad_keyval_ref[...] = shared[:width].astype(F32)
    for index in range(down.shape[0]):
        cols = slice(index * LANES, (index + 1) * LANES)
        grad_down_ref[:, cols] = down[index].astype(F32)
        grad_up_ref[:, cols] = up[index].astype(F32)
        grad_output_ref[:, cols] = ends[2 * index].astype(F32)
        grad_query_ref[:, cols] = ends[2 * index + 1].astype(F32)
    for index, vector in enumerate(vector_refs):
        starts = [width + 16 * k + index for k in range(width // LANES)]
        rows = [shared[start : start + 1] for start in starts]
        vector[...] = jnp.concatenate(rows, axis=1).astype(F32).reshape(vector.shape)


def shards(
    dp,
    tokens,
    cotangent,
    tags,
    tag_weight,
    query_weight,
    key_value_weight,
    output_weight,
    up_weight,
    down_weight,
    norm_gain_one,
    norm_bias_one,
    norm_gain_two,
    norm_bias_two,
):
    plan = Plan(dp)
    _, own_len, width = tokens.shape
    full_len = 4 * own_len
    q_cols, kv_cols, hidden = query_weight.shape[1], key_value_weight.shape[1], up_weight.shape[1]
    heads = q_cols // HD
    wide = heads * TILE
    blocks, own_blocks = full_len // TILE, own_len // TILE
    frequencies = (10000.0 ** (-np.arange(0, ROT, 2, dtype=np.float32) / ROT)).astype(np.float32)
    angles = frequencies[:, None] * np.arange(full_len, dtype=np.float32)[None, :]
    table = np.concatenate([np.cos(angles), np.sin(angles)], axis=0).astype(np.float32)

    slices = width // LANES
    units = 2 * slices + 3
    end_rows = width + LANES
    extra = max(1, len(plan.extra))
    vmem = lambda *shape, kind=BF: pltpu.VMEM(shape, kind)
    dma = lambda *shape: pltpu.SemaphoreType.DMA(shape)
    scratch = [
        vmem(own_len, width),
        vmem(own_len, width),
        vmem(q_cols, width),
        vmem(width, kv_cols),
        vmem(q_cols, width),
        vmem(width, hidden),
        vmem(hidden, width),
        vmem(ROT, full_len, kind=F32),
        vmem(width, own_len),
        vmem(width, own_len),
        vmem(units, width, LANES),
        vmem(end_rows, LANES),
        dma(8),
        dma(5),
        vmem(2 * blocks, width, LANES),
        vmem(2 * blocks, width, LANES),
        vmem(2 * blocks, width, LANES),
        vmem(2 * blocks, width, LANES),
        vmem(2 * blocks, width, LANES),
        vmem(hidden, width),
        vmem(width, hidden),
        vmem(q_cols + kv_cols, width),
        vmem(width, q_cols + kv_cols),
        vmem(width, q_cols),
        vmem(2 * blocks, HD, wide // 2),
        vmem(HD, full_len),
        vmem(blocks, TILE, HD),
        vmem(HD + 16, full_len),
        vmem(blocks, TILE, HD),
        vmem(2 * blocks, HD, wide // 2),
        vmem(blocks, kv_cols, TILE),
        vmem(4, own_blocks, kv_cols, TILE),
        vmem(width, 8, kind=F32),
        vmem(8, width, kind=F32),
        vmem(width, LANES, kind=F32),
        vmem(q_cols, width, kind=F32),
        vmem(q_cols + kv_cols, width, kind=F32),
        vmem(blocks, TILE, wide, kind=F32),
        vmem(blocks, TILE, wide),
        vmem(HD + 16, wide, kind=F32),
        vmem(HD, full_len, kind=F32),
        vmem(HD, full_len, kind=F32),
        vmem(units, width, LANES),
        vmem(units, width - width // 8, LANES),
        vmem(units, extra, width // 8, LANES),
        vmem(end_rows, LANES),
        vmem(RING - 1, end_rows // RING, LANES),
        vmem(extra, end_rows // RING, LANES),
        vmem(4, end_rows // RING, LANES),
        vmem(2, blocks // 2, 2, width // 2, LANES),
        vmem(2, own_blocks, 2, width, LANES),
        vmem(2, own_blocks, 2, width, LANES),
        dma(2, own_blocks, 2, 3),
        dma(2, own_blocks, 2, 3),
        dma(2, blocks),
        dma(2, blocks),
        dma(2, blocks),
        dma(2, own_blocks, 2),
        dma(2 * SUBS, plan.steps),
        dma(2 * SUBS, plan.steps),
        dma(units, plan.stages),
        dma(units, plan.stages),
        dma(3, RING - 1),
        dma(3, RING - 1),
        dma(3),
        dma(3),
        dma(3),
        dma(3),
    ]
    in_vmem = pl.BlockSpec(memory_space=pltpu.VMEM)
    anywhere = pl.BlockSpec(memory_space=pl.ANY)
    in_smem = pl.BlockSpec(memory_space=pltpu.SMEM)
    block_out, grad_tokens, total, end_total = pl.pallas_call(
        functools.partial(block_kernel, plan),
        out_shape=(
            jax.ShapeDtypeStruct((width, own_len), BF),
            jax.ShapeDtypeStruct((width, own_len), BF),
            jax.ShapeDtypeStruct((units, width, LANES), BF),
            jax.ShapeDtypeStruct((end_rows, LANES), BF),
        ),
        in_specs=[in_smem] * 2 + [anywhere] * 7 + [in_vmem] * 4 + [anywhere],
        out_specs=(anywhere,) * 4,
        scratch_shapes=scratch,
        compiler_params=pltpu.CompilerParams(
            collective_id=0, has_side_effects=True, vmem_limit_bytes=63 << 20
        ),
    )(
        tags,
        tag_weight,
        tokens[0],
        cotangent[0],
        query_weight.T,
        key_value_weight,
        output_weight,
        up_weight,
        down_weight,
        norm_gain_one,
        norm_bias_one,
        norm_gain_two,
        norm_bias_two,
        jnp.asarray(table),
    )
    first_end = slices * width // q_cols
    finish_shapes = (
        ((own_len, width), BF),
        ((own_len, width), BF),
        ((q_cols, width), F32),
        ((width, kv_cols), F32),
        ((q_cols, width), F32),
        ((width, hidden), F32),
        ((hidden, width), F32),
        ((width,), F32),
        ((width,), F32),
        ((width,), F32),
        ((width,), F32),
    )
    group = 3
    by_columns = lambda rows: pl.BlockSpec((rows, group * LANES), lambda i: (0, i))
    by_rows = pl.BlockSpec((group * LANES, own_len), lambda i: (i, 0))
    block_out, grad_tokens, grad_query, grad_keyval, grad_output, grad_up, grad_down, *vectors = (
        pl.pallas_call(
            finish_kernel,
            grid=(slices // group,),
            out_shape=tuple(jax.ShapeDtypeStruct(*shape) for shape in finish_shapes),
            in_specs=[
                by_rows,
                by_rows,
                pl.BlockSpec((group, width, LANES), lambda i: (i, 0, 0)),
                pl.BlockSpec((group, width, LANES), lambda i: (slices // group + i, 0, 0)),
                pl.BlockSpec((2 * group, q_cols, LANES), lambda i: (first_end // group + i, 0, 0)),
                pl.BlockSpec((end_rows, LANES), lambda i: (0, 0)),
            ],
            out_specs=(
                by_columns(own_len),
                by_columns(own_len),
                by_columns(q_cols),
                pl.BlockSpec((width, kv_cols), lambda i: (0, 0)),
                by_columns(q_cols),
                by_columns(width),
                by_columns(hidden),
                pl.BlockSpec((width,), lambda i: (0,)),
                pl.BlockSpec((width,), lambda i: (0,)),
                pl.BlockSpec((width,), lambda i: (0,)),
                pl.BlockSpec((width,), lambda i: (0,)),
            ),
            compiler_params=pltpu.CompilerParams(vmem_limit_bytes=60 << 20),
        )(
            block_out,
            grad_tokens,
            total,
            total,
            total.reshape(units * width // q_cols, q_cols, LANES),
            end_total,
        )
    )
    return (
        block_out[None],
        grad_tokens[None],
        grad_query.T,
        grad_keyval,
        grad_output,
        grad_up,
        grad_down,
        *vectors,
    )


def solution(mesh):
    rows = P("dp", "tp", None)
    columns, depth, whole = P(None, "tp"), P("tp", None), P()
    in_specs = (rows, rows, P("dp"), whole, columns, whole, depth, columns, depth) + (whole,) * 4
    out_specs = (rows, rows, columns, whole, depth, columns, depth) + (whole,) * 4
    return jax.shard_map(
        functools.partial(shards, mesh.shape["dp"]),
        mesh=mesh,
        in_specs=in_specs,
        out_specs=out_specs,
        check_vma=False,
    )
```

```python
import functools

import jax
import jax.numpy as jnp
import numpy as np
from jax import lax
from jax.experimental import pallas as pl
from jax.experimental.pallas import tpu as pltpu
from jax.sharding import PartitionSpec as P

HD = 64
ROT = 16
HALF = ROT // 2
TILE = 256
LANES = 128
RING = 8
SUBS = 3
MESH = pl.DeviceIdType.MESH
BF = jnp.bfloat16
F32 = jnp.float32


def mm(left, right):
    return jnp.dot(left, right, preferred_element_type=F32)


def mm_t(left, right):
    return lax.dot_general(left, right, (((1,), (1,)), ((), ())), preferred_element_type=F32)


def turn(values, cosine, sine):
    front, back = values[:HALF], values[HALF:ROT]
    return jnp.concatenate(
        [front * cosine - back * sine, back * cosine + front * sine, values[ROT:]], axis=0
    )


class Plan:
    def __init__(self, dp):
        self.bits = dp.bit_length() - 1
        self.extra = [2**position for position in range(3, self.bits)]
        self.stages = 6 + len(self.extra)
        self.steps = 2 * (RING - 1) + len(self.extra)
        self.slots = SUBS * (self.steps + 1)

    def strides(self, kind):
        return (1 + kind, 2 - kind, 4)


class Bundle:
    def __init__(self, plan, d, t, part, landed, swapped, total, send, recv):
        self.plan, self.d, self.t = plan, d, t
        self.part, self.landed, self.swapped, self.total = part, landed, swapped, total
        self.send, self.recv = send, recv
        self.rows = part.shape[1]

    def bit(self, stride):
        return (self.d // stride) % 2

    def partner(self, stride):
        return self.d + (1 - 2 * self.bit(stride)) * stride

    def span(self, kind, depth):
        start = 0
        for level in range(depth):
            start = start + self.bit(self.plan.strides(kind)[level]) * (self.rows >> (level + 1))
        return pl.multiple_of(start, 16), self.rows >> depth

    def copy(self, unit, kind, stage):
        order, extra = self.plan.strides(kind), self.plan.extra
        if stage < 3:
            start, size = self.span(kind, stage)
            position = order[stage]
            half = size // 2
            other = pl.multiple_of(start + (1 - self.bit(position)) * half, 16)
            source = self.part.at[unit, pl.ds(other, half)]
            target = self.landed.at[unit, pl.ds(self.rows - size, half)]
        elif stage < 3 + len(extra):
            start, size = self.span(kind, 3)
            position = extra[stage - 3]
            source = self.part.at[unit, pl.ds(start, size)]
            target = self.swapped.at[unit, stage - 3]
        else:
            depth = self.plan.stages - stage
            start, size = self.span(kind, depth)
            position = order[depth - 1]
            source = self.total.at[unit, pl.ds(start, size)]
            target = source
        return pltpu.make_async_remote_copy(
            src_ref=source,
            dst_ref=target,
            send_sem=self.send.at[unit, stage],
            recv_sem=self.recv.at[unit, stage],
            device_id=(self.partner(position), self.t),
            device_id_type=MESH,
        )

    def start(self, unit, kind, stage):
        self.copy(unit, kind, stage).start()

    def finish(self, unit, kind, stage, publish=True):
        self.copy(unit, kind, stage).wait()
        last = 2 + len(self.plan.extra)
        if stage <= last:
            if stage < 3:
                start, size = self.span(kind, stage + 1)
                arrived = self.landed[unit, pl.ds(self.rows - 2 * size, size)]
            else:
                start, size = self.span(kind, 3)
                arrived = self.swapped[unit, stage - 3]
            mine = self.part[unit, pl.ds(start, size)]
            summed = (mine.astype(F32) + arrived.astype(F32)).astype(BF)
            if stage == last and publish:
                self.total[unit, pl.ds(start, size)] = summed
            else:
                self.part[unit, pl.ds(start, size)] = summed


class Ring:
    def __init__(self, plan, d, t, part, landed, swapped, total, send, recv, height):
        self.plan, self.d, self.t = plan, d, t
        self.part, self.landed, self.swapped, self.total = part, landed, swapped, total
        self.send, self.recv = send, recv
        self.height = height
        self.rows = part.shape[1] // RING
        self.first = d - d % RING
        line, side = (d % RING) // 2, d % 2
        self.place = line + side * (RING - 1 - 2 * line)
        self.neighbours = [
            self.device(lax.rem(self.place + ahead, jnp.int32(RING))) for ahead in (1, RING - 1)
        ]

    def device(self, place):
        far = place // (RING // 2)
        return self.first + (1 - far) * 2 * place + far * (2 * RING - 1 - 2 * place)

    def units(self, way, sub):
        return pl.ds((SUBS * way + sub) * self.height, self.height)

    def chunk(self, way, ahead):
        index = lax.rem(self.place + RING + (1, -1)[way] * ahead, jnp.int32(RING))
        return pl.ds(pl.multiple_of(index * self.rows, 16), self.rows)

    def copy(self, way, sub, phase, index, step):
        units = self.units(way, sub)
        peer = self.neighbours[way]
        if phase == 0:
            source = self.part.at[units, self.chunk(way, -index)]
            slot = pl.ds(pl.multiple_of(index * self.rows, 16), self.rows)
            target = self.landed.at[units, slot]
        elif phase == 1:
            stride = self.plan.extra[index]
            peer = self.d + (1 - 2 * ((self.d // stride) % 2)) * stride
            source = self.part.at[units, self.chunk(way, 1)]
            target = self.swapped.at[units, index]
        else:
            source = self.total.at[units, self.chunk(way, 1 - index)]
            target = source
        return pltpu.make_async_remote_copy(
            src_ref=source,
            dst_ref=target,
            send_sem=self.send.at[SUBS * way + sub, step],
            recv_sem=self.recv.at[SUBS * way + sub, step],
            device_id=(peer, self.t),
            device_id_type=MESH,
        )

    def finish(self, way, sub, phase, index, step, last):
        if phase == 2:
            return
        units = self.units(way, sub)
        if phase == 0:
            slot = pl.ds(pl.multiple_of(index * self.rows, 16), self.rows)
            rows, arrived = self.chunk(way, -1 - index), self.landed[units, slot]
        else:
            rows, arrived = self.chunk(way, 1), self.swapped[units, index]
        summed = (self.part[units, rows].astype(F32) + arrived.astype(F32)).astype(BF)
        (self.total if last else self.part)[units, rows] = summed

    def slot(self, number):
        number = jnp.int32(number)
        step = lax.div(number, jnp.int32(SUBS))
        sub = number - step * SUBS
        extra = len(self.plan.extra)
        turns = RING - 1
        middle = turns + extra

        def when(condition, ended, begun, last=False):
            @pl.when(condition)
            def _():
                if ended is not None:
                    for way in range(2):
                        self.copy(way, sub, *ended, step - 1).wait()
                        self.finish(way, sub, *ended, step - 1, last)
                        if begun is not None:
                            self.copy(way, sub, *begun, step).start()
                else:
                    for way in range(2):
                        self.copy(way, sub, *begun, step).start()

        when(step == 0, None, (0, 0))
        when((step > 0) & (step < turns), (0, step - 1), (0, step))
        for index in range(extra + 1):
            ended = (0, turns - 1) if index == 0 else (1, index - 1)
            begun = (2, 0) if index == extra else (1, index)
            when(step == turns + index, ended, begun, last=index == extra)
        when((step > middle) & (step < self.plan.steps), (2, step - 1 - middle), (2, step - middle))
        when(step == self.plan.steps, (2, turns - 1), None)


def block_kernel(
    plan,
    tags_ref,
    tag_weight_ref,
    tok_hbm,
    cot_hbm,
    query_t_hbm,
    keyval_hbm,
    output_hbm,
    up_hbm,
    down_hbm,
    gain_one_ref,
    bias_one_ref,
    gain_two_ref,
    bias_two_ref,
    table_hbm,
    block_out_hbm,
    grad_tokens_hbm,
    total_hbm,
    end_total_hbm,
    tok_ref,
    cot_ref,
    query_t_ref,
    keyval_ref,
    output_ref,
    up_ref,
    down_ref,
    table_ref,
    block_out_ref,
    grad_tokens_ref,
    total_ref,
    end_total_ref,
    load_sem,
    store_sem,
    x_all,
    gr_all,
    n1_all,
    br_all,
    g_all,
    up_t,
    down_t,
    qkv_t,
    qkv_w,
    out_t,
    q_t,
    k_t,
    k_r,
    v_t,
    v_r,
    do_t,
    gkv_all,
    kv_land,
    norms_c,
    norms_r,
    bias_acc,
    sum_out,
    sum_qkv,
    score,
    prob,
    acc,
    d_key,
    d_value,
    part,
    landed,
    swapped,
    end_part,
    end_land,
    end_swap,
    tp_land,
    pre,
    from_sib,
    from_x,
    ag_send,
    ag_recv,
    rs_send,
    rs_recv,
    rs_send_x,
    rs_recv_x,
    ring_send,
    ring_recv,
    dp_send,
    dp_recv,
    end_send,
    end_recv,
    tp_send,
    tp_recv,
    kv_send,
    kv_recv,
):
    d, t = lax.axis_index("dp"), lax.axis_index("tp")
    chip, core = t // 2, t % 2
    sib = t + 1 - 2 * core
    across = (t + 2) % 4
    diag = (sib + 2) % 4
    width = tok_ref.shape[1]
    hidden = up_ref.shape[1]
    q_cols = query_t_ref.shape[0]
    heads = q_cols // HD
    own_blocks = tok_ref.shape[0] // TILE
    blocks = 4 * own_blocks
    half_width = width // 2
    tall = width // TILE

    slices = width // LANES
    base = 2 * slices
    big = Bundle(plan, d, t, part, landed, swapped, total_ref, dp_send, dp_recv)
    ring = Ring(
        plan, d, t, part, landed, swapped, total_ref, ring_send, ring_recv, slices // SUBS
    )

    loads = [
        pltpu.make_async_copy(source, target, load_sem.at[index])
        for index, (source, target) in enumerate(
            (
                (tok_hbm, tok_ref),
                (cot_hbm, cot_ref),
                (up_hbm, up_ref),
                (down_hbm, down_ref),
                (query_t_hbm, query_t_ref),
                (keyval_hbm, keyval_ref),
                (output_hbm, output_ref),
                (table_hbm, table_ref),
            )
        )
    ]
    for load in loads:
        load.start()

    barrier = pltpu.get_barrier_semaphore()
    first_of_ring, spot = d - d % RING, d % RING
    ring_peers = [first_of_ring + (spot + hop) % RING for hop in range(1, RING)]
    extra_peers = [d + (1 - 2 * ((d // stride) % 2)) * stride for stride in plan.extra]
    peers = [(d, sib), (d, across), (d, diag)] + [(peer, t) for peer in ring_peers + extra_peers]
    for peer in peers:
        pl.semaphore_signal(barrier, inc=1, device_id=peer, device_id_type=MESH)
    pl.semaphore_wait(barrier, len(peers))

    row_weight = tag_weight_ref[tags_ref[0]]

    sets = (x_all, gr_all)

    def pair(ref, block):
        return jnp.concatenate([ref[2 * block], ref[2 * block + 1]], axis=1)

    def put_pair(ref, block, value):
        ref[2 * block] = value[:, :LANES]
        ref[2 * block + 1] = value[:, LANES:]

    def half_lanes(start, half):
        return pl.ds(pl.multiple_of(start + half * LANES, LANES), LANES)

    def gather_copy(kind, piece, half, owner, route):
        place = owner * own_blocks + piece
        target = {0: sib, 1: across, 2: sib}[route]
        view = sets[kind].at[2 * place + half]
        return pltpu.make_async_remote_copy(
            src_ref=view,
            dst_ref=view,
            send_sem=ag_send.at[kind, piece, half, route],
            recv_sem=ag_recv.at[kind, piece, half, route],
            device_id=(d, target),
            device_id_type=MESH,
        )

    for piece in range(own_blocks):
        for half in range(2):
            place = 2 * (t * own_blocks + piece) + half
            first = piece * TILE + half * LANES
            rows = slice(first, first + LANES)
            if first == 0:
                loads[0].wait()
            x_all[place] = tok_ref[rows, :].T
            gather_copy(0, piece, half, t, 1).start()
            gather_copy(0, piece, half, t, 0).start()
            if first == 0:
                loads[1].wait()
            gr_all[place] = (cot_ref[rows, :].astype(F32) * row_weight).astype(BF).T
            gather_copy(1, piece, half, t, 1).start()
            gather_copy(1, piece, half, t, 0).start()

    for load in loads[2:]:
        load.wait()
    up_t[...] = up_ref[...].T
    down_t[...] = down_ref[...].T
    qkv_t[:q_cols] = query_t_ref[...]
    qkv_t[q_cols:] = keyval_ref[...].T
    qkv_w[...] = qkv_t[...].T
    out_t[...] = output_ref[...].T
    for index, norm in enumerate((gain_one_ref, bias_one_ref, gain_two_ref, bias_two_ref)):
        norms_r[index : index + 1] = norm[...].reshape(1, width)
    norms_c[...] = norms_r[...].T
    score[...] = jnp.zeros_like(score)
    bias_acc[...] = jnp.zeros_like(bias_acc)
    sum_out[...] = jnp.zeros_like(sum_out)
    sum_qkv[...] = jnp.zeros_like(sum_qkv)
    d_key[...] = jnp.zeros_like(d_key)
    d_value[...] = jnp.zeros_like(d_value)

    def standardize(x):
        mean = jnp.sum(x, axis=0, keepdims=True) * (1.0 / width)
        centred = x - mean
        variance = jnp.sum(centred * centred, axis=0, keepdims=True) * (1.0 / width)
        inverse = lax.rsqrt(variance + 1e-05)
        return centred * inverse, inverse

    def feed_forward(step, carry):
        late, piece, half = step // 4, (step % 4) // 2, step % 2
        owners = (
            (1 - late) * t + late * across,
            (1 - late) * sib + late * diag,
        )
        places = [owner * own_blocks + piece for owner in owners]
        sides = [slice(0, LANES), slice(LANES, TILE)]

        @pl.when(late == 0)
        def _():
            for kind in range(2):
                gather_copy(kind, piece, half, sib, 0).wait_recv()

        @pl.when(late == 1)
        def _():
            for kind in range(2):
                gather_copy(kind, piece, half, across, 1).wait_recv()
                gather_copy(kind, piece, half, across, 2).start()
            for kind in range(2):
                gather_copy(kind, piece, half, diag, 2).wait_recv()

        def load(ref):
            return jnp.concatenate([ref[2 * place + half] for place in places], axis=1)

        def store(ref, value):
            for place, side in zip(places, sides):
                ref[2 * place + half] = value[:, side]

        normal, _ = standardize(load(x_all).astype(F32))
        n1 = (normal * norms_c[:, 0:1] + norms_c[:, 1:2]).astype(BF)
        n2 = (normal * norms_c[:, 2:3] + norms_c[:, 3:4]).astype(BF)
        store(n1_all, n1)
        gr = load(gr_all)
        qkv = mm(qkv_t[...], n1)
        lanes = [half_lanes(place * TILE, half) for place in places]
        cosine = jnp.concatenate([table_ref[:HALF, at] for at in lanes], axis=1)
        sine = jnp.concatenate([table_ref[HALF:, at] for at in lanes], axis=1)
        grad_context = mm(output_ref[...], gr)
        for head in range(heads):
            rows = slice(head * HD, (head + 1) * HD)
            turned = (turn(qkv[rows], cosine, sine) * (HD**-0.5)).astype(BF)
            grads = grad_context[rows].astype(BF)
            for place, side in zip(places, sides):
                at = slice(head * LANES, (head + 1) * LANES)
                q_t[2 * place + half, :, at] = turned[:, side]
                do_t[2 * place + half, :, at] = grads[:, side]
        key = turn(qkv[q_cols : q_cols + HD], cosine, sine)
        value = qkv[q_cols + HD :]
        for place, side, at in zip(places, sides, lanes):
            k_t[:, at] = key[:, side].astype(BF)
            v_t[:HD, at] = value[:, side].astype(BF)
            v_t[HD:, at] = jnp.ones((v_t.shape[0] - HD, LANES), BF)
            k_r[place, half_lanes(0, half), :] = key[:, side].T.astype(BF)
            v_r[place, half_lanes(0, half), :] = value[:, side].T.astype(BF)

        chunks = [slice(c * TILE, (c + 1) * TILE) for c in range(tall)]

        def activate(pre_act):
            cdf = 0.5 + 0.5 * lax.erf(pre_act * 0.7071067811865476)
            density = jnp.exp(-0.5 * pre_act * pre_act) * 0.3989422804014327
            return (pre_act * cdf).astype(BF), cdf + pre_act * density

        pre_acts = [mm(up_t[chunks[0], :], n2)]
        grad_mids, middles, grads = [], [], []
        for c in range(tall):
            grad_mids.append(mm(down_ref[chunks[c], :], gr))
            if c + 1 < tall:
                pre_acts.append(mm(up_t[chunks[c + 1], :], n2))
            middle, slope = activate(pre_acts[c])
            middles.append(middle)
            grads.append((grad_mids[c] * slope).astype(BF))
            if c > 0:
                score[c - 1] += mm_t(middles[c - 1], gr)
        middle = jnp.concatenate(middles, axis=0)
        grad_hidden = jnp.concatenate(grads, axis=0)
        score[tall - 1] += mm_t(middles[-1], gr)
        store(br_all, mm(down_t[...], middle).astype(BF))
        up_two = mm(up_ref[...], grad_hidden)
        bias_acc[...] += up_two[:, :LANES] + up_two[:, LANES:]
        store(g_all, (up_two * norms_c[:, 2:3]).astype(BF))
        score[tall : 2 * tall] += mm_t(n2, grad_hidden).reshape(tall, TILE, hidden)
        return carry

    lax.fori_loop(0, blocks, feed_forward, 0)

    def gathered(index, carry):
        piece, half = index // 2, index % 2
        for kind in range(2):
            gather_copy(kind, piece, half, t, 0).wait_send()
            gather_copy(kind, piece, half, t, 1).wait_send()
            gather_copy(kind, piece, half, across, 2).wait_send()
        return carry

    lax.fori_loop(0, 2 * own_blocks, gathered, 0)

    for first in range(SUBS):
        for index in range(first * slices // SUBS, (first + 1) * slices // SUBS):
            cols = slice(index * LANES, (index + 1) * LANES)
            part[index] = score[:tall, :, cols].reshape(hidden, LANES).astype(BF)
            part[slices + index] = score[tall : 2 * tall, :, cols].reshape(width, LANES).astype(BF)
        ring.slot(first)
    for index in range(tall):
        rows = slice(index * TILE, (index + 1) * TILE)
        product = jnp.sum(up_ref[rows, :].astype(F32) * score[tall + index], axis=1, keepdims=True)
        norms_c[rows, 4:5] = product
    norms_c[:, 5:6] = jnp.sum(bias_acc[...], axis=1, keepdims=True)
    bias_acc[...] = jnp.zeros_like(bias_acc)

    outs = (br_all, g_all)

    def block_of(step):
        return step // 2 + (blocks // 2) * (step % 2)

    def pre_copy(kind, step, block):
        rows = pl.ds(pl.multiple_of((1 - core) * half_width, 16), half_width)
        return pltpu.make_async_remote_copy(
            src_ref=outs[kind].at[pl.ds(2 * block, 2), rows],
            dst_ref=pre.at[kind, step // 2],
            send_sem=rs_send.at[kind, step],
            recv_sem=rs_recv.at[kind, step],
            device_id=(d, sib),
            device_id_type=MESH,
        )

    def sib_copy(kind, step, block):
        return pltpu.make_async_remote_copy(
            src_ref=outs[kind].at[pl.ds(2 * block, 2)],
            dst_ref=from_sib.at[kind, block % own_blocks],
            send_sem=rs_send.at[kind, step],
            recv_sem=rs_recv.at[kind, step],
            device_id=(d, sib),
            device_id_type=MESH,
        )

    def x_copy(kind, block, sender_core, owner):
        rows = pl.ds(pl.multiple_of(sender_core * half_width, 16), half_width)
        return pltpu.make_async_remote_copy(
            src_ref=outs[kind].at[pl.ds(2 * block, 2), rows],
            dst_ref=from_x.at[kind, block % own_blocks, :, rows],
            send_sem=rs_send_x.at[kind, block],
            recv_sem=rs_recv_x.at[kind, block % own_blocks, sender_core],
            device_id=(d, owner),
            device_id_type=MESH,
        )

    def scatter_first(kind, step):
        block = block_of(step)
        owner = block // own_blocks

        @pl.when(owner // 2 != chip)
        def _():
            pre_copy(kind, step, block).start()

        @pl.when((owner // 2 == chip) & (owner != t))
        def _():
            sib_copy(kind, step, block).start()

    def scatter_second(kind, step):
        block = block_of(step)
        owner = block // own_blocks

        @pl.when(owner // 2 != chip)
        def _():
            pre_copy(kind, step, block).wait()
            rows = pl.ds(pl.multiple_of(core * half_width, 16), half_width)
            mine = outs[kind][pl.ds(2 * block, 2), rows].astype(F32)
            outs[kind][pl.ds(2 * block, 2), rows] = (mine + pre[kind, step // 2].astype(F32)).astype(BF)
            x_copy(kind, block, core, owner).start()

        @pl.when((owner // 2 == chip) & (owner != t))
        def _():
            sib_copy(kind, step, block).wait_send()

    def scatter_sent(kind, step):
        block = block_of(step)
        owner = block // own_blocks

        @pl.when(owner // 2 != chip)
        def _():
            x_copy(kind, block, core, owner).wait_send()

    def scatter_arrived(kind, piece):
        block = t * own_blocks + piece
        step = 2 * (block % (blocks // 2)) + block // (blocks // 2)
        sib_copy(kind, step, block).wait_recv()
        for sender_core in range(2):
            x_copy(kind, block, sender_core, t).wait_recv()
        halves = [
            outs[kind][2 * block + half].astype(F32)
            + from_sib[kind, piece, half].astype(F32)
            + from_x[kind, piece, half].astype(F32)
            for half in range(2)
        ]
        return jnp.concatenate(halves, axis=1)

    def emit_block_out(piece):
        cols = slice(piece * TILE, (piece + 1) * TILE)
        x = pair(x_all, t * own_blocks + piece).astype(F32)
        block_out_ref[:, cols] = (x + scatter_arrived(0, piece)).astype(BF)

    def emit_grad_tokens(piece):
        place = t * own_blocks + piece
        if piece == 0:
            for hop in range(3):
                kv_copy(t, hop, (t + hop + 1) % 4).wait_recv()
        key_value_grad = gkv_all[place].astype(F32)
        for hop in range(3):
            key_value_grad = key_value_grad + kv_land[hop, piece].astype(F32)
        up_kv = mm(qkv_w[:, q_cols:], key_value_grad.astype(BF))
        scaled = scatter_arrived(1, piece) + up_kv * norms_c[:, 0:1]
        normal, inverse = standardize(pair(x_all, place).astype(F32))
        mean_one = jnp.sum(scaled, axis=0, keepdims=True) * (1.0 / width)
        mean_two = jnp.sum(scaled * normal, axis=0, keepdims=True) * (1.0 / width)
        grad_tokens_ref[:, piece * TILE : (piece + 1) * TILE] = (
            pair(gr_all, place).astype(F32) + inverse * (scaled - mean_one - normal * mean_two)
        ).astype(BF)

    def attend(step, number):
        heavy = step % 2
        ring.slot(number)
        number = number + 1
        block = block_of(step)
        queries = jnp.concatenate([q_t[2 * block], q_t[2 * block + 1]], axis=1)
        wide = heads * TILE

        def of_head(value, head):
            first = value[:, head * LANES : (head + 1) * LANES]
            second = value[:, (heads + head) * LANES : (heads + head + 1) * LANES]
            return jnp.concatenate([first, second], axis=1)

        def in_pairs(count, body, start):
            carry = lax.fori_loop(0, count // 4, lambda i, c: body(4 * i, 4, c), start)
            carry = lax.fori_loop(count // 4 * 2, count // 2, lambda i, c: body(2 * i, 2, c), carry)
            return lax.fori_loop(count // 2 * 2, count, lambda i, c: body(i, 1, c), carry)

        def lanes_of(j, tiles):
            return pl.ds(pl.multiple_of(j * TILE, TILE), tiles * TILE)

        def scores(j, tiles, top):
            tile = mm(k_r[pl.ds(j, tiles)].reshape(tiles * TILE, HD), queries)
            score[pl.ds(j, tiles)] = tile.reshape(tiles, TILE, wide)
            return jnp.maximum(top, jnp.max(tile.reshape(tiles * TILE // 8, 8, wide), axis=0))

        top = in_pairs(block, scores, jnp.full((8, wide), -1e30, F32))
        tile = mm(k_r[block], queries)
        past = lax.broadcasted_iota(jnp.int32, (TILE, wide), 0)
        now = lax.broadcasted_iota(jnp.int32, (TILE, wide), 1)
        now = now // (wide // 2) * LANES + now % LANES
        tile = jnp.where(past <= now, tile, -1e30)
        score[block] = tile
        top = jnp.maximum(top, jnp.max(tile.reshape(TILE // 8, 8, wide), axis=0))
        top = jnp.max(top, axis=0, keepdims=True)

        acc[...] = jnp.zeros_like(acc)

        @pl.when(heavy == 1)
        def _():
            ring.slot(number)

        number = number + heavy

        def weigh(j, tiles, carry):
            weights = jnp.exp(score[pl.ds(j, tiles)] - top).astype(BF)
            prob[pl.ds(j, tiles)] = weights
            acc[...] += mm(v_t[:, lanes_of(j, tiles)], weights.reshape(tiles * TILE, wide))
            return carry

        in_pairs(block + 1, weigh, 0)
        inverse = 1.0 / acc[HD : HD + 1]
        context = acc[:HD] * inverse
        grad = (pair(do_t, block).astype(F32) * inverse).astype(BF)
        delta = jnp.sum(grad.astype(F32) * context, axis=0, keepdims=True)
        acc[:HD] = jnp.zeros((HD, wide), F32)

        context_rows = jnp.concatenate([of_head(context, h) for h in range(heads)], axis=0).astype(BF)
        branch = mm(out_t[...], context_rows) + pair(br_all, block).astype(F32)
        put_pair(br_all, block, branch.astype(BF))
        scatter_first(0, step)

        @pl.when(step > 0)
        def _():
            scatter_second(1, step - 1)


        def back(j, tiles, number):
            ring.slot(number)
            weights = prob[pl.ds(j, tiles)].reshape(tiles * TILE, wide)
            grad_probs = mm(v_r[pl.ds(j, tiles)].reshape(tiles * TILE, HD), grad)
            grad_scores = (weights.astype(F32) * (grad_probs - delta)).astype(BF)
            acc[:HD] += mm(k_t[:, lanes_of(j, tiles)], grad_scores)
            d_key[:, lanes_of(j, tiles)] += mm_t(queries, grad_scores)
            d_value[:, lanes_of(j, tiles)] += mm_t(grad, weights)
            return number + 1

        number = in_pairs(block + 1, back, number)
        lanes = pl.ds(pl.multiple_of(block * TILE, TILE), TILE)
        cosine, sine = table_ref[:HALF, lanes], table_ref[HALF:, lanes]
        grad_queries = acc[:HD]
        turned = [
            turn(of_head(grad_queries, head), cosine, -sine) * (HD**-0.5) for head in range(heads)
        ]
        turned = jnp.concatenate(turned, axis=0).astype(BF)
        scatter_second(0, step)
        ring.slot(number)
        number = number + 1
        scaled = mm(qkv_w[:, :q_cols], turned) * norms_c[:, 0:1] + pair(g_all, block).astype(F32)
        put_pair(g_all, block, scaled.astype(BF))
        scatter_first(1, step)
        sum_out[...] += mm_t(context_rows, pair(gr_all, block))
        sum_qkv[:q_cols] += mm_t(turned, pair(n1_all, block))
        bias_acc[:q_cols] += turned[:, :LANES].astype(F32) + turned[:, LANES:].astype(F32)
        return number

    lax.fori_loop(0, blocks, attend, SUBS)
    groups = [n // 4 + n % 4 // 2 + n % 2 for n in range(1, blocks + 1)]
    attended = SUBS + sum(groups) + 2 * blocks + blocks // 2
    scatter_second(1, blocks - 1)
    for index in range(slices):
        cols = slice(index * LANES, (index + 1) * LANES)
        for which, source in ((0, sum_out[:, cols]), (1, sum_qkv[:q_cols, cols])):
            row = (2 * index + which) * q_cols
            part[base + row // width, row % width : row % width + q_cols] = source.astype(BF)
    ends = [(base, 0), (base + 1, 1), (base + 2, 0)]
    for unit, kind in ends:
        big.start(unit, kind, 0)

    def key_value(step, carry):
        for block in (2 * step, 2 * step + 1):
            lanes = pl.ds(pl.multiple_of(block * TILE, TILE), TILE)
            cosine, sine = table_ref[:HALF, lanes], table_ref[HALF:, lanes]
            key_grads = turn(d_key[:, lanes], cosine, -sine)
            grads = jnp.concatenate([key_grads, d_value[:, lanes]], axis=0).astype(BF)
            gkv_all[block] = grads
            bias_acc[q_cols : q_cols + 2 * HD] += grads[:, :LANES].astype(F32) + grads[:, LANES:].astype(F32)
            sum_qkv[q_cols:] += mm_t(grads, pair(n1_all, block))
        return carry

    lax.fori_loop(0, blocks // 2, key_value, 0)

    def kv_copy(owner, hop, target):
        return pltpu.make_async_remote_copy(
            src_ref=gkv_all.at[pl.ds(owner * own_blocks, own_blocks)],
            dst_ref=kv_land.at[hop],
            send_sem=kv_send.at[hop],
            recv_sem=kv_recv.at[hop],
            device_id=(d, target),
            device_id_type=MESH,
        )

    for hop in range(3):
        owner = (t + hop + 1) % 4
        kv_copy(owner, hop, owner).start()

    end_part[:width] = sum_qkv[q_cols:].T.astype(BF)
    row_sums = jnp.sum(bias_acc[: q_cols + 2 * HD], axis=1, keepdims=True)
    shift_one = jnp.sum(qkv_t[...].astype(F32) * row_sums, axis=0, keepdims=True)
    shift_two = norms_c[:, 5:6]
    product_one = jnp.sum(qkv_t[...].astype(F32) * sum_qkv[...], axis=0, keepdims=True)
    gain_one = (product_one - norms_r[1:2] * shift_one) / norms_r[0:1]
    gain_two = (norms_c[:, 4:5] - norms_c[:, 3:4] * shift_two) / norms_c[:, 2:3]
    lane = lax.broadcasted_iota(jnp.int32, (width, 8), 1)
    columns = jnp.where(lane == 0, gain_two, shift_two).T
    rows = jnp.concatenate([gain_one, shift_one, columns[:6]], axis=0)
    end_part[width:] = jnp.zeros((end_part.shape[0] - width, LANES), BF)
    for index in range(slices):
        end_part[width + 16 * index : width + 16 * index + 8] = rows[
            :, index * LANES : (index + 1) * LANES
        ].astype(BF)

    end_rows = end_part.shape[0] // RING

    def end_chunk(index):
        return pl.ds(pl.multiple_of(index * end_rows, 16), end_rows)

    def end_copy(hop, gather):
        peer = (spot + hop) % RING
        done = end_total_ref.at[end_chunk(spot)]
        return pltpu.make_async_remote_copy(
            src_ref=done if gather else end_part.at[end_chunk(peer)],
            dst_ref=done if gather else end_land.at[hop - 1],
            send_sem=end_send.at[int(gather), hop - 1],
            recv_sem=end_recv.at[int(gather), hop - 1],
            device_id=(first_of_ring + peer, t),
            device_id_type=MESH,
        )

    def end_exchange(index):
        return pltpu.make_async_remote_copy(
            src_ref=end_part.at[end_chunk(spot)],
            dst_ref=end_swap.at[index],
            send_sem=end_send.at[2, index],
            recv_sem=end_recv.at[2, index],
            device_id=(extra_peers[index], t),
            device_id_type=MESH,
        )

    def tp_copy(sender, hop):
        return pltpu.make_async_remote_copy(
            src_ref=tp_land.at[sender],
            dst_ref=tp_land.at[sender],
            send_sem=tp_send.at[hop],
            recv_sem=tp_recv.at[hop],
            device_id=(d, (t + hop + 1) % 4),
            device_id_type=MESH,
        )

    hops = range(1, RING)
    stores = [
        pltpu.make_async_copy(source, target, store_sem.at[index])
        for index, (source, target) in enumerate(
            (
                (block_out_ref, block_out_hbm),
                (grad_tokens_ref, grad_tokens_hbm),
                (total_ref.at[pl.ds(0, base)], total_hbm.at[pl.ds(0, base)]),
                (total_ref.at[pl.ds(base, 3)], total_hbm.at[pl.ds(base, 3)]),
                (end_total_ref, end_total_hbm),
            )
        )
    ]
    for hop in hops:
        end_copy(hop, False).start()

    def end_reduced():
        for hop in hops:
            end_copy(hop, False).wait()
        summed = end_part[end_chunk(spot)].astype(F32)
        for hop in hops:
            summed = summed + end_land[hop - 1].astype(F32)
        for index in range(len(plan.extra)):
            end_part[end_chunk(spot)] = summed.astype(BF)
            end_exchange(index).start()
            end_exchange(index).wait()
            summed = summed.astype(BF).astype(F32) + end_swap[index].astype(F32)
        tp_land[t] = summed.astype(BF)
        for hop in range(3):
            tp_copy(t, hop).start()

    def end_shared():
        for hop in range(3):
            tp_copy((t + 3 - hop) % 4, hop).wait_recv()
        land = [tp_land[sender].astype(F32) for sender in range(4)]
        end_total_ref[end_chunk(spot)] = (land[0] + land[1] + land[2] + land[3]).astype(BF)
        for hop in hops:
            end_copy(hop, True).start()

    ring_slots = list(range(attended, plan.slots))
    for beat in range(max(plan.stages, 1 + (len(ring_slots) + 1) // 2)):
        if beat < plan.stages:
            for unit, kind in ends:
                big.finish(unit, kind, beat)
                if beat + 1 < plan.stages:
                    big.start(unit, kind, beat + 1)
        for index in ring_slots[2 * beat : 2 * beat + 2]:
            ring.slot(index)
        if beat == 0:
            emit_block_out(0)
        if beat == 1:
            end_reduced()
            emit_block_out(1)
            stores[0].start()
        if beat == 2:
            end_shared()
            emit_grad_tokens(0)
        if beat == 3:
            emit_grad_tokens(1)
            stores[1].start()
        if beat == (len(ring_slots) + 1) // 2:
            stores[2].start()
    for hop in hops:
        end_copy(hop, True).wait()
    stores[3].start()
    stores[4].start()
    for hop in range(3):
        tp_copy(t, hop).wait_send()
    for hop in range(3):
        kv_copy((t + hop + 1) % 4, hop, (t + hop + 1) % 4).wait_send()

    def drain(step, carry):
        for kind in range(2):
            scatter_sent(kind, step)
        return carry

    lax.fori_loop(0, blocks, drain, 0)
    for store in stores:
        store.wait()


def finish_kernel(
    block_out_t,
    grad_tokens_t,
    down,
    up,
    ends,
    shared,
    block_out_ref,
    grad_tokens_ref,
    grad_query_ref,
    grad_keyval_ref,
    grad_output_ref,
    grad_up_ref,
    grad_down_ref,
    *vector_refs,
):
    width = down.shape[1]
    block_out_ref[...] = block_out_t[...].T
    grad_tokens_ref[...] = grad_tokens_t[...].T
    grad_keyval_ref[...] = shared[:width].astype(F32)
    for index in range(down.shape[0]):
        cols = slice(index * LANES, (index + 1) * LANES)
        grad_down_ref[:, cols] = down[index].astype(F32)
        grad_up_ref[:, cols] = up[index].astype(F32)
        grad_output_ref[:, cols] = ends[2 * index].astype(F32)
        grad_query_ref[:, cols] = ends[2 * index + 1].astype(F32)
    for index, vector in enumerate(vector_refs):
        starts = [width + 16 * k + index for k in range(width // LANES)]
        rows = [shared[start : start + 1] for start in starts]
        vector[...] = jnp.concatenate(rows, axis=1).astype(F32).reshape(vector.shape)


def shards(
    dp,
    tokens,
    cotangent,
    tags,
    tag_weight,
    query_weight,
    key_value_weight,
    output_weight,
    up_weight,
    down_weight,
    norm_gain_one,
    norm_bias_one,
    norm_gain_two,
    norm_bias_two,
):
    plan = Plan(dp)
    _, own_len, width = tokens.shape
    full_len = 4 * own_len
    q_cols, kv_cols, hidden = query_weight.shape[1], key_value_weight.shape[1], up_weight.shape[1]
    heads = q_cols // HD
    wide = heads * TILE
    blocks, own_blocks = full_len // TILE, own_len // TILE
    frequencies = (10000.0 ** (-np.arange(0, ROT, 2, dtype=np.float32) / ROT)).astype(np.float32)
    angles = frequencies[:, None] * np.arange(full_len, dtype=np.float32)[None, :]
    table = np.concatenate([np.cos(angles), np.sin(angles)], axis=0).astype(np.float32)

    slices = width // LANES
    units = 2 * slices + 3
    end_rows = width + LANES
    extra = max(1, len(plan.extra))
    vmem = lambda *shape, kind=BF: pltpu.VMEM(shape, kind)
    dma = lambda *shape: pltpu.SemaphoreType.DMA(shape)
    scratch = [
        vmem(own_len, width),
        vmem(own_len, width),
        vmem(q_cols, width),
        vmem(width, kv_cols),
        vmem(q_cols, width),
        vmem(width, hidden),
        vmem(hidden, width),
        vmem(ROT, full_len, kind=F32),
        vmem(width, own_len),
        vmem(width, own_len),
        vmem(units, width, LANES),
        vmem(end_rows, LANES),
        dma(8),
        dma(5),
        vmem(2 * blocks, width, LANES),
        vmem(2 * blocks, width, LANES),
        vmem(2 * blocks, width, LANES),
        vmem(2 * blocks, width, LANES),
        vmem(2 * blocks, width, LANES),
        vmem(hidden, width),
        vmem(width, hidden),
        vmem(q_cols + kv_cols, width),
        vmem(width, q_cols + kv_cols),
        vmem(width, q_cols),
        vmem(2 * blocks, HD, wide // 2),
        vmem(HD, full_len),
        vmem(blocks, TILE, HD),
        vmem(HD + 16, full_len),
        vmem(blocks, TILE, HD),
        vmem(2 * blocks, HD, wide // 2),
        vmem(blocks, kv_cols, TILE),
        vmem(4, own_blocks, kv_cols, TILE),
        vmem(width, 8, kind=F32),
        vmem(8, width, kind=F32),
        vmem(width, LANES, kind=F32),
        vmem(q_cols, width, kind=F32),
        vmem(q_cols + kv_cols, width, kind=F32),
        vmem(blocks, TILE, wide, kind=F32),
        vmem(blocks, TILE, wide),
        vmem(HD + 16, wide, kind=F32),
        vmem(HD, full_len, kind=F32),
        vmem(HD, full_len, kind=F32),
        vmem(units, width, LANES),
        vmem(units, width - width // 8, LANES),
        vmem(units, extra, width // 8, LANES),
        vmem(end_rows, LANES),
        vmem(RING - 1, end_rows // RING, LANES),
        vmem(extra, end_rows // RING, LANES),
        vmem(4, end_rows // RING, LANES),
        vmem(2, blocks // 2, 2, width // 2, LANES),
        vmem(2, own_blocks, 2, width, LANES),
        vmem(2, own_blocks, 2, width, LANES),
        dma(2, own_blocks, 2, 3),
        dma(2, own_blocks, 2, 3),
        dma(2, blocks),
        dma(2, blocks),
        dma(2, blocks),
        dma(2, own_blocks, 2),
        dma(2 * SUBS, plan.steps),
        dma(2 * SUBS, plan.steps),
        dma(units, plan.stages),
        dma(units, plan.stages),
        dma(3, RING - 1),
        dma(3, RING - 1),
        dma(3),
        dma(3),
        dma(3),
        dma(3),
    ]
    in_vmem = pl.BlockSpec(memory_space=pltpu.VMEM)
    anywhere = pl.BlockSpec(memory_space=pl.ANY)
    in_smem = pl.BlockSpec(memory_space=pltpu.SMEM)
    block_out, grad_tokens, total, end_total = pl.pallas_call(
        functools.partial(block_kernel, plan),
        out_shape=(
            jax.ShapeDtypeStruct((width, own_len), BF),
            jax.ShapeDtypeStruct((width, own_len), BF),
            jax.ShapeDtypeStruct((units, width, LANES), BF),
            jax.ShapeDtypeStruct((end_rows, LANES), BF),
        ),
        in_specs=[in_smem] * 2 + [anywhere] * 7 + [in_vmem] * 4 + [anywhere],
        out_specs=(anywhere,) * 4,
        scratch_shapes=scratch,
        compiler_params=pltpu.CompilerParams(
            collective_id=0, has_side_effects=True, vmem_limit_bytes=63 << 20
        ),
    )(
        tags,
        tag_weight,
        tokens[0],
        cotangent[0],
        query_weight.T,
        key_value_weight,
        output_weight,
        up_weight,
        down_weight,
        norm_gain_one,
        norm_bias_one,
        norm_gain_two,
        norm_bias_two,
        jnp.asarray(table),
    )
    first_end = slices * width // q_cols
    finish_shapes = (
        ((own_len, width), BF),
        ((own_len, width), BF),
        ((q_cols, width), F32),
        ((width, kv_cols), F32),
        ((q_cols, width), F32),
        ((width, hidden), F32),
        ((hidden, width), F32),
        ((width,), F32),
        ((width,), F32),
        ((width,), F32),
        ((width,), F32),
    )
    group = 3
    by_columns = lambda rows: pl.BlockSpec((rows, group * LANES), lambda i: (0, i))
    by_rows = pl.BlockSpec((group * LANES, own_len), lambda i: (i, 0))
    block_out, grad_tokens, grad_query, grad_keyval, grad_output, grad_up, grad_down, *vectors = (
        pl.pallas_call(
            finish_kernel,
            grid=(slices // group,),
            out_shape=tuple(jax.ShapeDtypeStruct(*shape) for shape in finish_shapes),
            in_specs=[
                by_rows,
                by_rows,
                pl.BlockSpec((group, width, LANES), lambda i: (i, 0, 0)),
                pl.BlockSpec((group, width, LANES), lambda i: (slices // group + i, 0, 0)),
                pl.BlockSpec((2 * group, q_cols, LANES), lambda i: (first_end // group + i, 0, 0)),
                pl.BlockSpec((end_rows, LANES), lambda i: (0, 0)),
            ],
            out_specs=(
                by_columns(own_len),
                by_columns(own_len),
                by_columns(q_cols),
                pl.BlockSpec((width, kv_cols), lambda i: (0, 0)),
                by_columns(q_cols),
                by_columns(width),
                by_columns(hidden),
                pl.BlockSpec((width,), lambda i: (0,)),
                pl.BlockSpec((width,), lambda i: (0,)),
                pl.BlockSpec((width,), lambda i: (0,)),
                pl.BlockSpec((width,), lambda i: (0,)),
            ),
            compiler_params=pltpu.CompilerParams(vmem_limit_bytes=60 << 20),
        )(
            block_out,
            grad_tokens,
            total,
            total,
            total.reshape(units * width // q_cols, q_cols, LANES),
            end_total,
        )
    )
    return (
        block_out[None],
        grad_tokens[None],
        grad_query.T,
        grad_keyval,
        grad_output,
        grad_up,
        grad_down,
        *vectors,
    )


def solution(mesh):
    rows = P("dp", "tp", None)
    columns, depth, whole = P(None, "tp"), P("tp", None), P()
    in_specs = (rows, rows, P("dp"), whole, columns, whole, depth, columns, depth) + (whole,) * 4
    out_specs = (rows, rows, columns, whole, depth, columns, depth) + (whole,) * 4
    return jax.shard_map(
        functools.partial(shards, mesh.shape["dp"]),
        mesh=mesh,
        in_specs=in_specs,
        out_specs=out_specs,
        check_vma=False,
    )
```

```python
import functools

import jax
import jax.numpy as jnp
import numpy as np
from jax import lax
from jax.experimental import pallas as pl
from jax.experimental.pallas import tpu as pltpu
from jax.sharding import PartitionSpec as P

HD = 64
ROT = 16
HALF = ROT // 2
TILE = 256
LANES = 128
RING = 8
SUBS = 3
MESH = pl.DeviceIdType.MESH
BF = jnp.bfloat16
F32 = jnp.float32


def mm(left, right):
    return jnp.dot(left, right, preferred_element_type=F32)


def mm_t(left, right):
    return lax.dot_general(left, right, (((1,), (1,)), ((), ())), preferred_element_type=F32)


def turn(values, cosine, sine):
    front, back = values[:HALF], values[HALF:ROT]
    return jnp.concatenate(
        [front * cosine - back * sine, back * cosine + front * sine, values[ROT:]], axis=0
    )


class Plan:
    def __init__(self, dp):
        self.bits = dp.bit_length() - 1
        self.extra = [2**position for position in range(3, self.bits)]
        self.stages = 6 + len(self.extra)
        self.steps = 2 * (RING - 1) + len(self.extra)
        self.slots = SUBS * (self.steps + 1)

    def strides(self, kind):
        return (1 + kind, 2 - kind, 4)


class Bundle:
    def __init__(self, plan, d, t, part, landed, swapped, total, send, recv):
        self.plan, self.d, self.t = plan, d, t
        self.part, self.landed, self.swapped, self.total = part, landed, swapped, total
        self.send, self.recv = send, recv
        self.rows = part.shape[1]

    def bit(self, stride):
        return (self.d // stride) % 2

    def partner(self, stride):
        return self.d + (1 - 2 * self.bit(stride)) * stride

    def span(self, kind, depth):
        start = 0
        for level in range(depth):
            start = start + self.bit(self.plan.strides(kind)[level]) * (self.rows >> (level + 1))
        return pl.multiple_of(start, 16), self.rows >> depth

    def copy(self, unit, kind, stage):
        order, extra = self.plan.strides(kind), self.plan.extra
        if stage < 3:
            start, size = self.span(kind, stage)
            position = order[stage]
            half = size // 2
            other = pl.multiple_of(start + (1 - self.bit(position)) * half, 16)
            source = self.part.at[unit, pl.ds(other, half)]
            target = self.landed.at[unit, pl.ds(self.rows - size, half)]
        elif stage < 3 + len(extra):
            start, size = self.span(kind, 3)
            position = extra[stage - 3]
            source = self.part.at[unit, pl.ds(start, size)]
            target = self.swapped.at[unit, stage - 3]
        else:
            depth = self.plan.stages - stage
            start, size = self.span(kind, depth)
            position = order[depth - 1]
            source = self.total.at[unit, pl.ds(start, size)]
            target = source
        return pltpu.make_async_remote_copy(
            src_ref=source,
            dst_ref=target,
            send_sem=self.send.at[unit, stage],
            recv_sem=self.recv.at[unit, stage],
            device_id=(self.partner(position), self.t),
            device_id_type=MESH,
        )

    def start(self, unit, kind, stage):
        self.copy(unit, kind, stage).start()

    def finish(self, unit, kind, stage, publish=True):
        self.copy(unit, kind, stage).wait()
        last = 2 + len(self.plan.extra)
        if stage <= last:
            if stage < 3:
                start, size = self.span(kind, stage + 1)
                arrived = self.landed[unit, pl.ds(self.rows - 2 * size, size)]
            else:
                start, size = self.span(kind, 3)
                arrived = self.swapped[unit, stage - 3]
            mine = self.part[unit, pl.ds(start, size)]
            summed = (mine.astype(F32) + arrived.astype(F32)).astype(BF)
            if stage == last and publish:
                self.total[unit, pl.ds(start, size)] = summed
            else:
                self.part[unit, pl.ds(start, size)] = summed


class Ring:
    def __init__(self, plan, d, t, part, landed, swapped, total, send, recv, height):
        self.plan, self.d, self.t = plan, d, t
        self.part, self.landed, self.swapped, self.total = part, landed, swapped, total
        self.send, self.recv = send, recv
        self.height = height
        self.rows = part.shape[1] // RING
        self.first = d - d % RING
        line, side = (d % RING) // 2, d % 2
        self.place = line + side * (RING - 1 - 2 * line)
        self.neighbours = [
            self.device(lax.rem(self.place + ahead, jnp.int32(RING))) for ahead in (1, RING - 1)
        ]

    def device(self, place):
        far = place // (RING // 2)
        return self.first + (1 - far) * 2 * place + far * (2 * RING - 1 - 2 * place)

    def units(self, way, sub):
        return pl.ds((SUBS * way + sub) * self.height, self.height)

    def chunk(self, way, ahead):
        index = lax.rem(self.place + RING + (1, -1)[way] * ahead, jnp.int32(RING))
        return pl.ds(pl.multiple_of(index * self.rows, 16), self.rows)

    def copy(self, way, sub, phase, index, step):
        units = self.units(way, sub)
        peer = self.neighbours[way]
        if phase == 0:
            source = self.part.at[units, self.chunk(way, -index)]
            slot = pl.ds(pl.multiple_of(index * self.rows, 16), self.rows)
            target = self.landed.at[units, slot]
        elif phase == 1:
            stride = self.plan.extra[index]
            peer = self.d + (1 - 2 * ((self.d // stride) % 2)) * stride
            source = self.part.at[units, self.chunk(way, 1)]
            target = self.swapped.at[units, index]
        else:
            source = self.total.at[units, self.chunk(way, 1 - index)]
            target = source
        return pltpu.make_async_remote_copy(
            src_ref=source,
            dst_ref=target,
            send_sem=self.send.at[SUBS * way + sub, step],
            recv_sem=self.recv.at[SUBS * way + sub, step],
            device_id=(peer, self.t),
            device_id_type=MESH,
        )

    def finish(self, way, sub, phase, index, step, last):
        if phase == 2:
            return
        units = self.units(way, sub)
        if phase == 0:
            slot = pl.ds(pl.multiple_of(index * self.rows, 16), self.rows)
            rows, arrived = self.chunk(way, -1 - index), self.landed[units, slot]
        else:
            rows, arrived = self.chunk(way, 1), self.swapped[units, index]
        summed = (self.part[units, rows].astype(F32) + arrived.astype(F32)).astype(BF)
        (self.total if last else self.part)[units, rows] = summed

    def slot(self, number):
        number = jnp.int32(number)
        step = lax.div(number, jnp.int32(SUBS))
        sub = number - step * SUBS
        extra = len(self.plan.extra)
        turns = RING - 1
        middle = turns + extra

        def when(condition, ended, begun, last=False):
            @pl.when(condition)
            def _():
                if ended is not None:
                    for way in range(2):
                        self.copy(way, sub, *ended, step - 1).wait()
                        self.finish(way, sub, *ended, step - 1, last)
                        if begun is not None:
                            self.copy(way, sub, *begun, step).start()
                else:
                    for way in range(2):
                        self.copy(way, sub, *begun, step).start()

        when(step == 0, None, (0, 0))
        when((step > 0) & (step < turns), (0, step - 1), (0, step))
        for index in range(extra + 1):
            ended = (0, turns - 1) if index == 0 else (1, index - 1)
            begun = (2, 0) if index == extra else (1, index)
            when(step == turns + index, ended, begun, last=index == extra)
        when((step > middle) & (step < self.plan.steps), (2, step - 1 - middle), (2, step - middle))
        when(step == self.plan.steps, (2, turns - 1), None)


def block_kernel(
    plan,
    tags_ref,
    tag_weight_ref,
    tok_hbm,
    cot_hbm,
    query_t_hbm,
    keyval_hbm,
    output_hbm,
    up_hbm,
    down_hbm,
    gain_one_ref,
    bias_one_ref,
    gain_two_ref,
    bias_two_ref,
    table_hbm,
    block_out_hbm,
    grad_tokens_hbm,
    total_hbm,
    end_total_hbm,
    tok_ref,
    cot_ref,
    query_t_ref,
    keyval_ref,
    output_ref,
    up_ref,
    down_ref,
    table_ref,
    block_out_ref,
    grad_tokens_ref,
    total_ref,
    end_total_ref,
    load_sem,
    store_sem,
    x_all,
    gr_all,
    n1_all,
    br_all,
    g_all,
    up_t,
    down_t,
    qkv_t,
    qkv_w,
    out_t,
    q_t,
    k_t,
    k_r,
    v_t,
    v_r,
    do_t,
    gkv_all,
    kv_land,
    norms_c,
    norms_r,
    bias_acc,
    sum_out,
    sum_qkv,
    score,
    prob,
    acc,
    d_key,
    d_value,
    part,
    landed,
    swapped,
    end_part,
    end_land,
    end_swap,
    tp_land,
    pre,
    from_sib,
    from_x,
    ag_send,
    ag_recv,
    rs_send,
    rs_recv,
    rs_send_x,
    rs_recv_x,
    ring_send,
    ring_recv,
    dp_send,
    dp_recv,
    end_send,
    end_recv,
    tp_send,
    tp_recv,
    kv_send,
    kv_recv,
):
    d, t = lax.axis_index("dp"), lax.axis_index("tp")
    chip, core = t // 2, t % 2
    sib = t + 1 - 2 * core
    across = (t + 2) % 4
    diag = (sib + 2) % 4
    width = tok_ref.shape[1]
    hidden = up_ref.shape[1]
    q_cols = query_t_ref.shape[0]
    heads = q_cols // HD
    own_blocks = tok_ref.shape[0] // TILE
    blocks = 4 * own_blocks
    half_width = width // 2
    tall = width // TILE

    slices = width // LANES
    base = 2 * slices
    big = Bundle(plan, d, t, part, landed, swapped, total_ref, dp_send, dp_recv)
    ring = Ring(
        plan, d, t, part, landed, swapped, total_ref, ring_send, ring_recv, slices // SUBS
    )

    loads = [
        pltpu.make_async_copy(source, target, load_sem.at[index])
        for index, (source, target) in enumerate(
            (
                (tok_hbm, tok_ref),
                (cot_hbm, cot_ref),
                (up_hbm, up_ref),
                (down_hbm, down_ref),
                (query_t_hbm, query_t_ref),
                (keyval_hbm, keyval_ref),
                (output_hbm, output_ref),
                (table_hbm, table_ref),
            )
        )
    ]
    for load in loads:
        load.start()

    barrier = pltpu.get_barrier_semaphore()
    first_of_ring, spot = d - d % RING, d % RING
    ring_peers = [first_of_ring + (spot + hop) % RING for hop in range(1, RING)]
    extra_peers = [d + (1 - 2 * ((d // stride) % 2)) * stride for stride in plan.extra]
    peers = [(d, sib), (d, across), (d, diag)] + [(peer, t) for peer in ring_peers + extra_peers]
    for peer in peers:
        pl.semaphore_signal(barrier, inc=1, device_id=peer, device_id_type=MESH)
    pl.semaphore_wait(barrier, len(peers))

    row_weight = tag_weight_ref[tags_ref[0]]

    sets = (x_all, gr_all)

    def pair(ref, block):
        return jnp.concatenate([ref[2 * block], ref[2 * block + 1]], axis=1)

    def put_pair(ref, block, value):
        ref[2 * block] = value[:, :LANES]
        ref[2 * block + 1] = value[:, LANES:]

    def half_lanes(start, half):
        return pl.ds(pl.multiple_of(start + half * LANES, LANES), LANES)

    def gather_copy(kind, piece, half, owner, route):
        place = owner * own_blocks + piece
        target = {0: sib, 1: across, 2: sib}[route]
        view = sets[kind].at[2 * place + half]
        return pltpu.make_async_remote_copy(
            src_ref=view,
            dst_ref=view,
            send_sem=ag_send.at[kind, piece, half, route],
            recv_sem=ag_recv.at[kind, piece, half, route],
            device_id=(d, target),
            device_id_type=MESH,
        )

    for piece in range(own_blocks):
        for half in range(2):
            place = 2 * (t * own_blocks + piece) + half
            first = piece * TILE + half * LANES
            rows = slice(first, first + LANES)
            if first == 0:
                loads[0].wait()
            x_all[place] = tok_ref[rows, :].T
            gather_copy(0, piece, half, t, 1).start()
            gather_copy(0, piece, half, t, 0).start()
            if first == 0:
                loads[1].wait()
            gr_all[place] = (cot_ref[rows, :].astype(F32) * row_weight).astype(BF).T
            gather_copy(1, piece, half, t, 1).start()
            gather_copy(1, piece, half, t, 0).start()

    for load in loads[2:]:
        load.wait()
    up_t[...] = up_ref[...].T
    down_t[...] = down_ref[...].T
    qkv_t[:q_cols] = query_t_ref[...]
    qkv_t[q_cols:] = keyval_ref[...].T
    qkv_w[...] = qkv_t[...].T
    out_t[...] = output_ref[...].T
    for index, norm in enumerate((gain_one_ref, bias_one_ref, gain_two_ref, bias_two_ref)):
        norms_r[index : index + 1] = norm[...].reshape(1, width)
    norms_c[...] = norms_r[...].T
    score[...] = jnp.zeros_like(score)
    bias_acc[...] = jnp.zeros_like(bias_acc)
    sum_out[...] = jnp.zeros_like(sum_out)
    sum_qkv[...] = jnp.zeros_like(sum_qkv)
    d_key[...] = jnp.zeros_like(d_key)
    d_value[...] = jnp.zeros_like(d_value)

    def standardize(x):
        mean = jnp.sum(x, axis=0, keepdims=True) * (1.0 / width)
        centred = x - mean
        variance = jnp.sum(centred * centred, axis=0, keepdims=True) * (1.0 / width)
        inverse = lax.rsqrt(variance + 1e-05)
        return centred * inverse, inverse

    def feed_forward(step, carry):
        late, piece, half = step // 4, (step % 4) // 2, step % 2
        owners = (
            (1 - late) * t + late * across,
            (1 - late) * sib + late * diag,
        )
        places = [owner * own_blocks + piece for owner in owners]
        sides = [slice(0, LANES), slice(LANES, TILE)]

        @pl.when(late == 0)
        def _():
            for kind in range(2):
                gather_copy(kind, piece, half, sib, 0).wait_recv()

        @pl.when(late == 1)
        def _():
            for kind in range(2):
                gather_copy(kind, piece, half, across, 1).wait_recv()
                gather_copy(kind, piece, half, across, 2).start()
            for kind in range(2):
                gather_copy(kind, piece, half, diag, 2).wait_recv()

        def load(ref):
            return jnp.concatenate([ref[2 * place + half] for place in places], axis=1)

        def store(ref, value):
            for place, side in zip(places, sides):
                ref[2 * place + half] = value[:, side]

        normal, _ = standardize(load(x_all).astype(F32))
        n1 = (normal * norms_c[:, 0:1] + norms_c[:, 1:2]).astype(BF)
        n2 = (normal * norms_c[:, 2:3] + norms_c[:, 3:4]).astype(BF)
        store(n1_all, n1)
        gr = load(gr_all)
        qkv = mm(qkv_t[...], n1)
        lanes = [half_lanes(place * TILE, half) for place in places]
        cosine = jnp.concatenate([table_ref[:HALF, at] for at in lanes], axis=1)
        sine = jnp.concatenate([table_ref[HALF:, at] for at in lanes], axis=1)
        grad_context = mm(output_ref[...], gr)
        for head in range(heads):
            rows = slice(head * HD, (head + 1) * HD)
            turned = (turn(qkv[rows], cosine, sine) * (HD**-0.5)).astype(BF)
            grads = grad_context[rows].astype(BF)
            for place, side in zip(places, sides):
                at = slice(head * LANES, (head + 1) * LANES)
                q_t[2 * place + half, :, at] = turned[:, side]
                do_t[2 * place + half, :, at] = grads[:, side]
        key = turn(qkv[q_cols : q_cols + HD], cosine, sine)
        value = qkv[q_cols + HD :]
        for place, side, at in zip(places, sides, lanes):
            k_t[:, at] = key[:, side].astype(BF)
            v_t[:HD, at] = value[:, side].astype(BF)
            v_t[HD:, at] = jnp.ones((v_t.shape[0] - HD, LANES), BF)
            k_r[place, half_lanes(0, half), :] = key[:, side].T.astype(BF)
            v_r[place, half_lanes(0, half), :] = value[:, side].T.astype(BF)

        chunks = [slice(c * TILE, (c + 1) * TILE) for c in range(tall)]

        def activate(pre_act):
            cdf = 0.5 + 0.5 * lax.erf(pre_act * 0.7071067811865476)
            density = jnp.exp(-0.5 * pre_act * pre_act) * 0.3989422804014327
            return (pre_act * cdf).astype(BF), cdf + pre_act * density

        pre_acts = [mm(up_t[chunks[0], :], n2)]
        grad_mids, middles, grads = [], [], []
        for c in range(tall):
            grad_mids.append(mm(down_ref[chunks[c], :], gr))
            if c + 1 < tall:
                pre_acts.append(mm(up_t[chunks[c + 1], :], n2))
            middle, slope = activate(pre_acts[c])
            middles.append(middle)
            grads.append((grad_mids[c] * slope).astype(BF))
            if c > 0:
                score[c - 1] += mm_t(middles[c - 1], gr)
        middle = jnp.concatenate(middles, axis=0)
        grad_hidden = jnp.concatenate(grads, axis=0)
        score[tall - 1] += mm_t(middles[-1], gr)
        store(br_all, mm(down_t[...], middle).astype(BF))
        up_two = mm(up_ref[...], grad_hidden)
        bias_acc[...] += up_two[:, :LANES] + up_two[:, LANES:]
        store(g_all, (up_two * norms_c[:, 2:3]).astype(BF))
        score[tall : 2 * tall] += mm_t(n2, grad_hidden).reshape(tall, TILE, hidden)
        return carry

    lax.fori_loop(0, blocks, feed_forward, 0)

    def gathered(index, carry):
        piece, half = index // 2, index % 2
        for kind in range(2):
            gather_copy(kind, piece, half, t, 0).wait_send()
            gather_copy(kind, piece, half, t, 1).wait_send()
            gather_copy(kind, piece, half, across, 2).wait_send()
        return carry

    lax.fori_loop(0, 2 * own_blocks, gathered, 0)

    for first in range(SUBS):
        for index in range(first * slices // SUBS, (first + 1) * slices // SUBS):
            cols = slice(index * LANES, (index + 1) * LANES)
            part[index] = score[:tall, :, cols].reshape(hidden, LANES).astype(BF)
            part[slices + index] = score[tall : 2 * tall, :, cols].reshape(width, LANES).astype(BF)
        ring.slot(first)
    for index in range(tall):
        rows = slice(index * TILE, (index + 1) * TILE)
        product = jnp.sum(up_ref[rows, :].astype(F32) * score[tall + index], axis=1, keepdims=True)
        norms_c[rows, 4:5] = product
    norms_c[:, 5:6] = jnp.sum(bias_acc[...], axis=1, keepdims=True)
    bias_acc[...] = jnp.zeros_like(bias_acc)

    outs = (br_all, g_all)

    def block_of(step):
        return step // 2 + (blocks // 2) * (step % 2)

    def pre_copy(kind, step, block):
        rows = pl.ds(pl.multiple_of((1 - core) * half_width, 16), half_width)
        return pltpu.make_async_remote_copy(
            src_ref=outs[kind].at[pl.ds(2 * block, 2), rows],
            dst_ref=pre.at[kind, step // 2],
            send_sem=rs_send.at[kind, step],
            recv_sem=rs_recv.at[kind, step],
            device_id=(d, sib),
            device_id_type=MESH,
        )

    def sib_copy(kind, step, block):
        return pltpu.make_async_remote_copy(
            src_ref=outs[kind].at[pl.ds(2 * block, 2)],
            dst_ref=from_sib.at[kind, block % own_blocks],
            send_sem=rs_send.at[kind, step],
            recv_sem=rs_recv.at[kind, step],
            device_id=(d, sib),
            device_id_type=MESH,
        )

    def x_copy(kind, block, sender_core, owner):
        rows = pl.ds(pl.multiple_of(sender_core * half_width, 16), half_width)
        return pltpu.make_async_remote_copy(
            src_ref=outs[kind].at[pl.ds(2 * block, 2), rows],
            dst_ref=from_x.at[kind, block % own_blocks, :, rows],
            send_sem=rs_send_x.at[kind, block],
            recv_sem=rs_recv_x.at[kind, block % own_blocks, sender_core],
            device_id=(d, owner),
            device_id_type=MESH,
        )

    def scatter_first(kind, step):
        block = block_of(step)
        owner = block // own_blocks

        @pl.when(owner // 2 != chip)
        def _():
            pre_copy(kind, step, block).start()

        @pl.when((owner // 2 == chip) & (owner != t))
        def _():
            sib_copy(kind, step, block).start()

    def scatter_second(kind, step):
        block = block_of(step)
        owner = block // own_blocks

        @pl.when(owner // 2 != chip)
        def _():
            pre_copy(kind, step, block).wait()
            rows = pl.ds(pl.multiple_of(core * half_width, 16), half_width)
            mine = outs[kind][pl.ds(2 * block, 2), rows].astype(F32)
            outs[kind][pl.ds(2 * block, 2), rows] = (mine + pre[kind, step // 2].astype(F32)).astype(BF)
            x_copy(kind, block, core, owner).start()

        @pl.when((owner // 2 == chip) & (owner != t))
        def _():
            sib_copy(kind, step, block).wait_send()

    def scatter_sent(kind, step):
        block = block_of(step)
        owner = block // own_blocks

        @pl.when(owner // 2 != chip)
        def _():
            x_copy(kind, block, core, owner).wait_send()

    def scatter_arrived(kind, piece):
        block = t * own_blocks + piece
        step = 2 * (block % (blocks // 2)) + block // (blocks // 2)
        sib_copy(kind, step, block).wait_recv()
        for sender_core in range(2):
            x_copy(kind, block, sender_core, t).wait_recv()
        halves = [
            outs[kind][2 * block + half].astype(F32)
            + from_sib[kind, piece, half].astype(F32)
            + from_x[kind, piece, half].astype(F32)
            for half in range(2)
        ]
        return jnp.concatenate(halves, axis=1)

    def emit_block_out(piece):
        cols = slice(piece * TILE, (piece + 1) * TILE)
        x = pair(x_all, t * own_blocks + piece).astype(F32)
        block_out_ref[:, cols] = (x + scatter_arrived(0, piece)).astype(BF)

    def emit_grad_tokens(piece):
        place = t * own_blocks + piece
        if piece == 0:
            for hop in range(3):
                kv_copy(t, hop, (t + hop + 1) % 4).wait_recv()
        key_value_grad = gkv_all[place].astype(F32)
        for hop in range(3):
            key_value_grad = key_value_grad + kv_land[hop, piece].astype(F32)
        up_kv = mm(qkv_w[:, q_cols:], key_value_grad.astype(BF))
        scaled = scatter_arrived(1, piece) + up_kv * norms_c[:, 0:1]
        normal, inverse = standardize(pair(x_all, place).astype(F32))
        mean_one = jnp.sum(scaled, axis=0, keepdims=True) * (1.0 / width)
        mean_two = jnp.sum(scaled * normal, axis=0, keepdims=True) * (1.0 / width)
        grad_tokens_ref[:, piece * TILE : (piece + 1) * TILE] = (
            pair(gr_all, place).astype(F32) + inverse * (scaled - mean_one - normal * mean_two)
        ).astype(BF)

    def attend(step, number):
        heavy = step % 2
        ring.slot(number)
        number = number + 1
        block = block_of(step)
        queries = jnp.concatenate([q_t[2 * block], q_t[2 * block + 1]], axis=1)
        wide = heads * TILE

        def of_head(value, head):
            first = value[:, head * LANES : (head + 1) * LANES]
            second = value[:, (heads + head) * LANES : (heads + head + 1) * LANES]
            return jnp.concatenate([first, second], axis=1)

        def in_pairs(count, body, start):
            carry = lax.fori_loop(0, count // 4, lambda i, c: body(4 * i, 4, c), start)
            carry = lax.fori_loop(count // 4 * 2, count // 2, lambda i, c: body(2 * i, 2, c), carry)
            return lax.fori_loop(count // 2 * 2, count, lambda i, c: body(i, 1, c), carry)

        def lanes_of(j, tiles):
            return pl.ds(pl.multiple_of(j * TILE, TILE), tiles * TILE)

        def scores(j, tiles, top):
            tile = mm(k_r[pl.ds(j, tiles)].reshape(tiles * TILE, HD), queries)
            score[pl.ds(j, tiles)] = tile.reshape(tiles, TILE, wide)
            return jnp.maximum(top, jnp.max(tile.reshape(tiles * TILE // 8, 8, wide), axis=0))

        top = in_pairs(block, scores, jnp.full((8, wide), -1e30, F32))
        tile = mm(k_r[block], queries)
        past = lax.broadcasted_iota(jnp.int32, (TILE, wide), 0)
        now = lax.broadcasted_iota(jnp.int32, (TILE, wide), 1)
        now = now // (wide // 2) * LANES + now % LANES
        tile = jnp.where(past <= now, tile, -1e30)
        score[block] = tile
        top = jnp.maximum(top, jnp.max(tile.reshape(TILE // 8, 8, wide), axis=0))
        top = jnp.max(top, axis=0, keepdims=True)

        acc[...] = jnp.zeros_like(acc)

        @pl.when(heavy == 1)
        def _():
            ring.slot(number)

        number = number + heavy

        def weigh(j, tiles, carry):
            weights = jnp.exp(score[pl.ds(j, tiles)] - top).astype(BF)
            prob[pl.ds(j, tiles)] = weights
            acc[...] += mm(v_t[:, lanes_of(j, tiles)], weights.reshape(tiles * TILE, wide))
            return carry

        in_pairs(block + 1, weigh, 0)
        inverse = 1.0 / acc[HD : HD + 1]
        context = acc[:HD] * inverse
        grad = (pair(do_t, block).astype(F32) * inverse).astype(BF)
        delta = jnp.sum(grad.astype(F32) * context, axis=0, keepdims=True)
        acc[:HD] = jnp.zeros((HD, wide), F32)

        context_rows = jnp.concatenate([of_head(context, h) for h in range(heads)], axis=0).astype(BF)
        branch = mm(out_t[...], context_rows) + pair(br_all, block).astype(F32)
        put_pair(br_all, block, branch.astype(BF))
        scatter_first(0, step)

        @pl.when(step > 0)
        def _():
            scatter_second(1, step - 1)


        def back(j, tiles, number):
            ring.slot(number)
            weights = prob[pl.ds(j, tiles)].reshape(tiles * TILE, wide)
            grad_probs = mm(v_r[pl.ds(j, tiles)].reshape(tiles * TILE, HD), grad)
            grad_scores = (weights.astype(F32) * (grad_probs - delta)).astype(BF)
            acc[:HD] += mm(k_t[:, lanes_of(j, tiles)], grad_scores)
            d_key[:, lanes_of(j, tiles)] += mm_t(queries, grad_scores)
            d_value[:, lanes_of(j, tiles)] += mm_t(grad, weights)
            return number + 1

        number = in_pairs(block + 1, back, number)
        lanes = pl.ds(pl.multiple_of(block * TILE, TILE), TILE)
        cosine, sine = table_ref[:HALF, lanes], table_ref[HALF:, lanes]
        grad_queries = acc[:HD]
        turned = [
            turn(of_head(grad_queries, head), cosine, -sine) * (HD**-0.5) for head in range(heads)
        ]
        turned = jnp.concatenate(turned, axis=0).astype(BF)
        scatter_second(0, step)
        ring.slot(number)
        number = number + 1
        scaled = mm(qkv_w[:, :q_cols], turned) * norms_c[:, 0:1] + pair(g_all, block).astype(F32)
        put_pair(g_all, block, scaled.astype(BF))
        scatter_first(1, step)
        sum_out[...] += mm_t(context_rows, pair(gr_all, block))
        sum_qkv[:q_cols] += mm_t(turned, pair(n1_all, block))
        bias_acc[:q_cols] += turned[:, :LANES].astype(F32) + turned[:, LANES:].astype(F32)
        return number

    lax.fori_loop(0, blocks, attend, SUBS)
    groups = [n // 4 + n % 4 // 2 + n % 2 for n in range(1, blocks + 1)]
    attended = SUBS + sum(groups) + 2 * blocks + blocks // 2
    scatter_second(1, blocks - 1)
    for index in range(slices):
        cols = slice(index * LANES, (index + 1) * LANES)
        for which, source in ((0, sum_out[:, cols]), (1, sum_qkv[:q_cols, cols])):
            row = (2 * index + which) * q_cols
            part[base + row // width, row % width : row % width + q_cols] = source.astype(BF)
    ends = [(base, 0), (base + 1, 1), (base + 2, 0)]
    for unit, kind in ends:
        big.start(unit, kind, 0)

    def key_value(step, carry):
        for block in (2 * step, 2 * step + 1):
            lanes = pl.ds(pl.multiple_of(block * TILE, TILE), TILE)
            cosine, sine = table_ref[:HALF, lanes], table_ref[HALF:, lanes]
            key_grads = turn(d_key[:, lanes], cosine, -sine)
            grads = jnp.concatenate([key_grads, d_value[:, lanes]], axis=0).astype(BF)
            gkv_all[block] = grads
            bias_acc[q_cols : q_cols + 2 * HD] += grads[:, :LANES].astype(F32) + grads[:, LANES:].astype(F32)
            sum_qkv[q_cols:] += mm_t(grads, pair(n1_all, block))
        return carry

    lax.fori_loop(0, blocks // 2, key_value, 0)

    def kv_copy(owner, hop, target):
        return pltpu.make_async_remote_copy(
            src_ref=gkv_all.at[pl.ds(owner * own_blocks, own_blocks)],
            dst_ref=kv_land.at[hop],
            send_sem=kv_send.at[hop],
            recv_sem=kv_recv.at[hop],
            device_id=(d, target),
            device_id_type=MESH,
        )

    for hop in range(3):
        owner = (t + hop + 1) % 4
        kv_copy(owner, hop, owner).start()

    end_part[:width] = sum_qkv[q_cols:].T.astype(BF)
    row_sums = jnp.sum(bias_acc[: q_cols + 2 * HD], axis=1, keepdims=True)
    shift_one = jnp.sum(qkv_t[...].astype(F32) * row_sums, axis=0, keepdims=True)
    shift_two = norms_c[:, 5:6]
    product_one = jnp.sum(qkv_t[...].astype(F32) * sum_qkv[...], axis=0, keepdims=True)
    gain_one = (product_one - norms_r[1:2] * shift_one) / norms_r[0:1]
    gain_two = (norms_c[:, 4:5] - norms_c[:, 3:4] * shift_two) / norms_c[:, 2:3]
    lane = lax.broadcasted_iota(jnp.int32, (width, 8), 1)
    columns = jnp.where(lane == 0, gain_two, shift_two).T
    rows = jnp.concatenate([gain_one, shift_one, columns[:6]], axis=0)
    end_part[width:] = jnp.zeros((end_part.shape[0] - width, LANES), BF)
    for index in range(slices):
        end_part[width + 16 * index : width + 16 * index + 8] = rows[
            :, index * LANES : (index + 1) * LANES
        ].astype(BF)

    end_rows = end_part.shape[0] // RING

    def end_chunk(index):
        return pl.ds(pl.multiple_of(index * end_rows, 16), end_rows)

    def end_copy(hop, gather):
        peer = (spot + hop) % RING
        done = end_total_ref.at[end_chunk(spot)]
        return pltpu.make_async_remote_copy(
            src_ref=done if gather else end_part.at[end_chunk(peer)],
            dst_ref=done if gather else end_land.at[hop - 1],
            send_sem=end_send.at[int(gather), hop - 1],
            recv_sem=end_recv.at[int(gather), hop - 1],
            device_id=(first_of_ring + peer, t),
            device_id_type=MESH,
        )

    def end_exchange(index):
        return pltpu.make_async_remote_copy(
            src_ref=end_part.at[end_chunk(spot)],
            dst_ref=end_swap.at[index],
            send_sem=end_send.at[2, index],
            recv_sem=end_recv.at[2, index],
            device_id=(extra_peers[index], t),
            device_id_type=MESH,
        )

    def tp_copy(sender, hop):
        return pltpu.make_async_remote_copy(
            src_ref=tp_land.at[sender],
            dst_ref=tp_land.at[sender],
            send_sem=tp_send.at[hop],
            recv_sem=tp_recv.at[hop],
            device_id=(d, (t + hop + 1) % 4),
            device_id_type=MESH,
        )

    hops = range(1, RING)
    stores = [
        pltpu.make_async_copy(source, target, store_sem.at[index])
        for index, (source, target) in enumerate(
            (
                (block_out_ref, block_out_hbm),
                (grad_tokens_ref, grad_tokens_hbm),
                (total_ref.at[pl.ds(0, base)], total_hbm.at[pl.ds(0, base)]),
                (total_ref.at[pl.ds(base, 3)], total_hbm.at[pl.ds(base, 3)]),
                (end_total_ref, end_total_hbm),
            )
        )
    ]
    for hop in hops:
        end_copy(hop, False).start()

    def end_reduced():
        for hop in hops:
            end_copy(hop, False).wait()
        summed = end_part[end_chunk(spot)].astype(F32)
        for hop in hops:
            summed = summed + end_land[hop - 1].astype(F32)
        for index in range(len(plan.extra)):
            end_part[end_chunk(spot)] = summed.astype(BF)
            end_exchange(index).start()
            end_exchange(index).wait()
            summed = summed.astype(BF).astype(F32) + end_swap[index].astype(F32)
        tp_land[t] = summed.astype(BF)
        for hop in range(3):
            tp_copy(t, hop).start()

    def end_shared():
        for hop in range(3):
            tp_copy((t + 3 - hop) % 4, hop).wait_recv()
        land = [tp_land[sender].astype(F32) for sender in range(4)]
        end_total_ref[end_chunk(spot)] = (land[0] + land[1] + land[2] + land[3]).astype(BF)
        for hop in hops:
            end_copy(hop, True).start()

    ring_slots = list(range(attended, plan.slots))
    for beat in range(max(plan.stages, 1 + (len(ring_slots) + 1) // 2)):
        if beat < plan.stages:
            for unit, kind in ends:
                big.finish(unit, kind, beat)
                if beat + 1 < plan.stages:
                    big.start(unit, kind, beat + 1)
        for index in ring_slots[2 * beat : 2 * beat + 2]:
            ring.slot(index)
        if beat == 1:
            end_reduced()
            emit_block_out(0)
        if beat == 2:
            end_shared()
            emit_block_out(1)
            stores[0].start()
        if beat == 3:
            emit_grad_tokens(0)
        if beat == 4:
            emit_grad_tokens(1)
            stores[1].start()
        if beat == (len(ring_slots) + 1) // 2:
            stores[2].start()
    for hop in hops:
        end_copy(hop, True).wait()
    stores[3].start()
    stores[4].start()
    for hop in range(3):
        tp_copy(t, hop).wait_send()
    for hop in range(3):
        kv_copy((t + hop + 1) % 4, hop, (t + hop + 1) % 4).wait_send()

    def drain(step, carry):
        for kind in range(2):
            scatter_sent(kind, step)
        return carry

    lax.fori_loop(0, blocks, drain, 0)
    for store in stores:
        store.wait()


def finish_kernel(
    block_out_t,
    grad_tokens_t,
    down,
    up,
    ends,
    shared,
    block_out_ref,
    grad_tokens_ref,
    grad_query_ref,
    grad_keyval_ref,
    grad_output_ref,
    grad_up_ref,
    grad_down_ref,
    *vector_refs,
):
    width = down.shape[1]
    block_out_ref[...] = block_out_t[...].T
    grad_tokens_ref[...] = grad_tokens_t[...].T
    grad_keyval_ref[...] = shared[:width].astype(F32)
    for index in range(down.shape[0]):
        cols = slice(index * LANES, (index + 1) * LANES)
        grad_down_ref[:, cols] = down[index].astype(F32)
        grad_up_ref[:, cols] = up[index].astype(F32)
        grad_output_ref[:, cols] = ends[2 * index].astype(F32)
        grad_query_ref[:, cols] = ends[2 * index + 1].astype(F32)
    for index, vector in enumerate(vector_refs):
        starts = [width + 16 * k + index for k in range(width // LANES)]
        rows = [shared[start : start + 1] for start in starts]
        vector[...] = jnp.concatenate(rows, axis=1).astype(F32).reshape(vector.shape)


def shards(
    dp,
    tokens,
    cotangent,
    tags,
    tag_weight,
    query_weight,
    key_value_weight,
    output_weight,
    up_weight,
    down_weight,
    norm_gain_one,
    norm_bias_one,
    norm_gain_two,
    norm_bias_two,
):
    plan = Plan(dp)
    _, own_len, width = tokens.shape
    full_len = 4 * own_len
    q_cols, kv_cols, hidden = query_weight.shape[1], key_value_weight.shape[1], up_weight.shape[1]
    heads = q_cols // HD
    wide = heads * TILE
    blocks, own_blocks = full_len // TILE, own_len // TILE
    frequencies = (10000.0 ** (-np.arange(0, ROT, 2, dtype=np.float32) / ROT)).astype(np.float32)
    angles = frequencies[:, None] * np.arange(full_len, dtype=np.float32)[None, :]
    table = np.concatenate([np.cos(angles), np.sin(angles)], axis=0).astype(np.float32)

    slices = width // LANES
    units = 2 * slices + 3
    end_rows = width + LANES
    extra = max(1, len(plan.extra))
    vmem = lambda *shape, kind=BF: pltpu.VMEM(shape, kind)
    dma = lambda *shape: pltpu.SemaphoreType.DMA(shape)
    scratch = [
        vmem(own_len, width),
        vmem(own_len, width),
        vmem(q_cols, width),
        vmem(width, kv_cols),
        vmem(q_cols, width),
        vmem(width, hidden),
        vmem(hidden, width),
        vmem(ROT, full_len, kind=F32),
        vmem(width, own_len),
        vmem(width, own_len),
        vmem(units, width, LANES),
        vmem(end_rows, LANES),
        dma(8),
        dma(5),
        vmem(2 * blocks, width, LANES),
        vmem(2 * blocks, width, LANES),
        vmem(2 * blocks, width, LANES),
        vmem(2 * blocks, width, LANES),
        vmem(2 * blocks, width, LANES),
        vmem(hidden, width),
        vmem(width, hidden),
        vmem(q_cols + kv_cols, width),
        vmem(width, q_cols + kv_cols),
        vmem(width, q_cols),
        vmem(2 * blocks, HD, wide // 2),
        vmem(HD, full_len),
        vmem(blocks, TILE, HD),
        vmem(HD + 16, full_len),
        vmem(blocks, TILE, HD),
        vmem(2 * blocks, HD, wide // 2),
        vmem(blocks, kv_cols, TILE),
        vmem(4, own_blocks, kv_cols, TILE),
        vmem(width, 8, kind=F32),
        vmem(8, width, kind=F32),
        vmem(width, LANES, kind=F32),
        vmem(q_cols, width, kind=F32),
        vmem(q_cols + kv_cols, width, kind=F32),
        vmem(blocks, TILE, wide, kind=F32),
        vmem(blocks, TILE, wide),
        vmem(HD + 16, wide, kind=F32),
        vmem(HD, full_len, kind=F32),
        vmem(HD, full_len, kind=F32),
        vmem(units, width, LANES),
        vmem(units, width - width // 8, LANES),
        vmem(units, extra, width // 8, LANES),
        vmem(end_rows, LANES),
        vmem(RING - 1, end_rows // RING, LANES),
        vmem(extra, end_rows // RING, LANES),
        vmem(4, end_rows // RING, LANES),
        vmem(2, blocks // 2, 2, width // 2, LANES),
        vmem(2, own_blocks, 2, width, LANES),
        vmem(2, own_blocks, 2, width, LANES),
        dma(2, own_blocks, 2, 3),
        dma(2, own_blocks, 2, 3),
        dma(2, blocks),
        dma(2, blocks),
        dma(2, blocks),
        dma(2, own_blocks, 2),
        dma(2 * SUBS, plan.steps),
        dma(2 * SUBS, plan.steps),
        dma(units, plan.stages),
        dma(units, plan.stages),
        dma(3, RING - 1),
        dma(3, RING - 1),
        dma(3),
        dma(3),
        dma(3),
        dma(3),
    ]
    in_vmem = pl.BlockSpec(memory_space=pltpu.VMEM)
    anywhere = pl.BlockSpec(memory_space=pl.ANY)
    in_smem = pl.BlockSpec(memory_space=pltpu.SMEM)
    block_out, grad_tokens, total, end_total = pl.pallas_call(
        functools.partial(block_kernel, plan),
        out_shape=(
            jax.ShapeDtypeStruct((width, own_len), BF),
            jax.ShapeDtypeStruct((width, own_len), BF),
            jax.ShapeDtypeStruct((units, width, LANES), BF),
            jax.ShapeDtypeStruct((end_rows, LANES), BF),
        ),
        in_specs=[in_smem] * 2 + [anywhere] * 7 + [in_vmem] * 4 + [anywhere],
        out_specs=(anywhere,) * 4,
        scratch_shapes=scratch,
        compiler_params=pltpu.CompilerParams(
            collective_id=0, has_side_effects=True, vmem_limit_bytes=63 << 20
        ),
    )(
        tags,
        tag_weight,
        tokens[0],
        cotangent[0],
        query_weight.T,
        key_value_weight,
        output_weight,
        up_weight,
        down_weight,
        norm_gain_one,
        norm_bias_one,
        norm_gain_two,
        norm_bias_two,
        jnp.asarray(table),
    )
    first_end = slices * width // q_cols
    finish_shapes = (
        ((own_len, width), BF),
        ((own_len, width), BF),
        ((q_cols, width), F32),
        ((width, kv_cols), F32),
        ((q_cols, width), F32),
        ((width, hidden), F32),
        ((hidden, width), F32),
        ((width,), F32),
        ((width,), F32),
        ((width,), F32),
        ((width,), F32),
    )
    group = 3
    by_columns = lambda rows: pl.BlockSpec((rows, group * LANES), lambda i: (0, i))
    by_rows = pl.BlockSpec((group * LANES, own_len), lambda i: (i, 0))
    block_out, grad_tokens, grad_query, grad_keyval, grad_output, grad_up, grad_down, *vectors = (
        pl.pallas_call(
            finish_kernel,
            grid=(slices // group,),
            out_shape=tuple(jax.ShapeDtypeStruct(*shape) for shape in finish_shapes),
            in_specs=[
                by_rows,
                by_rows,
                pl.BlockSpec((group, width, LANES), lambda i: (i, 0, 0)),
                pl.BlockSpec((group, width, LANES), lambda i: (slices // group + i, 0, 0)),
                pl.BlockSpec((2 * group, q_cols, LANES), lambda i: (first_end // group + i, 0, 0)),
                pl.BlockSpec((end_rows, LANES), lambda i: (0, 0)),
            ],
            out_specs=(
                by_columns(own_len),
                by_columns(own_len),
                by_columns(q_cols),
                pl.BlockSpec((width, kv_cols), lambda i: (0, 0)),
                by_columns(q_cols),
                by_columns(width),
                by_columns(hidden),
                pl.BlockSpec((width,), lambda i: (0,)),
                pl.BlockSpec((width,), lambda i: (0,)),
                pl.BlockSpec((width,), lambda i: (0,)),
                pl.BlockSpec((width,), lambda i: (0,)),
            ),
            compiler_params=pltpu.CompilerParams(vmem_limit_bytes=60 << 20),
        )(
            block_out,
            grad_tokens,
            total,
            total,
            total.reshape(units * width // q_cols, q_cols, LANES),
            end_total,
        )
    )
    return (
        block_out[None],
        grad_tokens[None],
        grad_query.T,
        grad_keyval,
        grad_output,
        grad_up,
        grad_down,
        *vectors,
    )


def solution(mesh):
    rows = P("dp", "tp", None)
    columns, depth, whole = P(None, "tp"), P("tp", None), P()
    in_specs = (rows, rows, P("dp"), whole, columns, whole, depth, columns, depth) + (whole,) * 4
    out_specs = (rows, rows, columns, whole, depth, columns, depth) + (whole,) * 4
    return jax.shard_map(
        functools.partial(shards, mesh.shape["dp"]),
        mesh=mesh,
        in_specs=in_specs,
        out_specs=out_specs,
        check_vma=False,
    )
```
